32 devices in a mesh: rows: 8 (over y, x, core), blk: 4 (over z).
Axes of the slice: x: 2, y: 2, z: 4, core: 2. Of those that a mesh axis runs over, the one named last changes fastest.
Arguments:
- tokens: bfloat16 [16, 1024, 768], P('rows', 'blk'), may hold values from -6 to 6
- segments: int32 [16, 1024], P('rows', 'blk'), may hold values from 0 to 6, as said below
- query_weight: bfloat16 [768, 768], replicated, may hold values from -0.3125 to 0.3125
- query_bias: float32 [768], replicated, may hold values from -3 to 3
- key_weight: bfloat16 [768, 768], replicated, may hold values from -0.21875 to 0.21875
- value_weight: bfloat16 [768, 768], replicated, may hold values from -0.21875 to 0.21875
- value_bias: float32 [768], replicated, may hold values from -0.125 to 0.125
- out_weight: bfloat16 [768, 768], replicated, may hold values from -3 to 3
- out_bias: float32 [768], replicated, may hold values from -0.625 to 0.625
- first_gain: float32 [768], replicated, may hold values from 0.5 to 1.5
- first_shift: float32 [768], replicated, may hold values from -0.625 to 0.625
- up_weight: bfloat16 [768, 3072], replicated, may hold values from -0.21875 to 0.21875
- up_bias: float32 [3072], replicated, may hold values from -0.625 to 0.625
- down_weight: bfloat16 [3072, 768], replicated, may hold values from -0.109375 to 0.109375
- down_bias: float32 [768], replicated, may hold values from -0.625 to 0.625
- second_gain: float32 [768], replicated, may hold values from 0.5 to 1.5
- second_shift: float32 [768], replicated, may hold values from -0.625 to 0.625
- cotangent: bfloat16 [16, 1024, 768], P('rows', 'blk'), may hold values from -6 to 6
Outputs:
- layer_output: bfloat16 [16, 1024, 768], P('rows', 'blk')
- pooled: float32 [16, 6, 1728], P('rows')
- grad_tokens: bfloat16 [16, 1024, 768], P('rows', 'blk')
- grad_query_weight: float32 [768, 768], replicated
- grad_query_bias: float32 [768], replicated
- grad_key_weight: float32 [768, 768], replicated
- grad_value_weight: float32 [768, 768], replicated
- grad_value_bias: float32 [768], replicated
- grad_out_weight: float32 [768, 768], replicated
- grad_out_bias: float32 [768], replicated
- grad_first_gain: float32 [768], replicated
- grad_first_shift: float32 [768], replicated
- grad_up_weight: float32 [768, 3072], replicated
- grad_up_bias: float32 [3072], replicated
- grad_down_weight: float32 [3072, 768], replicated
- grad_down_bias: float32 [768], replicated
- grad_second_gain: float32 [768], replicated
- grad_second_shift: float32 [768], replicated
The draws below stay inside these ranges and needn't reach their ends.
Inputs may be any that keep to these rules, and one draw needn't show every extreme that they name: `segments`: in every sequence the ids never fall until padding begins; padding (0) fills the sequence's end, possibly empty; every id 1 to 6 appears in every sequence, each on consecutive tokens.
All inputs are finite; a program needn't handle non-finite values.
Results may differ from the reference program's by a relative error of at most 0.019.
Values may be sent and summed in bfloat16 or wider, within the bound.
No kernel may reach another device: no remote copies, remote signals or barrier semaphores. Data moves between devices by JAX's collectives and lax.ppermute only.
A program may use at most 192 MiB of HBM per device.

```python
import jax
import jax.numpy as jnp
from jax import lax

D = 768
H = 12
HD = 64
FF = 3072
TOK_BLK = 256
SEQ_DEV = 2
NSEG = 6
LEN = 1024
SEQUENCES = 16


def draw_segments(key, part):
    key_pad = jax.random.fold_in(key, 11)
    key_wts = jax.random.fold_in(key, 23)
    key_pick = jax.random.fold_in(key, 37)
    key_short = jax.random.fold_in(key, 41)
    key_place = jax.random.fold_in(key, 53)
    key_longpad = jax.random.fold_in(key, 67)
    groups = SEQUENCES // SEQ_DEV
    chosen = jax.random.randint(key_pick, (groups, 1), 0, SEQ_DEV)
    within = jnp.arange(SEQ_DEV, dtype=jnp.int32)[None, :]
    is_long = (within == chosen).reshape(SEQUENCES, 1)
    padding = jax.random.randint(key_pad, (SEQUENCES, 1), 0, LEN // 2)
    long_pad = jax.random.randint(key_longpad, (SEQUENCES, 1), 0, TOK_BLK // 2)
    padding = jnp.where(is_long, long_pad, padding)
    live_rows = LEN - padding
    weights = jax.random.randint(key_wts, (SEQUENCES, NSEG), 1, 4)
    running = jnp.cumsum(weights, axis=1)
    bounds_drawn = live_rows * running // running[:, NSEG - 1:NSEG]
    short_most = max(TOK_BLK // (2 * NSEG), 1)
    short_len = jax.random.randint(key_short, (SEQUENCES, NSEG), 1, short_most + 1)
    big_place = jax.random.randint(key_place, (SEQUENCES, 1), 0, NSEG)
    slots = jnp.arange(NSEG, dtype=jnp.int32)[None, :]
    short_only = jnp.where(slots == big_place, 0, short_len)
    big_len = live_rows - jnp.sum(short_only, axis=1, keepdims=True)
    seg_len = jnp.where(slots == big_place, big_len, short_only)
    bounds_long = jnp.cumsum(seg_len, axis=1)
    bounds = jnp.where(is_long, bounds_long, bounds_drawn)
    positions = jnp.arange(LEN, dtype=jnp.int32)[None, :]
    passed = (positions[:, :, None] >= bounds[:, None, :NSEG - 1]).astype(jnp.int32)
    seg_ids = 1 + jnp.sum(passed, axis=2)
    return jnp.where(positions < live_rows, seg_ids, 0).astype(jnp.int32)


def steps_of(key, shape, cuts, low, high):
    def one(axis_at, blocks):
        steps = jax.random.uniform(jax.random.fold_in(jax.random.fold_in(key, 6), axis_at), (blocks,), jnp.float32, low / len(cuts), high / len(cuts))
        return jnp.repeat(jnp.exp(steps), shape[axis_at] // blocks).reshape((-1,) + (1,) * (len(shape) - axis_at - 1))

    factor_of = one(*cuts[0])
    for cut in cuts[1:]:
        factor_of = factor_of * one(*cut)
    return factor_of


def bell_draw(stream_key, extent, width, bound, cuts=(), kind=jnp.bfloat16):
    entries = width * jax.random.normal(stream_key, extent, jnp.float32)
    if cuts:
        entries = entries * steps_of(stream_key, extent, cuts, -0.22, 0.18)
    return jnp.clip(entries, -bound, bound).astype(kind)


def setup_inputs(seed: int = 0) -> dict:
    keys = jax.random.split(jax.random.key(seed), 19)
    return {
        "tokens": bell_draw(keys[0], (SEQUENCES, LEN, D), 1.0, 6.0, ((0, 8), (1, 4))),
        "segments": draw_segments(jax.random.fold_in(keys[18], 71), 0),
        "query_weight": bell_draw(keys[2], (D, D), (D // 2) ** -0.5, 0.3125),
        "query_bias": bell_draw(keys[3], (D,), 0.5, 3.0, (), jnp.float32),
        "key_weight": bell_draw(keys[4], (D, D), D ** -0.5, 0.21875),
        "value_weight": bell_draw(keys[5], (D, D), D ** -0.5, 0.21875),
        "value_bias": bell_draw(keys[6], (D,), 0.02, 0.125, (), jnp.float32),
        "out_weight": bell_draw(keys[7], (D, D), (max(D * NSEG // LEN, 1)) ** -0.5, 3.0),
        "out_bias": bell_draw(keys[8], (D,), 0.1, 0.625, (), jnp.float32),
        "first_gain": jnp.clip(1.0 + 0.1 * jax.random.normal(keys[9], (D,), jnp.float32), 0.5, 1.5),
        "first_shift": bell_draw(keys[10], (D,), 0.1, 0.625, (), jnp.float32),
        "up_weight": bell_draw(keys[11], (D, FF), D ** -0.5, 0.21875),
        "up_bias": bell_draw(keys[12], (FF,), 0.1, 0.625, (), jnp.float32),
        "down_weight": bell_draw(keys[13], (FF, D), FF ** -0.5, 0.109375),
        "down_bias": bell_draw(keys[14], (D,), 0.1, 0.625, (), jnp.float32),
        "second_gain": jnp.clip(1.0 + 0.1 * jax.random.normal(keys[15], (D,), jnp.float32), 0.5, 1.5),
        "second_shift": bell_draw(keys[16], (D,), 0.1, 0.625, (), jnp.float32),
        "cotangent": bell_draw(keys[17], (SEQUENCES, LEN, D), 1.0, 6.0, ((0, 8), (1, 4))),
    }


@jax.custom_vjp
def low(v):
    return lax.optimization_barrier(v.astype(jnp.bfloat16)).astype(jnp.float32)

@jax.custom_vjp
def low_back(v):
    return v

def low_keep(v):
    return (low(v), None)

def low_pass(kept, grad):
    return (grad,)

def back_keep(v):
    return (v, None)

def back_low(kept, grad):
    return (low(grad),)
low.defvjp(low_keep, low_pass)
low_back.defvjp(back_keep, back_low)
highest = lax.Precision.HIGHEST
norm_eps = 1e-12
pool_eps = 1e-06

def matmul(left, right):
    return jnp.dot(left, right, precision=highest, preferred_element_type=jnp.float32)

def layer_norm(rows_in, gain_vec, shift_vec):
    row_mean = lax.optimization_barrier(jnp.mean(rows_in, axis=-1, keepdims=True))
    centred = rows_in - row_mean
    variance = lax.optimization_barrier(jnp.mean(centred * centred, axis=-1, keepdims=True))
    return centred * lax.rsqrt(variance + norm_eps) * gain_vec + shift_vec

def forward_layer(params, inputs, seg_row):
    query_weight, query_bias, key_weight, value_weight, value_bias, out_weight, out_bias, first_gain, first_shift, up_weight, up_bias, down_weight, down_bias, second_gain, second_shift = params
    length = inputs.shape[0]
    queries = low(low_back(0.125 * (matmul(inputs, query_weight) + query_bias)))
    key_rows = low(low_back(matmul(inputs, key_weight)))
    value_rows = low(low_back(matmul(inputs, value_weight) + value_bias))
    block_rows = min(512, length)
    key_heads = key_rows.reshape(length, H, HD)
    value_heads = value_rows.reshape(length, H, HD)
    query_blocks = queries.reshape(length // block_rows, block_rows, H, HD)
    seg_blocks = seg_row.reshape(length // block_rows, block_rows)

    def attend(block_args):
        query_block, seg_block = block_args
        scores = low_back(jnp.einsum('qhd,khd->hqk', query_block, key_heads, precision=highest))
        allowed = seg_block[:, None] == seg_row[None, :]
        expo = jnp.where(allowed[None], jnp.exp(scores), 0.0)
        totals = lax.optimization_barrier(jnp.sum(expo, axis=2))
        numerator = low_back(jnp.einsum('hqk,khd->qhd', low(expo), value_heads, precision=highest))
        return (numerator / jnp.transpose(totals)[:, :, None]).reshape(block_rows, H * HD)
    attended = lax.map(jax.checkpoint(attend), (query_blocks, seg_blocks)).reshape(length, H * HD)
    branch = low_back(matmul(low(attended), out_weight) + out_bias)
    hidden = layer_norm(inputs + branch, first_gain, first_shift)
    preact = low_back(matmul(low(hidden), up_weight) + up_bias)
    activation = low(jax.nn.gelu(preact, approximate=False))
    feed_out = low_back(matmul(activation, down_weight) + down_bias)
    return layer_norm(hidden + feed_out, second_gain, second_shift)

def matryoshka(averages):
    pieces = []
    for prefix in (D, D * 2 // 3, D // 3, D // 6, D // 12):
        leading = averages[..., :prefix]
        centred = leading - lax.optimization_barrier(jnp.mean(leading, axis=-1, keepdims=True))
        pieces.append(centred * lax.rsqrt(lax.optimization_barrier(jnp.mean(centred * centred, axis=-1, keepdims=True)) + pool_eps))
    return jnp.concatenate(pieces, axis=-1)

def pool_rows(outputs, seg_row):
    labels = jnp.arange(1, NSEG + 1, dtype=jnp.int32)
    onehot = (seg_row[None, :] == labels[:, None]).astype(jnp.float32)
    seg_sums = matmul(onehot, outputs)
    seg_counts = lax.optimization_barrier(jnp.sum(onehot, axis=1))
    return matryoshka(seg_sums / seg_counts[:, None])

def add_arrays(accumulated, current):
    return accumulated + current

def reference(tokens, segments, query_weight, query_bias, key_weight, value_weight, value_bias, out_weight, out_bias, first_gain, first_shift, up_weight, up_bias, down_weight, down_bias, second_gain, second_shift, cotangent):
    params = tuple((member.astype(jnp.float32) for member in (query_weight, query_bias, key_weight, value_weight, value_bias, out_weight, out_bias, first_gain, first_shift, up_weight, up_bias, down_weight, down_bias, second_gain, second_shift)))

    def one_sequence(grad_sums, row_data):
        token_row, seg_row, cot_row = row_data
        inputs = token_row.astype(jnp.float32)

        def apply_layer(param_set, layer_in):
            return forward_layer(param_set, layer_in, seg_row)
        outputs, pullback = jax.vjp(apply_layer, params, inputs)
        grads_params, grad_input = pullback(cot_row.astype(jnp.float32))
        grad_sums = jax.tree.map(add_arrays, grad_sums, grads_params)
        return (grad_sums, (outputs.astype(jnp.bfloat16), pool_rows(outputs, seg_row), grad_input.astype(jnp.bfloat16)))
    zero_grads = jax.tree.map(jnp.zeros_like, params)
    sums_out, stacked = lax.scan(one_sequence, zero_grads, (tokens, segments, cotangent))
    layer_output, pooled, grad_tokens = stacked
    return (layer_output, pooled, grad_tokens, sums_out[0], sums_out[1], sums_out[2], sums_out[3], sums_out[4], sums_out[5], sums_out[6], sums_out[7], sums_out[8], sums_out[9], sums_out[10], sums_out[11], sums_out[12], sums_out[13], sums_out[14])
```

```python
from functools import partial

import jax
import jax.numpy as jnp
from jax import lax
from jax.sharding import PartitionSpec as P

D = 768
H = 12
HD = 64
NSEG = 6

query_scale = 0.125
norm_eps = 1e-12
pool_eps = 1e-06
bf16 = jnp.bfloat16
f32 = jnp.float32


def matmul(left, right):
    return jnp.dot(left, right, preferred_element_type=f32)


def layer_norm(rows_in, gain_vec, shift_vec):
    row_mean = jnp.mean(rows_in, axis=-1, keepdims=True)
    centred = rows_in - row_mean
    inverse = lax.rsqrt(jnp.mean(centred * centred, axis=-1, keepdims=True) + norm_eps)
    normed = centred * inverse
    return (normed * gain_vec + shift_vec, normed, inverse)


def norm_backward(upstream, normed, inverse, gain_vec):
    scaled = upstream * gain_vec
    first_mean = jnp.mean(scaled, axis=-1, keepdims=True)
    second_mean = jnp.mean(scaled * normed, axis=-1, keepdims=True)
    return inverse * (scaled - first_mean - normed * second_mean)


def matryoshka(averages):
    pieces = []
    for prefix in (D, D * 2 // 3, D // 3, D // 6, D // 12):
        leading = averages[..., :prefix]
        centred = leading - jnp.mean(leading, axis=-1, keepdims=True)
        pieces.append(
            centred * lax.rsqrt(jnp.mean(centred * centred, axis=-1, keepdims=True) + pool_eps)
        )
    return jnp.concatenate(pieces, axis=-1)


def swap(value, axis, size, distance):
    return lax.ppermute(value, axis, [(i, i ^ distance) for i in range(size)])


def part_of(value, index, count):
    rows = value.shape[0] // count
    return lax.dynamic_slice_in_dim(value, index * rows, rows, 0)


def ordered(bit, mine, theirs):
    return jnp.where(
        bit == 0,
        jnp.concatenate([mine, theirs], 0),
        jnp.concatenate([theirs, mine], 0),
    )


class Links:
    def __init__(self, n_rows, n_blk):
        self.size = {"rows": n_rows, "blk": n_blk}
        self.at = {"rows": lax.axis_index("rows"), "blk": lax.axis_index("blk")}
        row_bits = [("rows", 1 << k) for k in range(n_rows.bit_length() - 1)]
        self.near, self.far = row_bits[:1], row_bits[1:]
        self.blk_bits = [("blk", 1 << k) for k in range(n_blk.bit_length() - 1)]

    def bit(self, stage):
        axis, distance = stage
        return (self.at[axis] // distance) % 2

    def swap(self, value, stage):
        axis, distance = stage
        return swap(value, axis, self.size[axis], distance)

    def halve(self, value, stage):
        bit = self.bit(stage)
        received = self.swap(part_of(value, 1 - bit, 2), stage)
        return (part_of(value, bit, 2).astype(f32) + received.astype(f32)).astype(bf16)

    def double(self, value, stage):
        return ordered(self.bit(stage), value, self.swap(value, stage))

    def all_reduce(self, value):
        for stage in self.near:
            value = self.halve(value, stage)
        half = value.shape[0] // 2
        left, right = value[:half], value[half:]
        for stage, other in zip(self.far, self.far[::-1]):
            left, right = self.halve(left, stage), self.halve(right, other)
        half = left.shape[0]
        value = jnp.concatenate([left, right], 0)
        for stage in self.blk_bits:
            value = self.halve(value, stage)
        for stage in self.blk_bits[::-1]:
            value = self.double(value, stage)
        left, right = value[:half], value[half:]
        for stage, other in zip(self.far[::-1], self.far):
            left, right = self.double(left, stage), self.double(right, other)
        value = jnp.concatenate([left, right], 0)
        for stage in self.near:
            value = self.double(value, stage)
        return value.astype(f32)

    def sum_small(self, value):
        for stage in self.blk_bits + self.near + self.far:
            value = value + self.swap(value, stage)
        return value


def local(
    n_rows,
    n_blk,
    tokens,
    segments,
    query_weight,
    query_bias,
    key_weight,
    value_weight,
    value_bias,
    out_weight,
    out_bias,
    first_gain,
    first_shift,
    up_weight,
    up_bias,
    down_weight,
    down_bias,
    second_gain,
    second_shift,
    cotangent,
):
    links = Links(n_rows, n_blk)
    pair, cross = ("blk", 1), ("blk", 2)
    blk_at = links.at["blk"]
    seq_at = blk_at // 2
    num_seq, tok_rows, width = tokens.shape
    ff = up_weight.shape[1]
    total_rows = 2 * tok_rows

    own = lax.dynamic_index_in_dim(tokens, seq_at, 0, keepdims=False)
    far_block = links.swap(lax.dynamic_index_in_dim(tokens, 1 - seq_at, 0, keepdims=False), cross)
    near_block = links.swap(own, pair)
    last_block = links.swap(far_block, pair)
    seg_pair = jnp.stack([segments, links.swap(segments, pair)])
    seg_cross = links.swap(seg_pair, cross)
    seg_mine = lax.dynamic_index_in_dim(seg_pair, seq_at, 1, keepdims=False)
    seg_far = lax.dynamic_index_in_dim(seg_cross, seq_at, 1, keepdims=False)
    seg_keys = jnp.concatenate([seg_mine[0], seg_far[0], seg_mine[1], seg_far[1]], 0)
    seg_query = seg_keys[:total_rows]
    cot_own = lax.dynamic_index_in_dim(cotangent, seq_at, 0, keepdims=False)
    cot_far = links.swap(lax.dynamic_index_in_dim(cotangent, 1 - seq_at, 0, keepdims=False), cross)
    upstream = jnp.concatenate([cot_own, cot_far], 0).astype(f32)

    flat_all = jnp.concatenate([own, far_block, near_block, last_block], 0)
    flat_in = flat_all[:total_rows]
    queries = (query_scale * (matmul(flat_in, query_weight) + query_bias)).astype(bf16)
    keys = matmul(flat_all, key_weight).astype(bf16)
    values = (matmul(flat_all, value_weight) + value_bias).astype(bf16)
    q_heads = queries.reshape(total_rows, H, HD)
    k_heads = keys.reshape(-1, H, HD)
    v_heads = values.reshape(-1, H, HD)
    allowed = seg_query[:, None] == seg_keys[None, :]

    def weights_of():
        scores = jnp.einsum("qhd,khd->hqk", q_heads, k_heads, preferred_element_type=f32)
        return jnp.where(allowed[None], jnp.exp(scores), 0.0)

    expo = weights_of()
    totals = jnp.transpose(jnp.sum(expo, axis=2))[..., None]
    numer = jnp.einsum("hqk,khd->qhd", expo.astype(bf16), v_heads, preferred_element_type=f32)
    attended = numer / totals
    attended_low = attended.reshape(total_rows, width).astype(bf16)
    branch = matmul(attended_low, out_weight) + out_bias
    hidden, normed_one, inverse_one = layer_norm(
        flat_in.astype(f32) + branch, first_gain, first_shift
    )
    hidden_low = hidden.astype(bf16)
    preact = matmul(hidden_low, up_weight) + up_bias
    activation_full, gelu_pull = jax.vjp(partial(jax.nn.gelu, approximate=False), preact)
    activation = activation_full.astype(bf16)
    feed_out = matmul(activation, down_weight) + down_bias
    outputs, normed_two, inverse_two = layer_norm(hidden + feed_out, second_gain, second_shift)

    labels = jnp.arange(1, NSEG + 1, dtype=jnp.int32)
    onehot = (seg_query[None, :] == labels[:, None]).astype(f32)
    seg_sums = jnp.dot(onehot, outputs, precision=lax.Precision.HIGHEST)
    counts = jnp.sum((seg_keys[None, :] == labels[:, None]).astype(f32), axis=1)
    seg_sums = seg_sums + links.swap(seg_sums, pair)
    pooled_one = seg_sums / counts[:, None]
    pooled_two = links.swap(pooled_one, cross)
    pooled = matryoshka(ordered(seq_at, pooled_one[None], pooled_two[None]))

    out_low = outputs.astype(bf16)
    out_back = links.swap(out_low[tok_rows:], cross)
    layer_output = ordered(seq_at, out_low[:tok_rows][None], out_back[None])

    grad_second_gain = jnp.sum(upstream * normed_two, axis=0)
    grad_second_shift = jnp.sum(upstream, axis=0)
    d_resid_two = norm_backward(upstream, normed_two, inverse_two, second_gain)
    d_feed = d_resid_two.astype(bf16)
    grad_down_weight = jnp.einsum("rf,rd->fd", activation, d_feed, preferred_element_type=f32)
    grad_down_bias = jnp.sum(d_feed.astype(f32), axis=0)
    d_activation = jnp.einsum("rd,fd->rf", d_feed, down_weight, preferred_element_type=f32)
    d_preact = gelu_pull(d_activation)[0].astype(bf16)
    up_parts = [
        jnp.einsum(
            "rd,rf->df", hidden_low, d_preact[:, k * width : (k + 1) * width],
            preferred_element_type=f32,
        ).astype(bf16)
        for k in range(ff // width)
    ]
    grad_up_bias = jnp.sum(d_preact.astype(f32), axis=0)
    d_hidden = d_resid_two + jnp.einsum(
        "rf,df->rd", d_preact, up_weight, preferred_element_type=f32
    )
    grad_first_gain = jnp.sum(d_hidden * normed_one, axis=0)
    grad_first_shift = jnp.sum(d_hidden, axis=0)
    d_resid_one = norm_backward(d_hidden, normed_one, inverse_one, first_gain)
    d_branch = d_resid_one.astype(bf16)
    grad_out_weight = jnp.einsum("rd,re->de", attended_low, d_branch, preferred_element_type=f32)
    grad_out_bias = jnp.sum(d_branch.astype(f32), axis=0)
    d_attended = jnp.einsum(
        "re,de->rd", d_branch, out_weight, preferred_element_type=f32
    ).reshape(total_rows, H, HD)
    d_total = -jnp.sum(d_attended * attended, axis=2, keepdims=True) / totals
    d_numer = (d_attended / totals).astype(bf16)

    expo = weights_of()
    d_prob = jnp.einsum("qhd,khd->hqk", d_numer, v_heads, preferred_element_type=f32)
    d_scores = (expo * (d_prob + jnp.transpose(d_total, (1, 0, 2)))).astype(bf16)
    d_query = jnp.einsum("hqk,khd->qhd", d_scores, k_heads, preferred_element_type=f32)
    d_query = d_query.reshape(total_rows, width).astype(bf16) * query_scale
    d_key = jnp.einsum("hqk,qhd->khd", d_scores, q_heads, preferred_element_type=f32)
    d_key = d_key.reshape(-1, width).astype(bf16)
    d_value = jnp.einsum("hqk,qhd->khd", expo.astype(bf16), d_numer, preferred_element_type=f32)
    d_value = d_value.reshape(-1, width).astype(bf16)

    def outer(left, right):
        return jnp.einsum("rd,re->de", left, right, preferred_element_type=f32).astype(bf16)

    attn_parts = [
        outer(flat_in, d_query),
        outer(flat_all, d_key),
        outer(flat_all, d_value),
        grad_out_weight.astype(bf16),
    ]
    grad_query_bias = jnp.sum(d_query.astype(f32), axis=0)
    grad_value_bias = jnp.sum(d_value.astype(f32), axis=0)

    def back(left, weight):
        return jnp.einsum("re,de->rd", left, weight, preferred_element_type=f32)

    d_mine = (
        d_resid_one
        + back(d_query, query_weight)
        + back(d_key[:total_rows], key_weight)
        + back(d_value[:total_rows], value_weight)
    )
    d_pair = back(d_key[total_rows:], key_weight) + back(d_value[total_rows:], value_weight)
    d_mine = (d_mine + links.swap(d_pair.astype(bf16), pair).astype(f32)).astype(bf16)
    d_back = links.swap(d_mine[tok_rows:], cross)
    grad_tokens = ordered(seq_at, d_mine[:tok_rows][None], d_back[None])

    vectors = [
        grad_query_bias, grad_value_bias, grad_out_bias, grad_first_gain, grad_first_shift,
        grad_down_bias, grad_second_gain, grad_second_shift,
    ]
    small = jnp.concatenate([v[None] for v in vectors] + [grad_up_bias.reshape(-1, width)], 0)
    small = links.sum_small(small)
    down_sum = links.all_reduce(grad_down_weight.astype(bf16))
    up_sum = links.all_reduce(jnp.concatenate(up_parts, 0))
    attn_sum = links.all_reduce(jnp.concatenate(attn_parts, 0))
    up_sum = jnp.concatenate(jnp.split(up_sum, ff // width, 0), 1)
    query_sum, key_sum, value_sum, out_sum = jnp.split(attn_sum, 4, 0)
    return (
        layer_output,
        pooled,
        grad_tokens,
        query_sum,
        small[0],
        key_sum,
        value_sum,
        small[1],
        out_sum,
        small[2],
        small[3],
        small[4],
        up_sum,
        small[8:].reshape(-1),
        down_sum,
        small[5],
        small[6],
        small[7],
    )


def solution(mesh):
    row_split = P("rows", "blk", None)
    return jax.shard_map(
        partial(local, mesh.shape["rows"], mesh.shape["blk"]),
        mesh=mesh,
        in_specs=(row_split, P("rows", "blk")) + (P(),) * 15 + (row_split,),
        out_specs=(row_split, P("rows", None, None), row_split) + (P(),) * 15,
        check_vma=False,
    )
```

```python
from functools import partial

import jax
import jax.numpy as jnp
from jax import lax
from jax.experimental import pallas as pl
from jax.experimental.pallas import tpu as pltpu
from jax.sharding import PartitionSpec as P

f32=jnp.float32; bf16=jnp.bfloat16
norm_eps=1e-12
NSEG=6
HD=64
def dot(a,b): return jnp.dot(a,b,preferred_element_type=f32)
def dot_nt(a,b): return lax.dot_general(a,b,(((1,),(1,)),((),())),preferred_element_type=f32)
def dot_tn(a,b): return lax.dot_general(a,b,(((0,),(0,)),((),())),preferred_element_type=f32)

def gelu_pair(x):
    t = 1.0 / (1.0 + (0.3275911 * 0.7071067811865476) * jnp.abs(x))
    e = jnp.exp(-0.5 * x * x)
    half = (0.5*0.254829592) + t*((0.5*-0.284496736) + t*((0.5*1.421413741) + t*((0.5*-1.453152027) + t*(0.5*1.061405429))))
    tail = half * t * e
    cdf = jnp.where(x > 0, 1.0 - tail, tail)
    return x * cdf, cdf + x * e * 0.3989422804014327

def in_hbm(*arrays):
    return tuple(pltpu.with_memory_space_constraint(a, pltpu.HBM) for a in arrays)

def wide(rows):
    return jnp.concatenate([rows[i:i+1,:] for i in range(rows.shape[0])], axis=1)

def same_segment(left, right):
    lab = lax.broadcasted_iota(jnp.int32, (8, 1), 0)
    hot = lambda s: (lab == s).astype(f32).astype(bf16)
    return (dot_tn(hot(left), hot(right)) - 1.0) * 1e30

OUT_B, G1, B1, DOWN_B, G2, B2, UP_B = range(7)
RB = 128

def rows_norm(r):
    m = jnp.mean(r, axis=-1, keepdims=True)
    c = r - m
    inv = lax.rsqrt(jnp.mean(c*c, axis=-1, keepdims=True) + norm_eps)
    return c * inv, inv

def norm_back(g, xh, inv):
    return inv * (g - jnp.mean(g, axis=-1, keepdims=True) - xh * jnp.mean(g*xh, axis=-1, keepdims=True))

def col_sum(v): return jnp.sum(v, axis=0, keepdims=True)

def mid_kernel(order_ref, att_ref, xa_ref, xb_ref, cota_ref, cotb_ref, itot_ref, seg_ref, ob_ref, g1_ref, b1_ref, db_ref, g2_ref, b2_ref, ub_ref, wo_hbm, wu_hbm, wd_hbm,
               out_ref, segsum_ref, small_ref, dres_ref, dn_ref, dt_ref, gout_ref, gsend_hbm, gkeep_hbm,
               wo, wu, wd, hid, hl, xh1, rs1, act, gp, feed, dfl, dhid, stage, wsem, gsem):
    R, W = att_ref.shape
    nc = wu.shape[0]
    def rows_of(a, b, i):
        h = a.shape[0] // RB
        return a[pl.ds(i*RB,RB),:] if i < h else b[pl.ds((i-h)*RB,RB),:]
    def copies(k):
        c = order_ref[k]
        return (pltpu.make_async_copy(wu_hbm.at[:, pl.ds(c*W, W)], wu.at[k], wsem.at[1+k]),
                pltpu.make_async_copy(wd_hbm.at[pl.ds(c*W, W), :], wd.at[k], wsem.at[1+nc+k]))
    cwo = pltpu.make_async_copy(wo_hbm, wo, wsem.at[0]); cwo.start()
    for k in range(nc):
        for cp in copies(k): cp.start()
    NB = R // RB
    vecs = (ob_ref, g1_ref, b1_ref, db_ref, g2_ref, b2_ref)
    row = lambda i: wide(vecs[i][...])
    lanes = W // 128
    cwo.wait()
    for i in range(NB):
        s = pl.ds(i*RB, RB)
        r = rows_of(xa_ref, xb_ref, i).astype(f32) + dot(att_ref[s, :].astype(bf16), wo[...]) + row(OUT_B)
        xh, inv = rows_norm(r)
        xh1[s,:] = xh
        rs1[s,:] = inv
        h = xh * row(G1) + row(B1)
        hid[s,:] = h
        hl[s,:] = h.astype(bf16)
    for k in range(nc):
        for cp in copies(k): cp.wait()
        ub = wide(ub_ref[pl.ds(order_ref[k]*lanes, lanes), :])
        for j in range(W//256):
            cs = slice(j*256, (j+1)*256)
            pre = dot(hl[...], wu[k, :, cs]) + ub[:, cs]
            a_, g_ = gelu_pair(pre)
            act[k, :, cs] = a_.astype(bf16)
            gp[k, :, cs] = g_.astype(gp.dtype)
        part = dot(act[k], wd[k])
        if k == 0: feed[...] = part
        else: feed[...] += part
    lab = lax.broadcasted_iota(jnp.int32, (8, 1), 0) + 1
    zero = jnp.zeros((1,W),f32)
    segsum = jnp.zeros((8, W), f32)
    sg = ss = sdb = zero
    for i in range(NB):
        s = pl.ds(i*RB, RB)
        xh, inv = rows_norm(hid[s,:] + feed[s,:] + row(DOWN_B))
        o = xh * row(G2) + row(B2)
        oh = o.astype(bf16)
        out_ref[s,:] = oh
        ol = (o - oh.astype(f32)).astype(bf16)
        hot = (lab == seg_ref[:, i*RB:(i+1)*RB]).astype(f32).astype(bf16)
        segsum = segsum + dot(hot, oh) + dot(hot, ol)
        u = rows_of(cota_ref, cotb_ref, i).astype(f32)
        sg = sg + col_sum(u*xh)
        ss = ss + col_sum(u)
        d = norm_back(u * row(G2), xh, inv)
        dhid[s,:] = d
        dl = d.astype(bf16)
        dfl[s,:] = dl
        sdb = sdb + col_sum(dl.astype(f32))
    segsum_ref[...] = segsum
    small_ref[pl.ds(DOWN_B,1), :] = sdb
    small_ref[pl.ds(G2,1), :] = sg
    small_ref[pl.ds(B2,1), :] = ss
    half = nc // 2
    def push(slot, k, kind):
        dst = gsend_hbm if k < half else gkeep_hbm
        return pltpu.make_async_copy(stage.at[slot], dst.at[pl.ds((2*(k % half) + kind)*W, W), :], gsem.at[slot])
    for k in range(nc):
        stage[k] = dot_tn(act[k], dfl[...]).astype(bf16)
        push(k, k, 0).start()
        da = dot_nt(dfl[...], wd[k])
        dp = (da * gp[k].astype(f32)).astype(bf16)
        act[k] = dp
        small_ref[pl.ds(UP_B + order_ref[k],1), :] = col_sum(dp.astype(f32))
        stage[nc+k] = dot_tn(hl[...], dp).astype(bf16)
        push(nc+k, k, 1).start()
        dhid[...] += dot_nt(dp, wu[k])
    sg = ss = sdb = zero
    for i in range(NB):
        s = pl.ds(i*RB, RB)
        dh = dhid[s,:]
        xh = xh1[s,:]
        sg = sg + col_sum(dh*xh)
        ss = ss + col_sum(dh)
        d = norm_back(dh * row(G1), xh, rs1[s,:])
        dres_ref[s,:] = d
        dl = d.astype(bf16)
        dfl[s,:] = dl
        sdb = sdb + col_sum(dl.astype(f32))
    small_ref[pl.ds(OUT_B,1), :] = sdb
    small_ref[pl.ds(G1,1), :] = sg
    small_ref[pl.ds(B1,1), :] = ss
    gout_ref[...] = dot_tn(att_ref[...].astype(bf16), dfl[...]).astype(bf16)
    l0 = lax.broadcasted_iota(jnp.int32, (128,128), 0) // HD
    l1 = lax.broadcasted_iota(jnp.int32, (128,128), 1) // HD
    same = (l0 == l1).astype(f32).astype(bf16)
    for i in range(NB):
        s = pl.ds(i*RB, RB)
        da = dot_nt(dfl[s,:], wo[...])
        it = itot_ref[s,:]
        dn_ref[s,:] = (da * it).astype(bf16)
        p = da * att_ref[s,:]
        ph = p.astype(bf16)
        plow = (p - ph.astype(f32)).astype(bf16)
        for j in range(W//128):
            cs = slice(j*128,(j+1)*128)
            dt_ref[s, cs] = -(dot(ph[:,cs], same) + dot(plow[:,cs], same)) * it[:,cs]
    for k in range(nc):
        push(k, k, 0).wait()
        push(nc+k, k, 1).wait()

def mid(order, att, x, cot, itot, seg_row, vecs, wo, wu, wd):
    R, W = att.shape
    nc = wu.shape[1] // W
    any_ = pl.BlockSpec(memory_space=pltpu.HBM)
    vm = pl.BlockSpec(memory_space=pltpu.VMEM)
    sm = pl.BlockSpec(memory_space=pltpu.SMEM)
    sd = jax.ShapeDtypeStruct
    return pl.pallas_call(
        mid_kernel,
        in_specs=[sm]+[vm]*14+[any_]*3,
        out_specs=[vm]*7+[any_, any_],
        out_shape=[sd((R,W),bf16), sd((8,W),f32), sd((UP_B+nc+6,W),f32), sd((R,W),f32), sd((R,W),bf16), sd((R,W),f32),
                   sd((W,W),bf16), sd((nc*W,W),bf16), sd((nc*W,W),bf16)],
        scratch_shapes=[pltpu.VMEM((W,W),bf16), pltpu.VMEM((nc,W,W),bf16), pltpu.VMEM((nc,W,W),bf16),
                        pltpu.VMEM((R,W),f32), pltpu.VMEM((R,W),bf16), pltpu.VMEM((R,W),f32), pltpu.VMEM((R,1),f32),
                        pltpu.VMEM((nc,R,W),bf16), pltpu.VMEM((nc,R,W),f32), pltpu.VMEM((R,W),f32), pltpu.VMEM((R,W),bf16), pltpu.VMEM((R,W),f32),
                        pltpu.VMEM((2*nc,W,W),bf16), pltpu.SemaphoreType.DMA((1+2*nc,)), pltpu.SemaphoreType.DMA((2*nc,))],
        compiler_params=pltpu.CompilerParams(vmem_limit_bytes=60*1024*1024),
        name="mid",
    )(order, *in_hbm(att, *x, *cot, itot), seg_row, *vecs, wo, wu, wd)

GW = 256
def head_pair_lanes():
    return lax.broadcasted_iota(jnp.int32, (1,128), 1) < HD

def gather_rows(refs, dst, sem):
    at, copies = 0, []
    for i, ref in enumerate(refs):
        copies.append(pltpu.make_async_copy(ref, dst.at[pl.ds(at, ref.shape[0]), :], sem.at[i]))
        at += ref.shape[0]
    return copies

def attn_fwd_kernel(n_parts, *refs):
    parts = refs[:n_parts]
    (wq_ref, wk_ref, wv_ref, qb_ref, vb_ref, sk_ref,
     q_ref, k_ref, v_ref, att_ref, itot_ref, bias, x_ref, sem) = refs[n_parts:]
    R = q_ref.shape[0]
    @pl.when(pl.program_id(0) == 0)
    def _():
        copies = gather_rows(parts, x_ref, sem)
        for c in copies: c.start()
        bias[...] = same_segment(sk_ref[:, 0:R], sk_ref[...])
        for c in copies: c.wait()
    lanes = GW // 128
    at = pl.ds(pl.program_id(0)*lanes, lanes)
    qb, vb = wide(qb_ref[at, :]), wide(vb_ref[at, :])
    q = (0.125*(dot(x_ref[0:R,:], wq_ref[...]) + qb)).astype(bf16)
    k = dot(x_ref[...], wk_ref[...]).astype(bf16)
    v = (dot(x_ref[...], wv_ref[...]) + vb).astype(bf16)
    q_ref[...] = q; k_ref[...] = k; v_ref[...] = v
    first = head_pair_lanes()
    for p in range(GW//128):
        cs = slice(p*128,(p+1)*128)
        qp, kp, vp = q[:,cs], k[:,cs], v[:,cs]
        one = jnp.ones_like(vp); zero=jnp.zeros_like(qp)
        res = []
        for h in range(2):
            mine = first if h==0 else jnp.logical_not(first)
            s = dot_nt(jnp.where(mine, qp, zero), kp)
            e = jnp.exp(s + bias[...]).astype(bf16)
            res.append(dot(e, jnp.where(mine, vp, one)))
        num = jnp.where(first, res[0], res[1])
        tot = pltpu.roll(jnp.where(first, res[1], res[0]), HD, 1)
        it = 1.0 / tot
        att_ref[:,cs] = num * it
        itot_ref[:,cs] = it

def attn_fwd(parts, wq, wk, wv, qb, vb, sk, R):
    W = wq.shape[0]
    N = sum(p.shape[0] for p in parts)
    sd = jax.ShapeDtypeStruct
    full = lambda a: pl.BlockSpec(a.shape, lambda j: (0,0))
    col = lambda r: pl.BlockSpec((r,GW), lambda j: (0,j))
    return pl.pallas_call(
        partial(attn_fwd_kernel, len(parts)), grid=(W//GW,),
        in_specs=[pl.BlockSpec(memory_space=pltpu.HBM)]*len(parts)+[col(W), col(W), col(W), full(qb), full(vb), full(sk)],
        out_specs=[col(R), col(N), col(N), col(R), col(R)],
        out_shape=[sd((R,W),bf16), sd((N,W),bf16), sd((N,W),bf16), sd((R,W),f32), sd((R,W),f32)],
        scratch_shapes=[pltpu.VMEM((R,N),f32), pltpu.VMEM((N,W),bf16), pltpu.SemaphoreType.DMA((len(parts),))],
        compiler_params=pltpu.CompilerParams(vmem_limit_bytes=24*1024*1024, dimension_semantics=("arbitrary",)),
        name="attn_fwd",
    )(*parts, *in_hbm(wq, wk, wv), qb, vb, sk)

def attn_bwd_kernel(q_ref, k_ref, v_ref, dn_ref, dt_ref, sk_ref, dq_ref, dk_ref, dv_ref, bias):
    @pl.when(pl.program_id(0) == 0)
    def _():
        bias[...] = same_segment(sk_ref[...], sk_ref[:, 0:q_ref.shape[0]])
    first = head_pair_lanes()
    lane = lax.broadcasted_iota(jnp.int32, (1,128), 1)
    for p in range(q_ref.shape[1]//128):
        cs = slice(p*128,(p+1)*128)
        qp, kp, vp, dnp = q_ref[:,cs], k_ref[:,cs], v_ref[:,cs], dn_ref[:,cs]
        dtr = pltpu.roll(dt_ref[:,cs], HD, 1)
        hi = dtr.astype(bf16)
        rest = dtr - hi.astype(f32)
        mid_ = rest.astype(bf16)
        low = (rest - mid_.astype(f32)).astype(bf16)
        res=[]
        for h in range(2):
            mine = first if h==0 else jnp.logical_not(first)
            o = HD if h==0 else 0
            ex = jnp.where(lane==o, hi, jnp.where(lane==o+1, mid_, jnp.where(lane==o+2, low, jnp.zeros_like(hi))))
            dne = jnp.where(mine, dnp, ex)
            ve = jnp.where(mine, vp, jnp.where((lane>=o)&(lane<o+3), jnp.ones_like(vp), jnp.zeros_like(vp)))
            s = dot_nt(jnp.where(mine, kp, jnp.zeros_like(kp)), qp)
            e = jnp.exp(s + bias[...])
            pr = dot_nt(ve, dne)
            ds = (e * pr).astype(bf16)
            dv = dot(e.astype(bf16), dnp)
            dk = dot(ds, qp)
            dq = dot_tn(ds, kp)
            res.append((dq,dk,dv))
        dq_ref[:,cs] = (jnp.where(first, res[0][0], res[1][0]).astype(bf16).astype(f32)*0.125).astype(bf16)
        dk_ref[:,cs] = jnp.where(first, res[0][1], res[1][1]).astype(bf16)
        dv_ref[:,cs] = jnp.where(first, res[0][2], res[1][2]).astype(bf16)

def attn_bwd(q,k,v,dn,dt,sk,start,count):
    R,W=q.shape; N=k.shape[0]
    sd = jax.ShapeDtypeStruct
    full = lambda a: pl.BlockSpec(a.shape, lambda j: (0,0))
    GB=128
    col = lambda r: pl.BlockSpec((r,GB), lambda j: (0,j+start))
    out = lambda r: pl.BlockSpec((r,GB), lambda j: (0,j))
    return pl.pallas_call(
        attn_bwd_kernel, grid=(count,),
        in_specs=[col(R), col(N), col(N), col(R), col(R), full(sk)],
        out_specs=[out(R), out(N), out(N)],
        out_shape=[sd((R,GB*count),bf16), sd((N,GB*count),bf16), sd((N,GB*count),bf16)],
        scratch_shapes=[pltpu.VMEM((N,R),f32)],
        compiler_params=pltpu.CompilerParams(vmem_limit_bytes=20*1024*1024, dimension_semantics=("arbitrary",)),
        name="attn_bwd",
    )(*in_hbm(q,k,v,dn,dt),sk)

def proj_bwd_kernel(n_parts, *refs):
    tokens = refs[:n_parts]
    (bit_ref, dqa_ref, dqb_ref, dka_ref, dkb_ref, dva_ref, dvb_ref, wq_ref, wk_ref, wv_ref, dres_ref, gout_ref,
     mine_ref, pair_ref, bsum_ref, gsend_hbm, gkeep_hbm, stage, x_ref, sem, xsem) = refs[n_parts:]
    copies = gather_rows(tokens, x_ref, xsem)
    for c in copies: c.start()
    R, CA = dqa_ref.shape
    W = x_ref.shape[1]
    bit = bit_ref[0]
    parts = (slice(0,CA), slice(CA,W))
    def push(i, start):
        src = gout_ref if i == 3 else stage.at[i]
        def go(dst):
            cp = pltpu.make_async_copy(src, dst.at[pl.ds((i%2)*W, W), :], sem.at[i])
            cp.start() if start else cp.wait()
        @pl.when(bit == i//2)
        def _(): go(gkeep_hbm)
        @pl.when(bit != i//2)
        def _(): go(gsend_hbm)
    push(3, True)
    for c in copies: c.wait()
    for i, refs in ((2,(dva_ref,dvb_ref)), (1,(dka_ref,dkb_ref)), (0,(dqa_ref,dqb_ref))):
        for ref, cs in zip(refs, parts):
            n = ref.shape[0]
            stage[i, :, cs] = dot_tn(x_ref[0:n,:], ref[...]).astype(bf16)
        push(i, True)
    def back(refs, w_ref, rows):
        return dot_nt(refs[0][rows,:], w_ref[:,parts[0]]) + dot_nt(refs[1][rows,:], w_ref[:,parts[1]])
    top, rest = slice(0,R), slice(R,2*R)
    pair_ref[...] = (back((dka_ref,dkb_ref), wk_ref, rest) + back((dva_ref,dvb_ref), wv_ref, rest)).astype(bf16)
    mine_ref[...] = (dres_ref[...] + back((dqa_ref,dqb_ref), wq_ref, top) + back((dka_ref,dkb_ref), wk_ref, top)
                     + back((dva_ref,dvb_ref), wv_ref, top))
    for ref, cs in zip((dqa_ref,dqb_ref), parts): bsum_ref[0:1,cs] = col_sum(ref[...].astype(f32))
    for ref, cs in zip((dva_ref,dvb_ref), parts): bsum_ref[1:2,cs] = col_sum(ref[...].astype(f32))
    for i in range(4): push(i, False)

def proj_bwd(bit, grads, tokens, wq, wk, wv, dres, gout):
    R, W = dres.shape
    any_ = pl.BlockSpec(memory_space=pltpu.HBM)
    vm = pl.BlockSpec(memory_space=pltpu.VMEM)
    sm = pl.BlockSpec(memory_space=pltpu.SMEM)
    sd = jax.ShapeDtypeStruct
    return pl.pallas_call(
        partial(proj_bwd_kernel, len(tokens)),
        in_specs=[any_]*len(tokens)+[sm]+[vm]*11, out_specs=[vm,vm,vm,any_,any_],
        out_shape=[sd((R,W),f32), sd((R,W),bf16), sd((2,W),f32), sd((2*W,W),bf16), sd((2*W,W),bf16)],
        scratch_shapes=[pltpu.VMEM((3,W,W),bf16), pltpu.VMEM((2*R,W),bf16), pltpu.SemaphoreType.DMA((4,)), pltpu.SemaphoreType.DMA((len(tokens),))],
        compiler_params=pltpu.CompilerParams(vmem_limit_bytes=32*1024*1024),
        name="proj_bwd",
    )(*tokens, bit, *in_hbm(*grads, wq, wk, wv, dres, gout))

def emit_kernel(up_from, n_prev, place_ref, own_m, own_r, oth_m, oth_r, *refs):
    outs, stage, sem = refs[n_prev:-2], refs[-2], refs[-1]
    n, W = own_m.shape
    bit = place_ref[0]
    mine, theirs = place_ref[1], place_ref[2]
    pieces = ((bit, mine, own_m), (bit, 1 - mine, own_r), (1 - bit, theirs, oth_m), (1 - bit, 1 - theirs, oth_r))
    def send(i, start):
        half, block, ref = pieces[i]
        for b in range(2):
            for h in range(2):
                if up_from is None: dst = outs[2*h + b]
                elif b == 0: dst = outs[0].at[pl.ds((2*h + up_from)*W, W), :]
                else: dst = outs[1].at[:, pl.ds((2*h + up_from)*W, W)]
                @pl.when((half == h) & (block == b))
                def _():
                    cp = pltpu.make_async_copy(stage.at[i], dst, sem.at[i])
                    cp.start() if start else cp.wait()
    for i, (half, block, ref) in enumerate(pieces):
        stage[i] = ref[...].astype(f32)
        send(i, True)
    for i in range(len(pieces)): send(i, False)

def emit(place, pieces, out_shape, up_from=None, prev=()):
    n, W = pieces[0].shape
    any_ = pl.BlockSpec(memory_space=pltpu.HBM)
    vm = pl.BlockSpec(memory_space=pltpu.VMEM)
    sm = pl.BlockSpec(memory_space=pltpu.SMEM)
    return pl.pallas_call(
        partial(emit_kernel, up_from, len(prev)),
        in_specs=[sm]+[vm]*4+[any_]*len(prev), out_specs=[any_]*len(out_shape),
        out_shape=[jax.ShapeDtypeStruct(s, f32) for s in out_shape],
        input_output_aliases={5+i: i for i in range(len(prev))},
        scratch_shapes=[pltpu.VMEM((4,n,W),f32), pltpu.SemaphoreType.DMA((4,))],
        compiler_params=pltpu.CompilerParams(vmem_limit_bytes=24*1024*1024),
        name="emit",
    )(place, *pieces, *prev)

def split_kernel(groups, bit_ref, keep_hbm, recv_hbm, *refs):
    outs, (a, b, o, sem) = refs[:2*groups], refs[2*groups:]
    n, W = outs[0].shape
    bit = bit_ref[0]
    def load(i):
        half = bit if i % 2 else 1 - bit
        src = pl.ds(((i//2)*2 + half)*n, n)
        return (pltpu.make_async_copy(keep_hbm.at[src, :], a.at[i], sem.at[0, i]),
                pltpu.make_async_copy(recv_hbm.at[src, :], b.at[i], sem.at[1, i]))
    for i in range(2*groups):
        for c in load(i): c.start()
    for i in range(2*groups):
        for c in load(i): c.wait()
        o[i] = (a[i].astype(f32) + b[i].astype(f32)).astype(bf16)
        pltpu.make_async_copy(o.at[i], outs[i], sem.at[2, i]).start()
    for i in range(2*groups): pltpu.make_async_copy(o.at[i], outs[i], sem.at[2, i]).wait()

def split_add(bit, keep, recv, groups):
    n, W = keep.shape[0] // (2*groups), keep.shape[1]
    any_ = pl.BlockSpec(memory_space=pltpu.HBM)
    return pl.pallas_call(
        partial(split_kernel, groups),
        in_specs=[pl.BlockSpec(memory_space=pltpu.SMEM), any_, any_], out_specs=[any_]*(2*groups),
        out_shape=[jax.ShapeDtypeStruct((n,W),bf16)]*(2*groups),
        scratch_shapes=[pltpu.VMEM((2*groups,n,W),bf16)]*3+[pltpu.SemaphoreType.DMA((3,2*groups))],
        compiler_params=pltpu.CompilerParams(vmem_limit_bytes=24*1024*1024),
        name="split_add",
    )(bit, keep, recv)

D = 768
pool_eps = 1e-06


def matryoshka(averages):
    pieces = []
    for prefix in (D, D * 2 // 3, D // 3, D // 6, D // 12):
        leading = averages[..., :prefix]
        centred = leading - jnp.mean(leading, axis=-1, keepdims=True)
        pieces.append(
            centred * lax.rsqrt(jnp.mean(centred * centred, axis=-1, keepdims=True) + pool_eps)
        )
    return jnp.concatenate(pieces, axis=-1)


def part_of(value, index, count):
    rows = value.shape[0] // count
    return lax.dynamic_slice_in_dim(value, index * rows, rows, 0)


def ordered(bit, mine, theirs):
    first = lax.broadcasted_iota(jnp.int32, (2,) + (1,) * mine.ndim, 0) == bit
    return jnp.where(first, mine[None], theirs[None]).reshape((-1,) + mine.shape[1:])


def sum_of(arrays):
    total = arrays[0].astype(f32)
    for array in arrays[1:]:
        total = total + array.astype(f32)
    return total.astype(bf16)


fence = lax.optimization_barrier


class Links:
    def __init__(self, n_rows, n_blk):
        self.size = {"rows": n_rows, "blk": n_blk}
        self.at = {"rows": lax.axis_index("rows"), "blk": lax.axis_index("blk")}
        self.near = ("rows", 0, 0)
        self.near_bit = self.at["rows"] % 2
        far = list(range(1, n_rows.bit_length() - 1))
        self.far = [("rows", a, b) for a, b in zip(far, far[::-1])]
        self.plain_far = [("rows", a, a) for a in far]
        self.blk_bits = [("blk", k, k) for k in range(n_blk.bit_length() - 1)]

    def bit(self, stage, flip=False):
        axis, even, odd = stage
        at = self.at[axis]
        if even == odd:
            return (at >> even) % 2
        near = 1 - self.near_bit if flip else self.near_bit
        return jnp.where(near == 0, (at >> even) % 2, (at >> odd) % 2)

    def swap(self, value, stage):
        axis, even, odd = stage
        pairs = [(i, i ^ (1 << (odd if i % 2 and even != odd else even))) for i in range(self.size[axis])]
        return lax.ppermute(value, axis, pairs)

    def halve(self, addends, stages):
        for stage in stages:
            bit = self.bit(stage)
            send = sum_of([part_of(a, 1 - bit, 2) for a in addends])
            addends = [part_of(a, bit, 2) for a in addends] + [self.swap(send, stage)]
        return addends

    def double(self, value, stages):
        for stage in stages[::-1]:
            value = ordered(self.bit(stage), value, self.swap(value, stage))
        return value

    def last(self, value):
        return value, self.swap(value, self.far[0]), self.swap(value, self.near)

    def finish(self, group):
        return (*group, self.swap(group[1], self.near))


def local(
    n_rows,
    n_blk,
    tokens,
    segments,
    query_weight,
    query_bias,
    key_weight,
    value_weight,
    value_bias,
    out_weight,
    out_bias,
    first_gain,
    first_shift,
    up_weight,
    up_bias,
    down_weight,
    down_bias,
    second_gain,
    second_shift,
    cotangent,
):
    links = Links(n_rows, n_blk)
    pair, cross = links.blk_bits
    seq_at = links.at["blk"] // 2
    near_bit = links.near_bit
    num_seq, tok_rows, width = tokens.shape
    ff = up_weight.shape[1]
    chunks = ff // width
    total_rows = 2 * tok_rows

    own = lax.dynamic_index_in_dim(tokens, seq_at, 0, keepdims=False)
    other = lax.dynamic_index_in_dim(tokens, 1 - seq_at, 0, keepdims=False)
    piece = tok_rows // 2
    far_a = links.swap(other[:piece], cross)
    far_b = links.swap(other[piece:], cross)
    near_block = links.swap(own, pair)
    seg_pair = jnp.stack([segments, links.swap(segments, pair)])
    seg_cross = links.swap(seg_pair, cross)
    last_a = links.swap(far_a, pair)
    last_b = links.swap(far_b, pair)
    seg_mine = lax.dynamic_index_in_dim(seg_pair, seq_at, 1, keepdims=False)
    seg_far = lax.dynamic_index_in_dim(seg_cross, seq_at, 1, keepdims=False)
    seg_keys = jnp.concatenate([seg_mine[0], seg_far[0], seg_mine[1], seg_far[1]], 0)
    seg_query = seg_keys[:total_rows]
    blocks = [own, far_a, far_b, near_block, last_a, last_b]
    cot_other = lax.dynamic_index_in_dim(cotangent, 1 - seq_at, 0, keepdims=False)
    cot_own = lax.dynamic_index_in_dim(cotangent, seq_at, 0, keepdims=False)
    cot_other, cot_own, *blocks = fence((cot_other, cot_own, *blocks))
    cot_far = links.swap(cot_other, cross)

    queries, keys, values, attended, inv_totals = attn_fwd(
        blocks, query_weight, key_weight, value_weight, query_bias.reshape(-1, 128),
        value_bias.reshape(-1, 128), seg_keys[None, :], total_rows,
    )
    vectors = [
        v.reshape(-1, 128)
        for v in (out_bias, first_gain, first_shift, down_bias, second_gain, second_shift, up_bias)
    ]
    half = chunks // 2
    order = jnp.concatenate(
        [(1 - near_bit) * half + jnp.arange(half), near_bit * half + jnp.arange(half)]
    ).astype(jnp.int32)
    far_block = jnp.concatenate(blocks[1:3], 0)
    out_low, seg_sums, small, d_resid, d_numer, d_total, grad_out, ffn_send, ffn_keep = mid(
        order, attended, (own, far_block), (cot_own, cot_far), inv_totals, seg_query[None, :],
        vectors, out_weight, up_weight, down_weight,
    )
    seg_row = seg_keys[None, :]
    back_in = (queries, keys, values, d_numer, d_total)
    first, rest = links.far[:1], links.far[1:]
    first_bit = links.bit(first[0]).reshape(1).astype(jnp.int32)
    ffn_recv = links.swap(ffn_send, links.near)
    grads_a = attn_bwd(*back_in, seg_row, 0, 2)
    ffn_keep, ffn_recv, grads_a, back_in = fence((ffn_keep, ffn_recv, grads_a, back_in))

    send_one, keep_one, send_two, keep_two = split_add(first_bit, ffn_keep, ffn_recv, 2)
    send_one, back_in = fence((send_one, back_in))
    one = [keep_one, links.swap(send_one, first[0])]
    grads_b = attn_bwd(*back_in, seg_row, 2, width // 128 - 2)
    one, send_two, grads_a, grads_b = fence((one, send_two, grads_a, grads_b))

    one = [sum_of(links.halve(one, rest))]
    two = [keep_two, links.swap(send_two, first[0])]
    out_back = links.swap(out_low[tok_rows:], cross)
    grads = [g for pair_of in zip(grads_a, grads_b) for g in pair_of]
    d_mine, d_pair, bias_sums, attn_send, attn_keep = proj_bwd(
        near_bit.reshape(1), grads, blocks, query_weight, key_weight,
        value_weight, d_resid, grad_out,
    )
    one, two, out_back, d_mine, d_pair, bias_sums, attn_send, attn_keep = fence(
        (one, two, out_back, d_mine, d_pair, bias_sums, attn_send, attn_keep)
    )

    attn_recv = links.swap(attn_send, links.near)
    two = [sum_of(links.halve(two, rest))]
    one = links.halve(one, [pair])
    layer_output = ordered(seq_at, out_low[:tok_rows][None], out_back[None])
    seg_sums = seg_sums[:NSEG]
    seg_recv = links.swap(seg_sums, pair)
    small = jnp.concatenate([small[: UP_B + chunks], bias_sums], 0)
    one, two, attn_recv, attn_keep, small, seg_sums, seg_recv, layer_output = fence(
        (one, two, attn_recv, attn_keep, small, seg_sums, seg_recv, layer_output)
    )

    send_three, keep_three = split_add(first_bit, attn_keep, attn_recv, 1)
    three = [keep_three, links.swap(send_three, first[0])]
    one = [sum_of(links.halve(one, [cross]))]
    two = links.halve(two, [pair])
    labels = jnp.arange(1, NSEG + 1, dtype=jnp.int32)
    counts = jnp.sum((seg_keys[None, :] == labels[:, None]).astype(f32), axis=1)
    pooled_one = (seg_sums + seg_recv) / counts[:, None]
    pooled_two = links.swap(pooled_one, cross)
    small = small + links.swap(small, pair)
    one, two, three, small, pooled_one, pooled_two = fence((one, two, three, small, pooled_one, pooled_two))

    three = [sum_of(links.halve(three, rest))]
    one = links.double(one[0], [cross])
    two = [sum_of(links.halve(two, [cross]))]
    small = small + links.swap(small, cross)
    pooled = matryoshka(ordered(seq_at, pooled_one[None], pooled_two[None]))
    one, two, three, small, pooled = fence((one, two, three, small, pooled))

    one = links.double(one, [pair])
    two = links.double(two[0], [cross])
    three = links.halve(three, [pair])
    small = small + links.swap(small, links.near)
    one, two, three, small = fence((one, two, three, small))

    one = links.double(one, rest)
    two = links.double(two, [pair])
    three = [sum_of(links.halve(three, [cross]))]
    for stage in links.plain_far:
        small = small + links.swap(small, stage)
    one, two, three, small, d_pair = fence((one, two, three, small, d_pair))

    one = links.last(one)
    two = links.double(two, rest)
    three = links.double(three[0], [cross])
    d_pair = links.swap(d_pair, pair)
    one, two, three, d_pair, d_mine = fence((one, two, three, d_pair, d_mine))

    two = links.last(two)
    three = links.double(three, [pair])
    one = links.finish(one)
    d_mine = (d_mine + d_pair.astype(f32)).astype(bf16)
    one, two, three, d_mine = fence((one, two, three, d_mine))

    place = jnp.stack([near_bit, links.bit(first[0]), links.bit(first[0], True)]).astype(jnp.int32)
    three = links.double(three, rest)
    two = links.finish(two)
    d_back = links.swap(d_mine[tok_rows:], cross)
    ffn_sums = emit(place, one, ((ff, width), (width, ff)), 0)
    two, three, d_mine, ffn_sums = fence((two, three, d_mine, ffn_sums))

    three = links.last(three)
    down_sum, up_sum = emit(place, two, ((ff, width), (width, ff)), 1, ffn_sums)
    three, d_mine, d_back, down_sum, up_sum = fence((three, d_mine, d_back, down_sum, up_sum))

    three = links.finish(three)
    grad_tokens = ordered(seq_at, d_mine[:tok_rows][None], d_back[None])
    query_sum, key_sum, value_sum, out_sum = emit(place, three, ((width, width),) * 4)
    return (
        layer_output,
        pooled,
        grad_tokens,
        query_sum,
        small[UP_B + chunks],
        key_sum,
        value_sum,
        small[UP_B + chunks + 1],
        out_sum,
        small[OUT_B],
        small[G1],
        small[B1],
        up_sum,
        small[UP_B : UP_B + chunks].reshape(-1),
        down_sum,
        small[DOWN_B],
        small[G2],
        small[B2],
    )


def solution(mesh):
    row_split = P("rows", "blk", None)
    return jax.shard_map(
        partial(local, mesh.shape["rows"], mesh.shape["blk"]),
        mesh=mesh,
        in_specs=(row_split, P("rows", "blk")) + (P(),) * 15 + (row_split,),
        out_specs=(row_split, P("rows", None, None), row_split) + (P(),) * 15,
        check_vma=False,
    )
```

```python
from functools import partial

import jax
import jax.numpy as jnp
from jax import lax
from jax.experimental import pallas as pl
from jax.experimental.pallas import tpu as pltpu
from jax.sharding import PartitionSpec as P

f32=jnp.float32; bf16=jnp.bfloat16
norm_eps=1e-12
NSEG=6
HD=64
def dot(a,b): return jnp.dot(a,b,preferred_element_type=f32)
def dot_nt(a,b): return lax.dot_general(a,b,(((1,),(1,)),((),())),preferred_element_type=f32)
def dot_tn(a,b): return lax.dot_general(a,b,(((0,),(0,)),((),())),preferred_element_type=f32)

def gelu_pair(x):
    t = 1.0 / (1.0 + (0.3275911 * 0.7071067811865476) * jnp.abs(x))
    e = jnp.exp(-0.5 * x * x)
    half = (0.5*0.254829592) + t*((0.5*-0.284496736) + t*((0.5*1.421413741) + t*((0.5*-1.453152027) + t*(0.5*1.061405429))))
    tail = half * t * e
    cdf = jnp.where(x > 0, 1.0 - tail, tail)
    return x * cdf, cdf + x * e * 0.3989422804014327

def in_hbm(*arrays):
    return tuple(pltpu.with_memory_space_constraint(a, pltpu.HBM) for a in arrays)

def wide(rows):
    return jnp.concatenate([rows[i:i+1,:] for i in range(rows.shape[0])], axis=1)

VM = pl.BlockSpec(memory_space=pltpu.VMEM)
SM = pl.BlockSpec(memory_space=pltpu.SMEM)
ANY = pl.BlockSpec(memory_space=pl.ANY)
FAR = pl.BlockSpec(memory_space=pltpu.HBM)
MIB = 1024 * 1024


def call(kernel, deps, args, in_specs, out_specs, out_shape, scratch=(), aliases=None, vmem=16, grid=(), name=None):
    n, m = len(deps), len(args)

    def body(*refs):
        kernel(*refs[n : n + m], *refs[n + m + 1 :])

    token, *outs = pl.pallas_call(
        body,
        grid=grid,
        in_specs=[ANY] * n + list(in_specs),
        out_specs=[FAR] + list(out_specs),
        out_shape=[pltpu.HBM((8, 128), f32)] + list(out_shape),
        scratch_shapes=list(scratch),
        input_output_aliases={n + k: 1 + v for k, v in (aliases or {}).items()},
        compiler_params=pltpu.CompilerParams(vmem_limit_bytes=int(vmem * MIB)),
        name=name,
    )(*deps, *args)
    return in_hbm(token)[0], outs


def same_segment(left, right):
    lab = lax.broadcasted_iota(jnp.int32, (8, 1), 0).astype(f32)
    hot = lambda s: (lab == s).astype(f32).astype(bf16)
    return (dot_tn(hot(left), hot(right)) - 1.0) * 1e30

OUT_B, G1, B1, DOWN_B, G2, B2, UP_B = range(7)
RB = 128

def rows_norm(r):
    m = jnp.mean(r, axis=-1, keepdims=True)
    c = r - m
    inv = lax.rsqrt(jnp.mean(c*c, axis=-1, keepdims=True) + norm_eps)
    return c * inv, inv

def norm_back(g, xh, inv):
    return inv * (g - jnp.mean(g, axis=-1, keepdims=True) - xh * jnp.mean(g*xh, axis=-1, keepdims=True))

def col_sum(v): return jnp.sum(v, axis=0, keepdims=True)

def mid_kernel(order_ref, att_ref, xa_ref, xb_ref, xc_ref, cota_hbm, cotb_hbm, itot_hbm, seg_ref, ob_ref, g1_ref, b1_ref, db_ref, g2_ref, b2_ref, ub_ref, wo_hbm, wu_hbm, wd_hbm,
               segsum_ref, small_ref, dres_ref, dn_ref, dt_ref, outo_hbm, outx_hbm, gout_hbm, send_one, send_two, keep_one, keep_two,
               wo, wu, wd, hid, hl, xh1, rs1, act, gp, feed, dfl, dhid, stage, cota_ref, cotb_ref, itot_ref, out_ref, gout_ref,
               wsem, gsem, csem):
    R, W = att_ref.shape
    nc = wu.shape[0]
    def rows_of(refs, i):
        for ref in refs:
            h = ref.shape[0] // RB
            if i < h:
                return ref[pl.ds(i*RB,RB),:]
            i -= h
    def copies(k):
        c = order_ref[k]
        return (pltpu.make_async_copy(wu_hbm.at[:, pl.ds(c*W, W)], wu.at[k], wsem.at[1+k]),
                pltpu.make_async_copy(wd_hbm.at[pl.ds(c*W, W), :], wd.at[k], wsem.at[1+nc+k]))
    cwo = pltpu.make_async_copy(wo_hbm, wo, wsem.at[0]); cwo.start()
    for k in range(nc):
        for cp in copies(k): cp.start()
    late = [pltpu.make_async_copy(src, dst, csem.at[i]) for i, (src, dst) in enumerate(
        ((cota_hbm, cota_ref), (cotb_hbm, cotb_ref), (itot_hbm, itot_ref), (out_ref.at[pl.ds(0, R//2), :], outo_hbm), (gout_ref, gout_hbm),
         (out_ref.at[pl.ds(R//2, R//2), :], outx_hbm)))]
    for c in late[:3]: c.start()
    NB = R // RB
    vecs = (ob_ref, g1_ref, b1_ref, db_ref, g2_ref, b2_ref)
    row = lambda i: wide(vecs[i][...])
    lanes = W // 128
    cwo.wait()
    feed[...] = dot(att_ref[...].astype(bf16), wo[...])
    for i in range(NB):
        s = pl.ds(i*RB, RB)
        r = rows_of((xa_ref, xb_ref, xc_ref), i).astype(f32) + feed[s, :] + row(OUT_B)
        xh, inv = rows_norm(r)
        xh1[s,:] = xh
        rs1[s,:] = inv
        h = xh * row(G1) + row(B1)
        hid[s,:] = h
        hl[s,:] = h.astype(bf16)
    for k in range(nc):
        for cp in copies(k): cp.wait()
        ub = wide(ub_ref[pl.ds(order_ref[k]*lanes, lanes), :])
        for j in range(W//256):
            cs = slice(j*256, (j+1)*256)
            pre = dot(hl[...], wu[k, :, cs]) + ub[:, cs]
            a_, g_ = gelu_pair(pre)
            act[k, :, cs] = a_.astype(bf16)
            gp[k, :, cs] = g_.astype(gp.dtype)
        part = dot(act[k], wd[k])
        if k == 0: feed[...] = part
        else: feed[...] += part
    late[0].wait()
    late[1].wait()
    lab = (lax.broadcasted_iota(jnp.int32, (8, 1), 0) + 1).astype(f32)
    count = jnp.zeros((8, 1), f32)
    zero = jnp.zeros((1,W),f32)
    segsum = jnp.zeros((8, W), f32)
    sg = ss = sdb = zero
    for i in range(NB):
        s = pl.ds(i*RB, RB)
        xh, inv = rows_norm(hid[s,:] + feed[s,:] + row(DOWN_B))
        o = xh * row(G2) + row(B2)
        oh = o.astype(bf16)
        out_ref[s,:] = oh
        ol = (o - oh.astype(f32)).astype(bf16)
        hot = (lab == seg_ref[0:1, i*RB:(i+1)*RB]).astype(f32)
        count = count + jnp.sum(hot, axis=1, keepdims=True)
        hot = hot.astype(bf16)
        segsum = segsum + dot(hot, oh) + dot(hot, ol)
        u = rows_of((cota_ref, cotb_ref), i).astype(f32)
        sg = sg + col_sum(u*xh)
        ss = ss + col_sum(u)
        d = norm_back(u * row(G2), xh, inv)
        dhid[s,:] = d
        dl = d.astype(bf16)
        dfl[s,:] = dl
        sdb = sdb + col_sum(dl.astype(f32))
    late[3].start()
    late[5].start()
    segsum_ref[0:8, :] = segsum
    segsum_ref[8:16, :] = jnp.broadcast_to(count, (8, W))
    small_ref[pl.ds(DOWN_B,1), :] = sdb
    small_ref[pl.ds(G2,1), :] = sg
    small_ref[pl.ds(B2,1), :] = ss
    def push(slot, k, kind):
        dst = (send_one, send_two, keep_one, keep_two)[k]
        return pltpu.make_async_copy(stage.at[slot], dst.at[pl.ds(kind*W, W), :], gsem.at[slot])
    for k in range(nc):
        stage[k] = dot_tn(act[k], dfl[...]).astype(bf16)
        push(k, k, 0).start()
        da = dot_nt(dfl[...], wd[k])
        dp = (da * gp[k].astype(f32)).astype(bf16)
        act[k] = dp
        small_ref[pl.ds(UP_B + order_ref[k],1), :] = col_sum(dp.astype(f32))
        stage[nc+k] = dot_tn(hl[...], dp).astype(bf16)
        push(nc+k, k, 1).start()
        dhid[...] += dot_nt(dp, wu[k])
    sg = ss = sdb = zero
    for i in range(NB):
        s = pl.ds(i*RB, RB)
        dh = dhid[s,:]
        xh = xh1[s,:]
        sg = sg + col_sum(dh*xh)
        ss = ss + col_sum(dh)
        d = norm_back(dh * row(G1), xh, rs1[s,:])
        dres_ref[s,:] = d
        dl = d.astype(bf16)
        dfl[s,:] = dl
        sdb = sdb + col_sum(dl.astype(f32))
    small_ref[pl.ds(OUT_B,1), :] = sdb
    small_ref[pl.ds(G1,1), :] = sg
    small_ref[pl.ds(B1,1), :] = ss
    gout_ref[...] = dot_tn(att_ref[...].astype(bf16), dfl[...]).astype(bf16)
    late[4].start()
    late[2].wait()
    l0 = lax.broadcasted_iota(jnp.int32, (128,128), 0) // HD
    l1 = lax.broadcasted_iota(jnp.int32, (128,128), 1) // HD
    same = (l0 == l1).astype(f32).astype(bf16)
    feed[...] = dot_nt(dfl[...], wo[...])
    for i in range(NB):
        s = pl.ds(i*RB, RB)
        da = feed[s,:]
        it = itot_ref[s,:]
        dn_ref[s,:] = (da * it).astype(bf16)
        p = da * att_ref[s,:]
        ph = p.astype(bf16)
        plow = (p - ph.astype(f32)).astype(bf16)
        for j in range(W//128):
            cs = slice(j*128,(j+1)*128)
            dt_ref[s, cs] = -(dot(ph[:,cs], same) + dot(plow[:,cs], same)) * it[:,cs]
    for c in late[3:]: c.wait()
    for k in range(nc):
        push(k, k, 0).wait()
        push(nc+k, k, 1).wait()

def mid(order, att, x, cot, itot, seg_row, vecs, wo, wu, wd):
    R, W = att.shape
    nc = wu.shape[1] // W
    any_ = pl.BlockSpec(memory_space=pltpu.HBM)
    vm = pl.BlockSpec(memory_space=pltpu.VMEM)
    sm = pl.BlockSpec(memory_space=pltpu.SMEM)
    sd = pltpu.HBM
    return pl.pallas_call(
        mid_kernel,
        in_specs=[sm]+[vm]*4+[any_]*3+[vm]*8+[any_]*3,
        out_specs=[vm]*5+[any_]*7,
        out_shape=[sd((16,W),f32), sd((UP_B+nc+6,W),f32), sd((R,W),f32), sd((R,W),bf16), sd((R,W),f32), sd((R//2,W),bf16), sd((R//2,W),bf16),
                   sd((W,W),bf16)]+[sd((2*W,W),bf16)]*4,
        scratch_shapes=[pltpu.VMEM((W,W),bf16), pltpu.VMEM((nc,W,W),bf16), pltpu.VMEM((nc,W,W),bf16),
                        pltpu.VMEM((R,W),f32), pltpu.VMEM((R,W),bf16), pltpu.VMEM((R,W),f32), pltpu.VMEM((R,1),f32),
                        pltpu.VMEM((nc,R,W),bf16), pltpu.VMEM((nc,R,W),f32), pltpu.VMEM((R,W),f32), pltpu.VMEM((R,W),bf16), pltpu.VMEM((R,W),f32),
                        pltpu.VMEM((2*nc,W,W),bf16), pltpu.VMEM((R//2,W),bf16), pltpu.VMEM((R//2,W),bf16), pltpu.VMEM((R,W),f32),
                        pltpu.VMEM((R,W),bf16), pltpu.VMEM((W,W),bf16),
                        pltpu.SemaphoreType.DMA((1+2*nc,)), pltpu.SemaphoreType.DMA((2*nc,)), pltpu.SemaphoreType.DMA((6,))],
        compiler_params=pltpu.CompilerParams(vmem_limit_bytes=60*1024*1024),
        name="mid",
    )(order, *in_hbm(att, *x, *cot, itot, seg_row, *vecs, wo, wu, wd))

GW = 256
ID_ROWS = 16
def head_pair_lanes():
    return lax.broadcasted_iota(jnp.int32, (1,128), 1) < HD

def gather_rows(refs, dst, sem):
    at, copies = 0, []
    for i, ref in enumerate(refs):
        n = ref.shape[0] // 128 * 128
        copies.append(pltpu.make_async_copy(ref.at[pl.ds(0, n), :], dst.at[pl.ds(at, n), :], sem.at[i]))
        at += n
    return copies

def gather_ids(refs, dst, sem):
    tails = [ref for ref in refs if ref.shape[0] % 128]
    return [
        pltpu.make_async_copy(ref.at[pl.ds(ref.shape[0] - ID_ROWS, ID_ROWS), :], dst.at[i], sem.at[i])
        for i, ref in enumerate(tails)
    ]

def ids_of(ids, width):
    return jnp.concatenate([ids[i, 0:1, 0:width].astype(f32) for i in range(ids.shape[0])], axis=1)

def attend(q, k, v, bias, first):
    nums, tots = [], []
    for p in range(q.shape[1]//128):
        cs = slice(p*128,(p+1)*128)
        qp, kp, vp = q[:,cs], k[:,cs], v[:,cs]
        one = jnp.ones_like(vp); zero=jnp.zeros_like(qp)
        res = []
        for h in range(2):
            mine = first if h==0 else jnp.logical_not(first)
            s = dot_nt(jnp.where(mine, qp, zero), kp)
            e = jnp.exp(s + bias[...]).astype(bf16)
            res.append(dot(e, jnp.where(mine, vp, one)))
        nums.append(jnp.where(first, res[0], res[1]))
        tots.append(jnp.where(first, res[1], res[0]))
    return nums, tots

def attn_some_kernel(n_parts, *refs):
    parts = refs[:n_parts]
    (wq_ref, wk_ref, wv_ref, qb_ref, vb_ref,
     q_ref, k_ref, v_ref, num_ref, tot_ref, bias, x_ref, ids, sem, isem) = refs[n_parts:]
    R, N = q_ref.shape[0], k_ref.shape[0]
    @pl.when(pl.program_id(0) == 0)
    def _():
        marks = gather_ids(parts, ids, isem)
        copies = gather_rows(parts, x_ref, sem)
        for c in marks + copies: c.start()
        for c in marks: c.wait()
        row = ids_of(ids, N // ids.shape[0])
        bias[...] = same_segment(row[:, 0:R], row)
        for c in copies: c.wait()
    lanes = GW // 128
    at = pl.ds(pl.program_id(0)*lanes, lanes)
    qb, vb = wide(qb_ref[at, :]), wide(vb_ref[at, :])
    q = (0.125*(dot(x_ref[0:R,:], wq_ref[...]) + qb)).astype(bf16)
    k = dot(x_ref[...], wk_ref[...]).astype(bf16)
    v = (dot(x_ref[...], wv_ref[...]) + vb).astype(bf16)
    q_ref[...] = q; k_ref[...] = k; v_ref[...] = v
    nums, tots = attend(q, k, v, bias, head_pair_lanes())
    for p in range(lanes):
        num_ref[:, p*128:(p+1)*128] = nums[p]
        tot_ref[:, p*128:(p+1)*128] = tots[p]

def attn_some(parts, wq, wk, wv, qb, vb, R):
    W = wq.shape[0]
    N = sum(p.shape[0] // 128 * 128 for p in parts)
    n_ids = sum(1 for p in parts if p.shape[0] % 128)
    whole = N // n_ids * (n_ids + 1)
    sd = pltpu.HBM
    full = lambda a: pl.BlockSpec(a.shape, lambda j: (0,0))
    col = lambda r: pl.BlockSpec((r,GW), lambda j: (0,j))
    return pl.pallas_call(
        partial(attn_some_kernel, len(parts)), grid=(W//GW,),
        in_specs=[pl.BlockSpec(memory_space=pltpu.HBM)]*len(parts)+[col(W), col(W), col(W), full(qb), full(vb)],
        out_specs=[col(R), col(N), col(N), col(R), col(R)],
        out_shape=[sd((R,W),bf16), sd((whole,W),bf16), sd((whole,W),bf16), sd((R,W),f32), sd((R,W),f32)],
        scratch_shapes=[pltpu.VMEM((R,N),f32), pltpu.VMEM((N,W),bf16), pltpu.VMEM((n_ids,ID_ROWS,W),bf16),
                        pltpu.SemaphoreType.DMA((len(parts),)), pltpu.SemaphoreType.DMA((n_ids,))],
        compiler_params=pltpu.CompilerParams(vmem_limit_bytes=24*1024*1024, dimension_semantics=("arbitrary",)),
        name="attn_some",
    )(*in_hbm(*parts, wq, wk, wv, qb, vb))

def attn_last_kernel(n_parts, n_all, *refs):
    parts = refs[n_all-n_parts:n_all]
    (q_ref, wk_ref, wv_ref, vb_ref, num_ref, tot_ref, _, _,
     k_ref, v_ref, att_ref, itot_ref, sk_ref, bias, x_ref, ids, sem, isem) = refs[n_all:]
    R, N = q_ref.shape[0], k_ref.shape[0]
    whole = sk_ref.shape[1]
    @pl.when(pl.program_id(0) == 0)
    def _():
        marks = gather_ids(refs[:n_all], ids, isem)
        copies = gather_rows(parts, x_ref, sem)
        for c in marks + copies: c.start()
        for c in marks: c.wait()
        row = ids_of(ids, N)
        sk_ref[...] = jnp.broadcast_to(row, sk_ref.shape)
        bias[...] = same_segment(row[:, 0:R], row[:, whole-N:whole])
        for c in copies: c.wait()
    lanes = GW // 128
    vb = wide(vb_ref[pl.ds(pl.program_id(0)*lanes, lanes), :])
    k = dot(x_ref[...], wk_ref[...]).astype(bf16)
    v = (dot(x_ref[...], wv_ref[...]) + vb).astype(bf16)
    k_ref[...] = k; v_ref[...] = v
    nums, tots = attend(q_ref[...], k, v, bias, head_pair_lanes())
    for p in range(lanes):
        cs = slice(p*128, (p+1)*128)
        it = 1.0 / pltpu.roll(tots[p] + tot_ref[:, cs], HD, 1)
        att_ref[:,cs] = (nums[p] + num_ref[:, cs]) * it
        itot_ref[:,cs] = it

def attn_last(here, parts, q, wk, wv, vb, num, tot, k, v):
    R, W = q.shape
    N = sum(p.shape[0] // 128 * 128 for p in parts)
    whole = k.shape[0]
    sd = pltpu.HBM
    every = [*here, *parts]
    n = len(every)
    n_ids = sum(1 for p in every if p.shape[0] % 128)
    any_ = pl.BlockSpec(memory_space=pltpu.HBM)
    full = lambda a: pl.BlockSpec(a.shape, lambda j: (0,0))
    col = lambda r: pl.BlockSpec((r,GW), lambda j: (0,j))
    tail = pl.BlockSpec((N,GW), lambda j: (whole//N-1,j))
    return pl.pallas_call(
        partial(attn_last_kernel, len(parts), n), grid=(W//GW,),
        in_specs=[any_]*n+[col(R), col(W), col(W), full(vb), col(R), col(R), any_, any_],
        out_specs=[tail, tail, col(R), col(R), pl.BlockSpec((8,whole), lambda j: (0,0))],
        out_shape=[sd((whole,W),bf16), sd((whole,W),bf16), sd((R,W),f32), sd((R,W),f32), sd((8,whole),f32)],
        input_output_aliases={n+6: 0, n+7: 1},
        scratch_shapes=[pltpu.VMEM((R,N),f32), pltpu.VMEM((N,W),bf16), pltpu.VMEM((n_ids,ID_ROWS,W),bf16),
                        pltpu.SemaphoreType.DMA((n,)), pltpu.SemaphoreType.DMA((n_ids,))],
        compiler_params=pltpu.CompilerParams(vmem_limit_bytes=20*1024*1024, dimension_semantics=("arbitrary",)),
        name="attn_last",
    )(*in_hbm(*every, q, wk, wv, vb, num, tot), k, v)

def attn_bwd_kernel(q_ref, k_ref, v_ref, dn_ref, dt_ref, sk_ref, dq_ref, dk_ref, dv_ref, bias):
    @pl.when(pl.program_id(0) == 0)
    def _():
        row = sk_ref[0:1, :]
        bias[...] = same_segment(row, row[:, 0:q_ref.shape[0]])
    first = head_pair_lanes()
    lane = lax.broadcasted_iota(jnp.int32, (1,128), 1)
    for p in range(q_ref.shape[1]//128):
        cs = slice(p*128,(p+1)*128)
        qp, kp, vp, dnp = q_ref[:,cs], k_ref[:,cs], v_ref[:,cs], dn_ref[:,cs]
        dtr = pltpu.roll(dt_ref[:,cs], HD, 1)
        hi = dtr.astype(bf16)
        rest = dtr - hi.astype(f32)
        mid_ = rest.astype(bf16)
        low = (rest - mid_.astype(f32)).astype(bf16)
        res=[]
        for h in range(2):
            mine = first if h==0 else jnp.logical_not(first)
            o = HD if h==0 else 0
            ex = jnp.where(lane==o, hi, jnp.where(lane==o+1, mid_, jnp.where(lane==o+2, low, jnp.zeros_like(hi))))
            dne = jnp.where(mine, dnp, ex)
            ve = jnp.where(mine, vp, jnp.where((lane>=o)&(lane<o+3), jnp.ones_like(vp), jnp.zeros_like(vp)))
            s = dot_nt(jnp.where(mine, kp, jnp.zeros_like(kp)), qp)
            e = jnp.exp(s + bias[...])
            pr = dot_nt(ve, dne)
            ds = (e * pr).astype(bf16)
            dv = dot(e.astype(bf16), dnp)
            dk = dot(ds, qp)
            dq = dot_tn(ds, kp)
            res.append((dq,dk,dv))
        dq_ref[:,cs] = (jnp.where(first, res[0][0], res[1][0]).astype(bf16).astype(f32)*0.125).astype(bf16)
        dk_ref[:,cs] = jnp.where(first, res[0][1], res[1][1]).astype(bf16)
        dv_ref[:,cs] = jnp.where(first, res[0][2], res[1][2]).astype(bf16)

def attn_bwd(deps,q,k,v,dn,dt,sk,start,count):
    R,W=q.shape; N=k.shape[0]
    sd = pltpu.HBM
    GB=128
    col = lambda r: pl.BlockSpec((r,GB), lambda j: (0,j+start))
    out = lambda r: pl.BlockSpec((r,GB), lambda j: (0,j))
    return call(
        attn_bwd_kernel, deps, in_hbm(q,k,v,dn,dt,sk),
        [col(R), col(N), col(N), col(R), col(R), pl.BlockSpec(sk.shape, lambda j: (0,0))],
        [out(R), out(N), out(N)],
        [sd((R,GB*count),bf16), sd((N,GB*count),bf16), sd((N,GB*count),bf16)],
        [pltpu.VMEM((N,R),f32)], grid=(count,), vmem=16, name="attn_bwd",
    )

def spans(refs):
    at, out = 0, []
    for r in refs:
        out.append(slice(at, at + r.shape[1]))
        at += r.shape[1]
    return out

def token_grad_kernel(n_grads, *refs):
    grads, (wq_ref, wk_ref, wv_ref, dres_ref, own_ref, away_ref, pa_ref, pb_ref) = refs[:n_grads], refs[n_grads:]
    dq, dk, dv = grads[0::3], grads[1::3], grads[2::3]
    R = dq[0].shape[0]
    parts = spans(dq)
    def back(refs, w_ref, rows):
        total = dot_nt(refs[0][rows,:], w_ref[:,parts[0]])
        for r, cs in zip(refs[1:], parts[1:]): total = total + dot_nt(r[rows,:], w_ref[:,cs])
        return total
    top, rest = slice(0,R), slice(R,2*R)
    pair = (back(dk, wk_ref, rest) + back(dv, wv_ref, rest)).astype(bf16)
    pa_ref[...] = pair[:R//2]
    pb_ref[...] = pair[R//2:]
    mine = (dres_ref[...] + back(dq, wq_ref, top) + back(dk, wk_ref, top)
            + back(dv, wv_ref, top))
    own_ref[...] = mine[:R//2]
    away_ref[...] = mine[R//2:]

def token_grad(deps, grads, wq, wk, wv, dres):
    R, W = dres.shape
    sd = pltpu.HBM
    return call(
        partial(token_grad_kernel, len(grads)), deps, in_hbm(*grads, wq, wk, wv, dres),
        [VM]*(len(grads)+4), [VM]*4, [sd((R//2,W),f32)]*2+[sd((R//2,W),bf16)]*2, vmem=24, name="token_grad",
    )

def weight_grad_kernel(n_parts, n_grads, *refs):
    tokens, grads = refs[:n_parts], refs[n_parts:n_parts+n_grads]
    dq, dk, dv = grads[0::3], grads[1::3], grads[2::3]
    (bit_ref, gout_ref, bsum_ref, gsend_hbm, gkeep_hbm, stage, x_ref, sem, xsem) = refs[n_parts+n_grads:]
    copies = gather_rows(tokens, x_ref, xsem)
    for c in copies: c.start()
    W = x_ref.shape[1]
    bit = bit_ref[0]
    parts = spans(dq)
    def push(i, start):
        src = gout_ref if i == 3 else stage.at[i]
        def go(dst):
            cp = pltpu.make_async_copy(src, dst.at[pl.ds((i%2)*W, W), :], sem.at[i])
            cp.start() if start else cp.wait()
        @pl.when(bit == i//2)
        def _(): go(gkeep_hbm)
        @pl.when(bit != i//2)
        def _(): go(gsend_hbm)
    push(3, True)
    for c in copies: c.wait()
    for i, refs in ((2,dv), (1,dk), (0,dq)):
        for ref, cs in zip(refs, parts):
            n = ref.shape[0]
            stage[i, :, cs] = dot_tn(x_ref[0:n,:], ref[...]).astype(bf16)
        push(i, True)
    for ref, cs in zip(dq, parts): bsum_ref[0:1,cs] = col_sum(ref[...].astype(f32))
    for ref, cs in zip(dv, parts): bsum_ref[1:2,cs] = col_sum(ref[...].astype(f32))
    for i in range(4): push(i, False)

def weight_grad(deps, bits, grads, tokens, gout):
    R = grads[0].shape[0]
    W = gout.shape[0]
    sd = pltpu.HBM
    return call(
        partial(weight_grad_kernel, len(tokens), len(grads)), deps, (*in_hbm(*tokens, *grads), bits, *in_hbm(gout)),
        [FAR]*len(tokens)+[VM]*len(grads)+[SM, VM], [VM,FAR,FAR],
        [sd((2,W),f32), sd((2*W,W),bf16), sd((2*W,W),bf16)],
        [pltpu.VMEM((3,W,W),bf16), pltpu.VMEM((2*R,W),bf16), pltpu.SemaphoreType.DMA((4,)), pltpu.SemaphoreType.DMA((len(tokens),))],
        vmem=22, name="weight_grad",
    )

def emit_kernel(up_from, n_prev, second, bits_ref, *refs):
    n_in = len(second) * 2
    pieces_in, outs, (stage, sem) = refs[:n_in], refs[n_in+n_prev:-2], refs[-2:]
    n, W = pieces_in[0].shape
    bit, mine, theirs = bits_ref[0], bits_ref[1], bits_ref[2]
    pieces = []
    for i, s in enumerate(second):
        pieces.append((bit, 1 - mine if s else mine, pieces_in[2*i]))
        pieces.append((1 - bit, 1 - theirs if s else theirs, pieces_in[2*i+1]))
    def send(i, start):
        half, block, ref = pieces[i]
        for b in range(2):
            for h in range(2):
                if up_from is None: dst = outs[2*h + b]
                elif b == 0: dst = outs[0].at[pl.ds((2*h + up_from)*W, W), :]
                else: dst = outs[1].at[:, pl.ds((2*h + up_from)*W, W)]
                @pl.when((half == h) & (block == b))
                def _():
                    cp = pltpu.make_async_copy(stage.at[i], dst, sem.at[i])
                    cp.start() if start else cp.wait()
    for i, (half, block, ref) in enumerate(pieces):
        stage[i] = ref[...].astype(f32)
        send(i, True)
    for i in range(len(pieces)): send(i, False)

def emit(deps, bits, pieces, second, out_shape, up_from=None, prev=()):
    n, W = pieces[0].shape
    m = len(pieces)
    return call(
        partial(emit_kernel, up_from, len(prev), second), deps, (bits, *pieces, *prev),
        [SM]+[VM]*m+[FAR]*len(prev), [FAR]*len(out_shape), [pltpu.HBM(s, f32) for s in out_shape],
        [pltpu.VMEM((m,n,W),f32), pltpu.SemaphoreType.DMA((m,))],
        {1+m+i: i for i in range(len(prev))}, vmem=18, name="emit",
    )

def split_kernel(index, bits_ref, keep_hbm, recv_hbm, *refs):
    outs, (a, b, o, sem) = refs[:2], refs[2:]
    n, W = outs[0].shape
    bit = bits_ref[index]
    def load(i):
        src = pl.ds((bit if i else 1 - bit)*n, n)
        return (pltpu.make_async_copy(keep_hbm.at[src, :], a.at[i], sem.at[0, i]),
                pltpu.make_async_copy(recv_hbm.at[src, :], b.at[i], sem.at[1, i]))
    for i in range(2):
        for c in load(i): c.start()
    for i in range(2):
        for c in load(i): c.wait()
        o[i] = (a[i].astype(f32) + b[i].astype(f32)).astype(bf16)
        pltpu.make_async_copy(o.at[i], outs[i], sem.at[2, i]).start()
    for i in range(2): pltpu.make_async_copy(o.at[i], outs[i], sem.at[2, i]).wait()

def split_add(deps, bits, index, keep, recv):
    n, W = keep.shape[0] // 2, keep.shape[1]
    if n % 16:
        keep, recv, deps = lax.optimization_barrier((keep, recv, tuple(deps)))
        bit = bits[index]
        halves = [[lax.dynamic_slice_in_dim(a, b * n, n, 0).astype(f32) for a in (keep, recv)] for b in (1 - bit, bit)]
        return deps[0], [(a + b).astype(bf16) for a, b in halves]
    return call(
        partial(split_kernel, index), deps, (bits, *in_hbm(keep), recv), [SM, FAR, ANY], [FAR]*2,
        [pltpu.HBM((n,W),bf16)]*2, [pltpu.VMEM((2,n,W),bf16)]*3+[pltpu.SemaphoreType.DMA((3,2))],
        vmem=14*n*W/MIB+1, name="split_add",
    )

def join_kernel(index, bits_ref, mine_hbm, recv_hbm, out_hbm, both, sem):
    n = mine_hbm.shape[0]
    bit = bits_ref[index]
    loads = [pltpu.make_async_copy(src, both.at[pl.ds(at*n, n), :], sem.at[i])
             for i, (src, at) in enumerate(((mine_hbm, bit), (recv_hbm, 1 - bit)))]
    for c in loads: c.start()
    for c in loads: c.wait()
    out = pltpu.make_async_copy(both, out_hbm, sem.at[2])
    out.start()
    out.wait()

def join(deps, bits, index, mine, recv):
    n, W = mine.shape
    if n % 16:
        mine, recv, deps = lax.optimization_barrier((mine, recv, tuple(deps)))
        return deps[0], [jnp.where(bits[index] == 0, jnp.concatenate([mine, recv], 0), jnp.concatenate([recv, mine], 0))]
    return call(
        partial(join_kernel, index), deps, (bits, mine, recv), [SM, ANY, ANY], [ANY],
        [jax.ShapeDtypeStruct((2*n,W),bf16)], [pltpu.VMEM((2*n,W),bf16), pltpu.SemaphoreType.DMA((3,))],
        vmem=8*n*W/MIB+1, name="join",
    )

def add_kernel(a_ref, b_ref, o_ref):
    o_ref[...] = (a_ref[...].astype(f32) + b_ref[...].astype(f32)).astype(o_ref.dtype)

def add_to(deps, a, b, dtype):
    return call(add_kernel, deps, (a, b), [VM, VM], [VM], [jax.ShapeDtypeStruct(a.shape, dtype)], vmem=8, name="add")

def stack_kernel(*refs):
    out, at = refs[-1], 0
    for r in refs[:-1]:
        out[at:at+r.shape[0], :] = r[...]
        at += r.shape[0]

def stack_rows(deps, arrays):
    rows = sum(a.shape[0] for a in arrays)
    return call(stack_kernel, deps, arrays, [VM]*len(arrays), [VM],
                [jax.ShapeDtypeStruct((rows, arrays[0].shape[1]), f32)], vmem=4, name="stack_rows")

D = 768
pool_eps = 1e-06


def matryoshka(averages):
    pieces = []
    for prefix in (D, D * 2 // 3, D // 3, D // 6, D // 12):
        leading = averages[..., :prefix]
        centred = leading - jnp.mean(leading, axis=-1, keepdims=True)
        pieces.append(
            centred * lax.rsqrt(jnp.mean(centred * centred, axis=-1, keepdims=True) + pool_eps)
        )
    return jnp.concatenate(pieces, axis=-1)


def part_of(value, index, count):
    rows = value.shape[0] // count
    return lax.dynamic_slice_in_dim(value, index * rows, rows, 0)


def ordered(bit, mine, theirs):
    first = lax.broadcasted_iota(jnp.int32, (2,) + (1,) * mine.ndim, 0) == bit
    return jnp.where(first, mine[None], theirs[None]).reshape((-1,) + mine.shape[1:])


def sum_of(arrays):
    total = arrays[0].astype(f32)
    for array in arrays[1:]:
        total = total + array.astype(f32)
    return total.astype(bf16)


fence = lax.optimization_barrier


class Links:
    def __init__(self, n_rows, n_blk):
        self.size = {"rows": n_rows, "blk": n_blk}
        self.at = {"rows": lax.axis_index("rows"), "blk": lax.axis_index("blk")}
        self.near = ("rows", 0, 0)
        self.near_bit = self.at["rows"] % 2
        far = list(range(1, n_rows.bit_length() - 1))
        self.far = [("rows", a, b) for a, b in zip(far, far[::-1])]
        self.plain_far = [("rows", a, a) for a in far]
        self.blk_bits = [("blk", k, k) for k in range(n_blk.bit_length() - 1)]

    def bit(self, stage, flip=False):
        axis, even, odd = stage
        at = self.at[axis]
        if even == odd:
            return (at >> even) % 2
        near = 1 - self.near_bit if flip else self.near_bit
        return jnp.where(near == 0, (at >> even) % 2, (at >> odd) % 2)

    def swap(self, value, stage):
        axis, even, odd = stage
        pairs = [(i, i ^ (1 << (odd if i % 2 and even != odd else even))) for i in range(self.size[axis])]
        return lax.ppermute(value, axis, pairs)


class Steps:
    def __init__(self, links):
        self.links = links
        self.stages = links.far + links.blk_bits
        first = links.far[0]
        bits = [links.near_bit, links.bit(first), links.bit(first, True)]
        self.base = len(bits)
        bits += [links.bit(stage) for stage in self.stages]
        self.bits = jnp.stack(bits).astype(jnp.int32)
        self.swap = links.swap

    def run(self, function, *args):
        return function((), *args)[1]

    def cut(self, addends, stage):
        return self.run(split_add, self.bits, self.base + self.stages.index(stage), *addends)

    def halve(self, addends, stage):
        bit = self.links.bit(stage)
        send = sum_of([part_of(a, 1 - bit, 2) for a in addends])
        keep = sum_of([part_of(a, bit, 2) for a in addends])
        return keep, self.swap(send, stage)

    def total(self, addends, stage):
        value = sum_of(addends)
        return value, self.swap(value, stage)

    def double(self, pieces, stage, following):
        value = ordered(self.links.bit(stage), *pieces)
        return value, self.swap(value, following)

    def last(self, pieces, stage, final):
        value = ordered(self.links.bit(stage), *pieces)
        return value, self.swap(value, final), self.swap(value, self.links.near)

    def finish(self, group):
        return group[0], group[2], group[1], self.swap(group[1], self.links.near)


def local(
    n_rows,
    n_blk,
    tokens,
    segments,
    query_weight,
    query_bias,
    key_weight,
    value_weight,
    value_bias,
    out_weight,
    out_bias,
    first_gain,
    first_shift,
    up_weight,
    up_bias,
    down_weight,
    down_bias,
    second_gain,
    second_shift,
    cotangent,
):
    links = Links(n_rows, n_blk)
    pair, cross = links.blk_bits
    seq_at = links.at["blk"] // 2
    near_bit = links.near_bit
    num_seq, tok_rows, width = tokens.shape
    ff = up_weight.shape[1]
    chunks = ff // width
    total_rows = 2 * tok_rows

    piece = tok_rows // 2
    pick = lambda a, s: lax.dynamic_index_in_dim(a, s, 0, keepdims=False)
    other = pick(tokens, 1 - seq_at)
    id_rows = jnp.pad(segments.astype(bf16)[:, None, :], ((0, 0), (0, ID_ROWS - 1), (0, width - tok_rows)))
    own = jnp.concatenate([pick(tokens, seq_at), pick(id_rows, seq_at)], 0)
    other_b = jnp.concatenate([other[piece:], pick(id_rows, 1 - seq_at)], 0)
    far_a = links.swap(other[:piece], cross)
    far_b = links.swap(other_b, cross)
    near_block = links.swap(own, pair)
    last_a = links.swap(far_a, pair)
    last_b = links.swap(far_b, pair)
    cot_other = pick(cotangent, 1 - seq_at)
    cot_other, far_b, far_a = fence((cot_other, far_b, far_a))
    cot_far = links.swap(cot_other, cross)
    here, late = [own, far_a, far_b, near_block], [last_a, last_b]
    value_wide = value_bias.reshape(-1, 128)
    queries, keys, values, numer, totals = attn_some(
        here, query_weight, key_weight, value_weight, query_bias.reshape(-1, 128), value_wide, total_rows
    )
    cot_own = pick(cotangent, seq_at)
    cot_own, late, queries, keys, values, numer, totals = fence(
        (cot_own, late, queries, keys, values, numer, totals)
    )
    blocks = [*here, *late]
    keys, values, attended, inv_totals, seg_row = attn_last(
        here, late, queries, key_weight, value_weight, value_wide, numer, totals, keys, values
    )
    vectors = [
        v.reshape(-1, 128)
        for v in (out_bias, first_gain, first_shift, down_bias, second_gain, second_shift, up_bias)
    ]
    half = chunks // 2
    order = jnp.concatenate(
        [(1 - near_bit) * half + jnp.arange(half), near_bit * half + jnp.arange(half)]
    ).astype(jnp.int32)
    (
        seg_sums, small, d_resid, d_numer, d_total, out_own, out_away, grad_out,
        send_one, send_two, keep_one, keep_two,
    ) = mid(
        order, attended, (own, far_a, far_b), (cot_own, cot_far), inv_totals, seg_row,
        vectors, out_weight, up_weight, down_weight,
    )
    back_in = (queries, keys, values, d_numer, d_total)
    tc = Steps(links)
    bits = tc.bits
    first, *rest = links.far
    backward = rest[::-1] + [first]
    ffn_shape, attn_shape = ((ff, width), (width, ff)), ((width, width),) * 4
    vectors = UP_B + chunks + 2
    seg_at, row_end = vectors, vectors + 16
    pairs = width // 128

    near_end = pairs // 3
    recv_one = tc.swap(send_one, links.near)
    recv_two = tc.swap(send_two, links.near)
    grads_a = tc.run(attn_bwd, *back_in, seg_row, 0, near_end)
    recv_one, recv_two, grads_a, back_in, out_away = fence((recv_one, recv_two, grads_a, back_in, out_away))

    send_one, one = tc.cut((keep_one, recv_one), first)
    send_one, recv_two, back_in, out_away = fence((send_one, recv_two, back_in, out_away))
    one = one, tc.swap(send_one, first)
    send_two, two = tc.cut((keep_two, recv_two), first)
    send_two, back_in, out_away = fence((send_two, back_in, out_away))
    two = two, tc.swap(send_two, first)
    out_back = tc.swap(out_away, cross)
    grads_b = tc.run(attn_bwd, *back_in, seg_row, near_end, pairs - near_end)
    grads = (*grads_a, *grads_b)
    bias_sums, attn_send, attn_keep = tc.run(weight_grad, bits, grads, blocks, grad_out)
    one, two, out_back, grads, bias_sums, attn_send = fence((one, two, out_back, grads, bias_sums, attn_send))

    for stage in rest:
        one = tc.halve(one, stage)
    attn_recv = tc.swap(attn_send, links.near)
    small = jnp.concatenate([small[: UP_B + chunks], bias_sums, seg_sums], 0)
    small_recv = tc.swap(small, pair)
    one, attn_recv, small, small_recv = fence((one, attn_recv, small, small_recv))

    send_three, three = tc.cut((attn_keep, attn_recv), first)
    send_three, one, two = fence((send_three, one, two))
    three = three, tc.swap(send_three, first)
    for stage in rest:
        two = tc.halve(two, stage)
    one = tc.halve(one, pair)
    small = small + small_recv
    small_recv = tc.swap(small, cross)
    d_own, d_away, pair_own, pair_away = tc.run(token_grad, grads, query_weight, key_weight, value_weight, d_resid)
    one, two, three, small, small_recv, d_own, d_away, pair_own, pair_away = fence(
        (one, two, three, small, small_recv, d_own, d_away, pair_own, pair_away)
    )

    for stage in rest:
        three = tc.halve(three, stage)
    one = tc.halve(one, cross)
    two = tc.halve(two, pair)
    both_sums = ordered(seq_at, small[None, seg_at:row_end], small_recv[None, seg_at:row_end])
    small = small[:vectors] + small_recv[:vectors]
    small_recv = tc.swap(small, links.near)
    one, two, three, small, small_recv, both_sums = fence((one, two, three, small, small_recv, both_sums))

    one = tc.total(one, cross)
    three = tc.halve(three, pair)
    two = tc.halve(two, cross)
    for stage in links.plain_far:
        small = small + small_recv
        small_recv = tc.swap(small, stage)
    one, two, three, small, small_recv, both_sums = fence((one, two, three, small, small_recv, both_sums))

    one = tc.double(one, cross, pair)
    two = tc.total(two, cross)
    three = tc.halve(three, cross)
    small = small + small_recv
    pooled = matryoshka(both_sums[:, :NSEG] / both_sums[:, 8 : 8 + NSEG])
    vector_sums = [small[i] for i in range(UP_B)] + [small[UP_B : UP_B + chunks].reshape(-1)]
    vector_sums += [small[UP_B + chunks], small[UP_B + chunks + 1]]
    layer_output = ordered(seq_at, out_own[None], out_back[None])
    one, two, three, pooled, vector_sums, layer_output = fence((one, two, three, pooled, vector_sums, layer_output))

    one = tc.double(one, pair, backward[0])
    two = tc.double(two, cross, pair)
    three = tc.total(three, cross)
    one, two, three, pair_away = fence((one, two, three, pair_away))

    for stage, following in zip(backward[:-2], backward[1:-1]):
        one = tc.double(one, stage, following)
    one = tc.last(one, backward[-2], first)
    two = tc.double(two, pair, backward[0])
    three = tc.double(three, cross, pair)
    pair_away = tc.swap(pair_away, pair)
    one, two, three, d_away, pair_away = fence((one, two, three, d_away, pair_away))

    three = tc.double(three, pair, backward[0])
    for stage, following in zip(backward[:-2], backward[1:-1]):
        two = tc.double(two, stage, following)
    two = tc.last(two, backward[-2], first)
    d_back = tc.swap((d_away + pair_away.astype(f32)).astype(bf16), cross)
    one = tc.finish(one)
    two, three, one, d_back, pair_own = fence((two, three, one, d_back, pair_own))

    for stage, following in zip(backward[:-2], backward[1:-1]):
        three = tc.double(three, stage, following)
    three = tc.last(three, backward[-2], first)
    pair_own = tc.swap(pair_own, pair)
    two = tc.finish(two)
    ffn_sums = tc.run(emit, bits, one, (False, True), ffn_shape, 0)
    down_sum, up_sum = tc.run(emit, bits, two, (False, True), ffn_shape, 1, ffn_sums)
    attn_sums = tc.run(emit, bits, (three[0], three[2]), (False,), attn_shape)
    three, pair_own, down_sum, up_sum, attn_sums, d_back = fence((three, pair_own, down_sum, up_sum, attn_sums, d_back))

    three = tc.finish(three)
    d_own = d_own + pair_own.astype(f32)
    grad_tokens = ordered(seq_at, d_own.astype(bf16)[None], d_back[None])
    query_sum, key_sum, value_sum, out_sum = tc.run(emit, bits, three[2:], (True,), attn_shape, None, attn_sums)
    return (
        layer_output,
        pooled,
        grad_tokens,
        query_sum,
        vector_sums[7],
        key_sum,
        value_sum,
        vector_sums[8],
        out_sum,
        vector_sums[OUT_B],
        vector_sums[G1],
        vector_sums[B1],
        up_sum,
        vector_sums[UP_B],
        down_sum,
        vector_sums[DOWN_B],
        vector_sums[G2],
        vector_sums[B2],
    )


def solution(mesh):
    row_split = P("rows", "blk", None)
    return jax.shard_map(
        partial(local, mesh.shape["rows"], mesh.shape["blk"]),
        mesh=mesh,
        in_specs=(row_split, P("rows", "blk")) + (P(),) * 15 + (row_split,),
        out_specs=(row_split, P("rows", None, None), row_split) + (P(),) * 15,
        check_vma=False,
    )
```

```python
from functools import partial

import jax
import jax.numpy as jnp
from jax import lax
from jax.experimental import pallas as pl
from jax.experimental.pallas import tpu as pltpu
from jax.sharding import PartitionSpec as P

f32=jnp.float32; bf16=jnp.bfloat16
norm_eps=1e-12
NSEG=6
HD=64
def dot(a,b): return jnp.dot(a,b,preferred_element_type=f32)
def dot_nt(a,b): return lax.dot_general(a,b,(((1,),(1,)),((),())),preferred_element_type=f32)
def dot_tn(a,b): return lax.dot_general(a,b,(((0,),(0,)),((),())),preferred_element_type=f32)

def gelu_pair(x):
    t = 1.0 / (1.0 + (0.3275911 * 0.7071067811865476) * jnp.abs(x))
    e = jnp.exp(-0.5 * x * x)
    half = (0.5*0.254829592) + t*((0.5*-0.284496736) + t*((0.5*1.421413741) + t*((0.5*-1.453152027) + t*(0.5*1.061405429))))
    tail = half * t * e
    cdf = jnp.where(x > 0, 1.0 - tail, tail)
    return x * cdf, cdf + x * e * 0.3989422804014327

def in_hbm(*arrays):
    return tuple(pltpu.with_memory_space_constraint(a, pltpu.HBM) for a in arrays)

def wide(rows):
    return jnp.concatenate([rows[i:i+1,:] for i in range(rows.shape[0])], axis=1)

VM = pl.BlockSpec(memory_space=pltpu.VMEM)
SM = pl.BlockSpec(memory_space=pltpu.SMEM)
ANY = pl.BlockSpec(memory_space=pl.ANY)
FAR = pl.BlockSpec(memory_space=pltpu.HBM)
MIB = 1024 * 1024


def call(kernel, deps, args, in_specs, out_specs, out_shape, scratch=(), aliases=None, vmem=16, grid=(), name=None):
    n, m = len(deps), len(args)

    def body(*refs):
        kernel(*refs[n : n + m], *refs[n + m + 1 :])

    token, *outs = pl.pallas_call(
        body,
        grid=grid,
        in_specs=[ANY] * n + list(in_specs),
        out_specs=[FAR] + list(out_specs),
        out_shape=[pltpu.HBM((8, 128), f32)] + list(out_shape),
        scratch_shapes=list(scratch),
        input_output_aliases={n + k: 1 + v for k, v in (aliases or {}).items()},
        compiler_params=pltpu.CompilerParams(vmem_limit_bytes=int(vmem * MIB)),
        name=name,
    )(*deps, *args)
    return in_hbm(token)[0], outs


def same_segment(left, right):
    lab = lax.broadcasted_iota(jnp.int32, (8, 1), 0).astype(f32)
    hot = lambda s: (lab == s).astype(f32).astype(bf16)
    return (dot_tn(hot(left), hot(right)) - 1.0) * 1e30

OUT_B, G1, B1, DOWN_B, G2, B2, UP_B = range(7)
RB = 128

def rows_norm(r):
    m = jnp.mean(r, axis=-1, keepdims=True)
    c = r - m
    inv = lax.rsqrt(jnp.mean(c*c, axis=-1, keepdims=True) + norm_eps)
    return c * inv, inv

def norm_back(g, xh, inv):
    return inv * (g - jnp.mean(g, axis=-1, keepdims=True) - xh * jnp.mean(g*xh, axis=-1, keepdims=True))

def col_sum(v): return jnp.sum(v, axis=0, keepdims=True)

def mid_kernel(order_ref, att_ref, xa_ref, xb_ref, xc_ref, cota_hbm, cotb_hbm, itot_hbm, seg_ref, ob_ref, g1_ref, b1_ref, db_ref, g2_ref, b2_ref, ub_ref, wo_hbm, wu_hbm, wd_hbm,
               segsum_ref, small_ref, dres_ref, dn_ref, dt_ref, outo_hbm, outx_hbm, gout_hbm, send_one, send_two, keep_one, keep_two,
               wo, wu, wd, hid, hl, xh1, rs1, act, gp, feed, dfl, dhid, stage, cota_ref, cotb_ref, itot_ref, out_ref, gout_ref,
               wsem, gsem, csem):
    R, W = att_ref.shape
    nc = wu.shape[0]
    def rows_of(refs, i):
        for ref in refs:
            h = ref.shape[0] // RB
            if i < h:
                return ref[pl.ds(i*RB,RB),:]
            i -= h
    def copies(k):
        c = order_ref[k]
        return (pltpu.make_async_copy(wu_hbm.at[:, pl.ds(c*W, W)], wu.at[k], wsem.at[1+k]),
                pltpu.make_async_copy(wd_hbm.at[pl.ds(c*W, W), :], wd.at[k], wsem.at[1+nc+k]))
    cwo = pltpu.make_async_copy(wo_hbm, wo, wsem.at[0]); cwo.start()
    for k in range(nc):
        for cp in copies(k): cp.start()
    late = [pltpu.make_async_copy(src, dst, csem.at[i]) for i, (src, dst) in enumerate(
        ((cota_hbm, cota_ref), (cotb_hbm, cotb_ref), (itot_hbm, itot_ref), (out_ref.at[pl.ds(0, R//2), :], outo_hbm), (gout_ref, gout_hbm),
         (out_ref.at[pl.ds(R//2, R//2), :], outx_hbm)))]
    for c in late[:3]: c.start()
    NB = R // RB
    vecs = (ob_ref, g1_ref, b1_ref, db_ref, g2_ref, b2_ref)
    row = lambda i: wide(vecs[i][...])
    lanes = W // 128
    cwo.wait()
    feed[...] = dot(att_ref[...].astype(bf16), wo[...])
    for i in range(NB):
        s = pl.ds(i*RB, RB)
        r = rows_of((xa_ref, xb_ref, xc_ref), i).astype(f32) + feed[s, :] + row(OUT_B)
        xh, inv = rows_norm(r)
        xh1[s,:] = xh
        rs1[s,:] = inv
        h = xh * row(G1) + row(B1)
        hid[s,:] = h
        hl[s,:] = h.astype(bf16)
    for k in range(nc):
        for cp in copies(k): cp.wait()
        ub = wide(ub_ref[pl.ds(order_ref[k]*lanes, lanes), :])
        for j in range(W//256):
            cs = slice(j*256, (j+1)*256)
            pre = dot(hl[...], wu[k, :, cs]) + ub[:, cs]
            a_, g_ = gelu_pair(pre)
            act[k, :, cs] = a_.astype(bf16)
            gp[k, :, cs] = g_.astype(gp.dtype)
        part = dot(act[k], wd[k])
        if k == 0: feed[...] = part
        else: feed[...] += part
    late[0].wait()
    late[1].wait()
    lab = (lax.broadcasted_iota(jnp.int32, (8, 1), 0) + 1).astype(f32)
    count = jnp.zeros((8, 1), f32)
    zero = jnp.zeros((1,W),f32)
    segsum = jnp.zeros((8, W), f32)
    sg = ss = sdb = zero
    for i in range(NB):
        s = pl.ds(i*RB, RB)
        xh, inv = rows_norm(hid[s,:] + feed[s,:] + row(DOWN_B))
        o = xh * row(G2) + row(B2)
        oh = o.astype(bf16)
        out_ref[s,:] = oh
        ol = (o - oh.astype(f32)).astype(bf16)
        hot = (lab == seg_ref[0:1, i*RB:(i+1)*RB]).astype(f32)
        count = count + jnp.sum(hot, axis=1, keepdims=True)
        hot = hot.astype(bf16)
        segsum = segsum + dot(hot, oh) + dot(hot, ol)
        u = rows_of((cota_ref, cotb_ref), i).astype(f32)
        sg = sg + col_sum(u*xh)
        ss = ss + col_sum(u)
        d = norm_back(u * row(G2), xh, inv)
        dhid[s,:] = d
        dl = d.astype(bf16)
        dfl[s,:] = dl
        sdb = sdb + col_sum(dl.astype(f32))
    late[3].start()
    late[5].start()
    segsum_ref[0:8, :] = segsum
    segsum_ref[8:16, :] = jnp.broadcast_to(count, (8, W))
    small_ref[pl.ds(DOWN_B,1), :] = sdb
    small_ref[pl.ds(G2,1), :] = sg
    small_ref[pl.ds(B2,1), :] = ss
    def push(slot, k, kind):
        dst = (send_one, send_two, keep_one, keep_two)[k]
        return pltpu.make_async_copy(stage.at[slot], dst.at[pl.ds(kind*W, W), :], gsem.at[slot])
    for k in range(nc):
        stage[k] = dot_tn(act[k], dfl[...]).astype(bf16)
        push(k, k, 0).start()
        da = dot_nt(dfl[...], wd[k])
        dp = (da * gp[k].astype(f32)).astype(bf16)
        act[k] = dp
        small_ref[pl.ds(UP_B + order_ref[k],1), :] = col_sum(dp.astype(f32))
        stage[nc+k] = dot_tn(hl[...], dp).astype(bf16)
        push(nc+k, k, 1).start()
        dhid[...] += dot_nt(dp, wu[k])
    sg = ss = sdb = zero
    for i in range(NB):
        s = pl.ds(i*RB, RB)
        dh = dhid[s,:]
        xh = xh1[s,:]
        sg = sg + col_sum(dh*xh)
        ss = ss + col_sum(dh)
        d = norm_back(dh * row(G1), xh, rs1[s,:])
        dres_ref[s,:] = d
        dl = d.astype(bf16)
        dfl[s,:] = dl
        sdb = sdb + col_sum(dl.astype(f32))
    small_ref[pl.ds(OUT_B,1), :] = sdb
    small_ref[pl.ds(G1,1), :] = sg
    small_ref[pl.ds(B1,1), :] = ss
    gout_ref[...] = dot_tn(att_ref[...].astype(bf16), dfl[...]).astype(bf16)
    late[4].start()
    late[2].wait()
    l0 = lax.broadcasted_iota(jnp.int32, (128,128), 0) // HD
    l1 = lax.broadcasted_iota(jnp.int32, (128,128), 1) // HD
    same = (l0 == l1).astype(f32).astype(bf16)
    feed[...] = dot_nt(dfl[...], wo[...])
    for i in range(NB):
        s = pl.ds(i*RB, RB)
        da = feed[s,:]
        it = itot_ref[s,:]
        dn_ref[s,:] = (da * it).astype(bf16)
        p = da * att_ref[s,:]
        ph = p.astype(bf16)
        plow = (p - ph.astype(f32)).astype(bf16)
        for j in range(W//128):
            cs = slice(j*128,(j+1)*128)
            dt_ref[s, cs] = -(dot(ph[:,cs], same) + dot(plow[:,cs], same)) * it[:,cs]
    for c in late[3:]: c.wait()
    for k in range(nc):
        push(k, k, 0).wait()
        push(nc+k, k, 1).wait()

def mid(order, att, x, cot, itot, seg_row, vecs, wo, wu, wd):
    R, W = att.shape
    nc = wu.shape[1] // W
    any_ = pl.BlockSpec(memory_space=pltpu.HBM)
    vm = pl.BlockSpec(memory_space=pltpu.VMEM)
    sm = pl.BlockSpec(memory_space=pltpu.SMEM)
    sd = pltpu.HBM
    return pl.pallas_call(
        mid_kernel,
        in_specs=[sm]+[vm]*4+[any_]*3+[vm]*8+[any_]*3,
        out_specs=[vm]*5+[any_]*7,
        out_shape=[sd((16,W),f32), sd((UP_B+nc+6,W),f32), sd((R,W),f32), sd((R,W),bf16), sd((R,W),f32), sd((R//2,W),bf16), sd((R//2,W),bf16),
                   sd((W,W),bf16)]+[sd((2*W,W),bf16)]*4,
        scratch_shapes=[pltpu.VMEM((W,W),bf16), pltpu.VMEM((nc,W,W),bf16), pltpu.VMEM((nc,W,W),bf16),
                        pltpu.VMEM((R,W),f32), pltpu.VMEM((R,W),bf16), pltpu.VMEM((R,W),f32), pltpu.VMEM((R,1),f32),
                        pltpu.VMEM((nc,R,W),bf16), pltpu.VMEM((nc,R,W),f32), pltpu.VMEM((R,W),f32), pltpu.VMEM((R,W),bf16), pltpu.VMEM((R,W),f32),
                        pltpu.VMEM((2*nc,W,W),bf16), pltpu.VMEM((R//2,W),bf16), pltpu.VMEM((R//2,W),bf16), pltpu.VMEM((R,W),f32),
                        pltpu.VMEM((R,W),bf16), pltpu.VMEM((W,W),bf16),
                        pltpu.SemaphoreType.DMA((1+2*nc,)), pltpu.SemaphoreType.DMA((2*nc,)), pltpu.SemaphoreType.DMA((6,))],
        compiler_params=pltpu.CompilerParams(vmem_limit_bytes=60*1024*1024),
        name="mid",
    )(order, *in_hbm(att, *x, *cot, itot, seg_row, *vecs, wo, wu, wd))

GW = 256
ID_ROWS = 16
def head_pair_lanes():
    return lax.broadcasted_iota(jnp.int32, (1,128), 1) < HD

def gather_rows(refs, dst, sem):
    at, copies = 0, []
    for i, ref in enumerate(refs):
        n = ref.shape[0] // 128 * 128
        copies.append(pltpu.make_async_copy(ref.at[pl.ds(0, n), :], dst.at[pl.ds(at, n), :], sem.at[i]))
        at += n
    return copies

def gather_ids(refs, dst, sem):
    tails = [ref for ref in refs if ref.shape[0] % 128]
    return [
        pltpu.make_async_copy(ref.at[pl.ds(ref.shape[0] - ID_ROWS, ID_ROWS), :], dst.at[i], sem.at[i])
        for i, ref in enumerate(tails)
    ]

def ids_of(ids, width):
    return jnp.concatenate([ids[i, 0:1, 0:width].astype(f32) for i in range(ids.shape[0])], axis=1)

def attend(q, k, v, bias, first):
    nums, tots = [], []
    for p in range(q.shape[1]//128):
        cs = slice(p*128,(p+1)*128)
        qp, kp, vp = q[:,cs], k[:,cs], v[:,cs]
        one = jnp.ones_like(vp); zero=jnp.zeros_like(qp)
        res = []
        for h in range(2):
            mine = first if h==0 else jnp.logical_not(first)
            s = dot_nt(jnp.where(mine, qp, zero), kp)
            e = jnp.exp(s + bias[...]).astype(bf16)
            res.append(dot(e, jnp.where(mine, vp, one)))
        nums.append(jnp.where(first, res[0], res[1]))
        tots.append(jnp.where(first, res[1], res[0]))
    return nums, tots

def attn_some_kernel(n_parts, *refs):
    parts = refs[:n_parts]
    (wq_ref, wk_ref, wv_ref, qb_ref, vb_ref,
     q_ref, k_ref, v_ref, num_ref, tot_ref, bias, x_ref, ids, sem, isem) = refs[n_parts:]
    R, N = q_ref.shape[0], k_ref.shape[0]
    @pl.when(pl.program_id(0) == 0)
    def _():
        marks = gather_ids(parts, ids, isem)
        copies = gather_rows(parts, x_ref, sem)
        for c in marks + copies: c.start()
        for c in marks: c.wait()
        row = ids_of(ids, N // ids.shape[0])
        bias[...] = same_segment(row[:, 0:R], row)
        for c in copies: c.wait()
    lanes = GW // 128
    at = pl.ds(pl.program_id(0)*lanes, lanes)
    qb, vb = wide(qb_ref[at, :]), wide(vb_ref[at, :])
    q = (0.125*(dot(x_ref[0:R,:], wq_ref[...]) + qb)).astype(bf16)
    k = dot(x_ref[...], wk_ref[...]).astype(bf16)
    v = (dot(x_ref[...], wv_ref[...]) + vb).astype(bf16)
    q_ref[...] = q; k_ref[...] = k; v_ref[...] = v
    nums, tots = attend(q, k, v, bias, head_pair_lanes())
    for p in range(lanes):
        num_ref[:, p*128:(p+1)*128] = nums[p]
        tot_ref[:, p*128:(p+1)*128] = tots[p]

def attn_some(parts, wq, wk, wv, qb, vb, R):
    W = wq.shape[0]
    N = sum(p.shape[0] // 128 * 128 for p in parts)
    n_ids = sum(1 for p in parts if p.shape[0] % 128)
    whole = N // n_ids * (n_ids + 1)
    sd = pltpu.HBM
    full = lambda a: pl.BlockSpec(a.shape, lambda j: (0,0))
    col = lambda r: pl.BlockSpec((r,GW), lambda j: (0,j))
    return pl.pallas_call(
        partial(attn_some_kernel, len(parts)), grid=(W//GW,),
        in_specs=[pl.BlockSpec(memory_space=pltpu.HBM)]*len(parts)+[col(W), col(W), col(W), full(qb), full(vb)],
        out_specs=[col(R), col(N), col(N), col(R), col(R)],
        out_shape=[sd((R,W),bf16), sd((whole,W),bf16), sd((whole,W),bf16), sd((R,W),f32), sd((R,W),f32)],
        scratch_shapes=[pltpu.VMEM((R,N),f32), pltpu.VMEM((N,W),bf16), pltpu.VMEM((n_ids,ID_ROWS,W),bf16),
                        pltpu.SemaphoreType.DMA((len(parts),)), pltpu.SemaphoreType.DMA((n_ids,))],
        compiler_params=pltpu.CompilerParams(vmem_limit_bytes=24*1024*1024, dimension_semantics=("arbitrary",)),
        name="attn_some",
    )(*in_hbm(*parts, wq, wk, wv, qb, vb))

def attn_last_kernel(n_parts, n_all, *refs):
    parts = refs[n_all-n_parts:n_all]
    (q_ref, wk_ref, wv_ref, vb_ref, num_ref, tot_ref, _, _,
     k_ref, v_ref, att_ref, itot_ref, sk_ref, bias, x_ref, ids, sem, isem) = refs[n_all:]
    R, N = q_ref.shape[0], k_ref.shape[0]
    whole = sk_ref.shape[1]
    @pl.when(pl.program_id(0) == 0)
    def _():
        marks = gather_ids(refs[:n_all], ids, isem)
        copies = gather_rows(parts, x_ref, sem)
        for c in marks + copies: c.start()
        for c in marks: c.wait()
        row = ids_of(ids, N)
        sk_ref[...] = jnp.broadcast_to(row, sk_ref.shape)
        bias[...] = same_segment(row[:, 0:R], row[:, whole-N:whole])
        for c in copies: c.wait()
    lanes = GW // 128
    vb = wide(vb_ref[pl.ds(pl.program_id(0)*lanes, lanes), :])
    k = dot(x_ref[...], wk_ref[...]).astype(bf16)
    v = (dot(x_ref[...], wv_ref[...]) + vb).astype(bf16)
    k_ref[...] = k; v_ref[...] = v
    nums, tots = attend(q_ref[...], k, v, bias, head_pair_lanes())
    for p in range(lanes):
        cs = slice(p*128, (p+1)*128)
        it = 1.0 / pltpu.roll(tots[p] + tot_ref[:, cs], HD, 1)
        att_ref[:,cs] = (nums[p] + num_ref[:, cs]) * it
        itot_ref[:,cs] = it

def attn_last(here, parts, q, wk, wv, vb, num, tot, k, v):
    R, W = q.shape
    N = sum(p.shape[0] // 128 * 128 for p in parts)
    whole = k.shape[0]
    sd = pltpu.HBM
    every = [*here, *parts]
    n = len(every)
    n_ids = sum(1 for p in every if p.shape[0] % 128)
    any_ = pl.BlockSpec(memory_space=pltpu.HBM)
    full = lambda a: pl.BlockSpec(a.shape, lambda j: (0,0))
    col = lambda r: pl.BlockSpec((r,GW), lambda j: (0,j))
    tail = pl.BlockSpec((N,GW), lambda j: (whole//N-1,j))
    return pl.pallas_call(
        partial(attn_last_kernel, len(parts), n), grid=(W//GW,),
        in_specs=[any_]*n+[col(R), col(W), col(W), full(vb), col(R), col(R), any_, any_],
        out_specs=[tail, tail, col(R), col(R), pl.BlockSpec((8,whole), lambda j: (0,0))],
        out_shape=[sd((whole,W),bf16), sd((whole,W),bf16), sd((R,W),f32), sd((R,W),f32), sd((8,whole),f32)],
        input_output_aliases={n+6: 0, n+7: 1},
        scratch_shapes=[pltpu.VMEM((R,N),f32), pltpu.VMEM((N,W),bf16), pltpu.VMEM((n_ids,ID_ROWS,W),bf16),
                        pltpu.SemaphoreType.DMA((n,)), pltpu.SemaphoreType.DMA((n_ids,))],
        compiler_params=pltpu.CompilerParams(vmem_limit_bytes=20*1024*1024, dimension_semantics=("arbitrary",)),
        name="attn_last",
    )(*in_hbm(*every, q, wk, wv, vb, num, tot), k, v)

def attn_bwd_kernel(q_ref, k_ref, v_ref, dn_ref, dt_ref, sk_ref, dq_ref, dk_ref, dv_ref, bias):
    @pl.when(pl.program_id(0) == 0)
    def _():
        row = sk_ref[0:1, :]
        bias[...] = same_segment(row, row[:, 0:q_ref.shape[0]])
    first = head_pair_lanes()
    lane = lax.broadcasted_iota(jnp.int32, (1,128), 1)
    for p in range(q_ref.shape[1]//128):
        cs = slice(p*128,(p+1)*128)
        qp, kp, vp, dnp = q_ref[:,cs], k_ref[:,cs], v_ref[:,cs], dn_ref[:,cs]
        dtr = pltpu.roll(dt_ref[:,cs], HD, 1)
        hi = dtr.astype(bf16)
        rest = dtr - hi.astype(f32)
        mid_ = rest.astype(bf16)
        low = (rest - mid_.astype(f32)).astype(bf16)
        res=[]
        for h in range(2):
            mine = first if h==0 else jnp.logical_not(first)
            o = HD if h==0 else 0
            ex = jnp.where(lane==o, hi, jnp.where(lane==o+1, mid_, jnp.where(lane==o+2, low, jnp.zeros_like(hi))))
            dne = jnp.where(mine, dnp, ex)
            ve = jnp.where(mine, vp, jnp.where((lane>=o)&(lane<o+3), jnp.ones_like(vp), jnp.zeros_like(vp)))
            s = dot_nt(jnp.where(mine, kp, jnp.zeros_like(kp)), qp)
            e = jnp.exp(s + bias[...])
            pr = dot_nt(ve, dne)
            ds = (e * pr).astype(bf16)
            dv = dot(e.astype(bf16), dnp)
            dk = dot(ds, qp)
            dq = dot_tn(kp, ds)
            res.append((dq,dk,dv))
        dq = jnp.concatenate([res[0][0][0:HD, :], res[1][0][HD:, :]], axis=0)
        dq_ref[:,cs] = (jnp.transpose(dq).astype(bf16).astype(f32)*0.125).astype(bf16)
        dk_ref[:,cs] = jnp.where(first, res[0][1], res[1][1]).astype(bf16)
        dv_ref[:,cs] = jnp.where(first, res[0][2], res[1][2]).astype(bf16)

def attn_bwd(deps,q,k,v,dn,dt,sk,start,count):
    R,W=q.shape; N=k.shape[0]
    sd = pltpu.HBM
    GB=128
    col = lambda r: pl.BlockSpec((r,GB), lambda j: (0,j+start))
    out = lambda r: pl.BlockSpec((r,GB), lambda j: (0,j))
    return call(
        attn_bwd_kernel, deps, in_hbm(q,k,v,dn,dt,sk),
        [col(R), col(N), col(N), col(R), col(R), pl.BlockSpec(sk.shape, lambda j: (0,0))],
        [out(R), out(N), out(N)],
        [sd((R,GB*count),bf16), sd((N,GB*count),bf16), sd((N,GB*count),bf16)],
        [pltpu.VMEM((N,R),f32)], grid=(count,), vmem=16, name="attn_bwd",
    )

def spans(refs):
    at, out = 0, []
    for r in refs:
        out.append(slice(at, at + r.shape[1]))
        at += r.shape[1]
    return out

def token_grad_kernel(n_grads, *refs):
    grads, (wq_ref, wk_ref, wv_ref, dres_ref, own_ref, away_ref, pa_ref, pb_ref) = refs[:n_grads], refs[n_grads:]
    dq, dk, dv = grads[0::3], grads[1::3], grads[2::3]
    R = dq[0].shape[0]
    parts = spans(dq)
    def back(refs, w_ref, rows):
        total = dot_nt(refs[0][rows,:], w_ref[:,parts[0]])
        for r, cs in zip(refs[1:], parts[1:]): total = total + dot_nt(r[rows,:], w_ref[:,cs])
        return total
    top, rest = slice(0,R), slice(R,2*R)
    pair = (back(dk, wk_ref, rest) + back(dv, wv_ref, rest)).astype(bf16)
    pa_ref[...] = pair[:R//2]
    pb_ref[...] = pair[R//2:]
    mine = (dres_ref[...] + back(dq, wq_ref, top) + back(dk, wk_ref, top)
            + back(dv, wv_ref, top))
    own_ref[...] = mine[:R//2]
    away_ref[...] = mine[R//2:]

def token_grad(deps, grads, wq, wk, wv, dres):
    R, W = dres.shape
    sd = pltpu.HBM
    return call(
        partial(token_grad_kernel, len(grads)), deps, in_hbm(*grads, wq, wk, wv, dres),
        [VM]*(len(grads)+4), [VM]*4, [sd((R//2,W),f32)]*2+[sd((R//2,W),bf16)]*2, vmem=24, name="token_grad",
    )

def weight_grad_kernel(n_parts, n_grads, *refs):
    tokens, grads = refs[:n_parts], refs[n_parts:n_parts+n_grads]
    dq, dk, dv = grads[0::3], grads[1::3], grads[2::3]
    (bit_ref, gout_ref, bsum_ref, gsend_hbm, gkeep_hbm, stage, x_ref, sem, xsem) = refs[n_parts+n_grads:]
    copies = gather_rows(tokens, x_ref, xsem)
    for c in copies: c.start()
    W = x_ref.shape[1]
    bit = bit_ref[0]
    parts = spans(dq)
    def push(i, start):
        src = gout_ref if i == 3 else stage.at[i]
        def go(dst):
            cp = pltpu.make_async_copy(src, dst.at[pl.ds((i%2)*W, W), :], sem.at[i])
            cp.start() if start else cp.wait()
        @pl.when(bit == i//2)
        def _(): go(gkeep_hbm)
        @pl.when(bit != i//2)
        def _(): go(gsend_hbm)
    push(3, True)
    for c in copies: c.wait()
    for i, refs in ((2,dv), (1,dk), (0,dq)):
        for ref, cs in zip(refs, parts):
            n = ref.shape[0]
            stage[i, :, cs] = dot_tn(x_ref[0:n,:], ref[...]).astype(bf16)
        push(i, True)
    for ref, cs in zip(dq, parts): bsum_ref[0:1,cs] = col_sum(ref[...].astype(f32))
    for ref, cs in zip(dv, parts): bsum_ref[1:2,cs] = col_sum(ref[...].astype(f32))
    for i in range(4): push(i, False)

def weight_grad(deps, bits, grads, tokens, gout):
    R = grads[0].shape[0]
    W = gout.shape[0]
    sd = pltpu.HBM
    return call(
        partial(weight_grad_kernel, len(tokens), len(grads)), deps, (*in_hbm(*tokens, *grads), bits, *in_hbm(gout)),
        [FAR]*len(tokens)+[VM]*len(grads)+[SM, VM], [VM,FAR,FAR],
        [sd((2,W),f32), sd((2*W,W),bf16), sd((2*W,W),bf16)],
        [pltpu.VMEM((3,W,W),bf16), pltpu.VMEM((2*R,W),bf16), pltpu.SemaphoreType.DMA((4,)), pltpu.SemaphoreType.DMA((len(tokens),))],
        vmem=22, name="weight_grad",
    )

def emit_kernel(up_from, n_prev, second, bits_ref, *refs):
    n_in = len(second) * 2
    pieces_in, outs, (stage, sem) = refs[:n_in], refs[n_in+n_prev:-2], refs[-2:]
    n, W = pieces_in[0].shape
    bit, mine, theirs = bits_ref[0], bits_ref[1], bits_ref[2]
    pieces = []
    for i, s in enumerate(second):
        pieces.append((bit, 1 - mine if s else mine, pieces_in[2*i]))
        pieces.append((1 - bit, 1 - theirs if s else theirs, pieces_in[2*i+1]))
    def send(i, start):
        half, block, ref = pieces[i]
        for b in range(2):
            for h in range(2):
                if up_from is None: dst = outs[2*h + b]
                elif b == 0: dst = outs[0].at[pl.ds((2*h + up_from)*W, W), :]
                else: dst = outs[1].at[:, pl.ds((2*h + up_from)*W, W)]
                @pl.when((half == h) & (block == b))
                def _():
                    cp = pltpu.make_async_copy(stage.at[i], dst, sem.at[i])
                    cp.start() if start else cp.wait()
    for i, (half, block, ref) in enumerate(pieces):
        stage[i] = ref[...].astype(f32)
        send(i, True)
    for i in range(len(pieces)): send(i, False)

def emit(deps, bits, pieces, second, out_shape, up_from=None, prev=()):
    n, W = pieces[0].shape
    m = len(pieces)
    return call(
        partial(emit_kernel, up_from, len(prev), second), deps, (bits, *pieces, *prev),
        [SM]+[VM]*m+[FAR]*len(prev), [FAR]*len(out_shape), [pltpu.HBM(s, f32) for s in out_shape],
        [pltpu.VMEM((m,n,W),f32), pltpu.SemaphoreType.DMA((m,))],
        {1+m+i: i for i in range(len(prev))}, vmem=18, name="emit",
    )

def split_kernel(index, bits_ref, keep_hbm, recv_hbm, *refs):
    outs, (a, b, o, sem) = refs[:2], refs[2:]
    n = outs[0].shape[0]
    bit = bits_ref[index]
    steps = o.shape[0] // 2
    rows = n // steps
    def load(i):
        src = pl.ds((bit if i // steps else 1 - bit)*n + i % steps*rows, rows)
        return (pltpu.make_async_copy(keep_hbm.at[src, :], a.at[i], sem.at[0, i]),
                pltpu.make_async_copy(recv_hbm.at[src, :], b.at[i], sem.at[1, i]))
    def store(i):
        return pltpu.make_async_copy(o.at[i], outs[i // steps].at[pl.ds(i % steps*rows, rows), :], sem.at[2, i])
    for i in range(2*steps):
        for c in load(i): c.start()
    for i in range(2*steps):
        for c in load(i): c.wait()
        o[i] = (a[i].astype(f32) + b[i].astype(f32)).astype(bf16)
        store(i).start()
    for i in range(2*steps): store(i).wait()

def split_add(deps, bits, index, keep, recv):
    n, W = keep.shape[0] // 2, keep.shape[1]
    if n % 16:
        keep, recv, deps = lax.optimization_barrier((keep, recv, tuple(deps)))
        bit = bits[index]
        halves = [[lax.dynamic_slice_in_dim(a, b * n, n, 0).astype(f32) for a in (keep, recv)] for b in (1 - bit, bit)]
        return deps[0], [(a + b).astype(bf16) for a, b in halves]
    steps = n // 192 if n % 192 == 0 else 1
    return call(
        partial(split_kernel, index), deps, (bits, *in_hbm(keep), recv), [SM, FAR, ANY], [FAR]*2,
        [pltpu.HBM((n,W),bf16)]*2,
        [pltpu.VMEM((2*steps,n//steps,W),bf16)]*3+[pltpu.SemaphoreType.DMA((3,2*steps))],
        vmem=14*n*W/MIB+1, name="split_add",
    )

def join_kernel(index, bits_ref, mine_hbm, recv_hbm, out_hbm, both, sem):
    n = mine_hbm.shape[0]
    bit = bits_ref[index]
    loads = [pltpu.make_async_copy(src, both.at[pl.ds(at*n, n), :], sem.at[i])
             for i, (src, at) in enumerate(((mine_hbm, bit), (recv_hbm, 1 - bit)))]
    for c in loads: c.start()
    for c in loads: c.wait()
    out = pltpu.make_async_copy(both, out_hbm, sem.at[2])
    out.start()
    out.wait()

def join(deps, bits, index, mine, recv):
    n, W = mine.shape
    if n % 16:
        mine, recv, deps = lax.optimization_barrier((mine, recv, tuple(deps)))
        return deps[0], [jnp.where(bits[index] == 0, jnp.concatenate([mine, recv], 0), jnp.concatenate([recv, mine], 0))]
    return call(
        partial(join_kernel, index), deps, (bits, mine, recv), [SM, ANY, ANY], [ANY],
        [jax.ShapeDtypeStruct((2*n,W),bf16)], [pltpu.VMEM((2*n,W),bf16), pltpu.SemaphoreType.DMA((3,))],
        vmem=8*n*W/MIB+1, name="join",
    )

def add_kernel(a_ref, b_ref, o_ref):
    o_ref[...] = (a_ref[...].astype(f32) + b_ref[...].astype(f32)).astype(o_ref.dtype)

def add_to(deps, a, b, dtype):
    return call(add_kernel, deps, (a, b), [VM, VM], [VM], [jax.ShapeDtypeStruct(a.shape, dtype)], vmem=8, name="add")

def stack_kernel(*refs):
    out, at = refs[-1], 0
    for r in refs[:-1]:
        out[at:at+r.shape[0], :] = r[...]
        at += r.shape[0]

def stack_rows(deps, arrays):
    rows = sum(a.shape[0] for a in arrays)
    return call(stack_kernel, deps, arrays, [VM]*len(arrays), [VM],
                [jax.ShapeDtypeStruct((rows, arrays[0].shape[1]), f32)], vmem=4, name="stack_rows")

D = 768
pool_eps = 1e-06


def matryoshka(averages):
    pieces = []
    for prefix in (D, D * 2 // 3, D // 3, D // 6, D // 12):
        leading = averages[..., :prefix]
        centred = leading - jnp.mean(leading, axis=-1, keepdims=True)
        pieces.append(
            centred * lax.rsqrt(jnp.mean(centred * centred, axis=-1, keepdims=True) + pool_eps)
        )
    return jnp.concatenate(pieces, axis=-1)


def part_of(value, index, count):
    rows = value.shape[0] // count
    return lax.dynamic_slice_in_dim(value, index * rows, rows, 0)


def ordered(bit, mine, theirs):
    first = lax.broadcasted_iota(jnp.int32, (2,) + (1,) * mine.ndim, 0) == bit
    return jnp.where(first, mine[None], theirs[None]).reshape((-1,) + mine.shape[1:])


def sum_of(arrays):
    total = arrays[0].astype(f32)
    for array in arrays[1:]:
        total = total + array.astype(f32)
    return total.astype(bf16)


fence = lax.optimization_barrier


class Links:
    def __init__(self, n_rows, n_blk):
        self.size = {"rows": n_rows, "blk": n_blk}
        self.at = {"rows": lax.axis_index("rows"), "blk": lax.axis_index("blk")}
        self.near = ("rows", 0, 0)
        self.near_bit = self.at["rows"] % 2
        far = list(range(1, n_rows.bit_length() - 1))
        self.far = [("rows", a, b) for a, b in zip(far, far[::-1])]
        self.plain_far = [("rows", a, a) for a in far]
        self.blk_bits = [("blk", k, k) for k in range(n_blk.bit_length() - 1)]

    def bit(self, stage, flip=False):
        axis, even, odd = stage
        at = self.at[axis]
        if even == odd:
            return (at >> even) % 2
        near = 1 - self.near_bit if flip else self.near_bit
        return jnp.where(near == 0, (at >> even) % 2, (at >> odd) % 2)

    def swap(self, value, stage):
        axis, even, odd = stage
        pairs = [(i, i ^ (1 << (odd if i % 2 and even != odd else even))) for i in range(self.size[axis])]
        return lax.ppermute(value, axis, pairs)


class Steps:
    def __init__(self, links):
        self.links = links
        self.stages = links.far + links.blk_bits
        first = links.far[0]
        bits = [links.near_bit, links.bit(first), links.bit(first, True)]
        self.base = len(bits)
        bits += [links.bit(stage) for stage in self.stages]
        self.bits = jnp.stack(bits).astype(jnp.int32)
        self.swap = links.swap

    def run(self, function, *args):
        return function((), *args)[1]

    def cut(self, addends, stage):
        return self.run(split_add, self.bits, self.base + self.stages.index(stage), *addends)

    def halve(self, addends, stage):
        bit = self.links.bit(stage)
        send = sum_of([part_of(a, 1 - bit, 2) for a in addends])
        keep = sum_of([part_of(a, bit, 2) for a in addends])
        return keep, self.swap(send, stage)

    def total(self, addends, stage):
        value = sum_of(addends)
        return value, self.swap(value, stage)

    def double(self, pieces, stage, following):
        value = ordered(self.links.bit(stage), *pieces)
        return value, self.swap(value, following)

    def last(self, pieces, stage, final):
        value = ordered(self.links.bit(stage), *pieces)
        return value, self.swap(value, final), self.swap(value, self.links.near)

    def finish(self, group):
        return group[0], group[2], group[1], self.swap(group[1], self.links.near)


def local(
    n_rows,
    n_blk,
    tokens,
    segments,
    query_weight,
    query_bias,
    key_weight,
    value_weight,
    value_bias,
    out_weight,
    out_bias,
    first_gain,
    first_shift,
    up_weight,
    up_bias,
    down_weight,
    down_bias,
    second_gain,
    second_shift,
    cotangent,
):
    links = Links(n_rows, n_blk)
    pair, cross = links.blk_bits
    seq_at = links.at["blk"] // 2
    near_bit = links.near_bit
    num_seq, tok_rows, width = tokens.shape
    ff = up_weight.shape[1]
    chunks = ff // width
    total_rows = 2 * tok_rows

    piece = tok_rows // 2
    pick = lambda a, s: lax.dynamic_index_in_dim(a, s, 0, keepdims=False)
    other = pick(tokens, 1 - seq_at)
    id_rows = jnp.pad(segments.astype(bf16)[:, None, :], ((0, 0), (0, ID_ROWS - 1), (0, width - tok_rows)))
    own = jnp.concatenate([pick(tokens, seq_at), pick(id_rows, seq_at)], 0)
    other_b = jnp.concatenate([other[piece:], pick(id_rows, 1 - seq_at)], 0)
    far_a = links.swap(other[:piece], cross)
    far_b = links.swap(other_b, cross)
    near_block = links.swap(own, pair)
    last_a = links.swap(far_a, pair)
    last_b = links.swap(far_b, pair)
    cot_other = pick(cotangent, 1 - seq_at)
    cot_other, far_b, far_a = fence((cot_other, far_b, far_a))
    cot_far = links.swap(cot_other, cross)
    here, late = [own, far_a, far_b, near_block], [last_a, last_b]
    value_wide = value_bias.reshape(-1, 128)
    queries, keys, values, numer, totals = attn_some(
        here, query_weight, key_weight, value_weight, query_bias.reshape(-1, 128), value_wide, total_rows
    )
    cot_own = pick(cotangent, seq_at)
    cot_own, late, queries, keys, values, numer, totals = fence(
        (cot_own, late, queries, keys, values, numer, totals)
    )
    blocks = [*here, *late]
    keys, values, attended, inv_totals, seg_row = attn_last(
        here, late, queries, key_weight, value_weight, value_wide, numer, totals, keys, values
    )
    vectors = [
        v.reshape(-1, 128)
        for v in (out_bias, first_gain, first_shift, down_bias, second_gain, second_shift, up_bias)
    ]
    half = chunks // 2
    order = jnp.concatenate(
        [(1 - near_bit) * half + jnp.arange(half), near_bit * half + jnp.arange(half)]
    ).astype(jnp.int32)
    (
        seg_sums, small, d_resid, d_numer, d_total, out_own, out_away, grad_out,
        send_one, send_two, keep_one, keep_two,
    ) = mid(
        order, attended, (own, far_a, far_b), (cot_own, cot_far), inv_totals, seg_row,
        vectors, out_weight, up_weight, down_weight,
    )
    back_in = (queries, keys, values, d_numer, d_total)
    tc = Steps(links)
    bits = tc.bits
    first, *rest = links.far
    backward = rest[::-1] + [first]
    ffn_shape, attn_shape = ((ff, width), (width, ff)), ((width, width),) * 4
    vectors = UP_B + chunks + 2
    seg_at, row_end = vectors, vectors + 16
    pairs = width // 128

    near_end = pairs // 3
    recv_one = tc.swap(send_one, links.near)
    recv_two = tc.swap(send_two, links.near)
    grads_a = tc.run(attn_bwd, *back_in, seg_row, 0, near_end)
    recv_one, recv_two, grads_a, back_in, out_away = fence((recv_one, recv_two, grads_a, back_in, out_away))

    send_one, one = tc.cut((keep_one, recv_one), first)
    send_one, recv_two, back_in, out_away = fence((send_one, recv_two, back_in, out_away))
    one = one, tc.swap(send_one, first)
    send_two, two = tc.cut((keep_two, recv_two), first)
    send_two, back_in, out_away = fence((send_two, back_in, out_away))
    two = two, tc.swap(send_two, first)
    out_back = tc.swap(out_away, cross)
    grads_b = tc.run(attn_bwd, *back_in, seg_row, near_end, pairs - near_end)
    send_one, one = tc.cut(one, rest[0])
    send_one, grads_a, grads_b, out_back = fence((send_one, grads_a, grads_b, out_back))
    one = one, tc.swap(send_one, rest[0])
    grads = (*grads_a, *grads_b)
    bias_sums, attn_send, attn_keep = tc.run(weight_grad, bits, grads, blocks, grad_out)
    one, two, grads, bias_sums, attn_send = fence((one, two, grads, bias_sums, attn_send))

    for stage in rest:
        two = tc.halve(two, stage)
    for stage in [*rest[1:], pair]:
        one = tc.halve(one, stage)
    attn_recv = tc.swap(attn_send, links.near)
    small = jnp.concatenate([small[: UP_B + chunks], bias_sums, seg_sums], 0)
    small_recv = tc.swap(small, cross)
    one, two, attn_recv, small, small_recv = fence((one, two, attn_recv, small, small_recv))

    send_three, three = tc.cut((attn_keep, attn_recv), first)
    send_three, one, two = fence((send_three, one, two))
    three = three, tc.swap(send_three, first)
    one = tc.halve(one, cross)
    two = tc.halve(two, pair)
    small = jnp.concatenate([small[:vectors] + small_recv[:vectors], small[vectors:], small_recv[vectors:]], 0)
    small_recv = tc.swap(small, pair)
    d_own, d_away, pair_own, pair_away = tc.run(token_grad, grads, query_weight, key_weight, value_weight, d_resid)
    one, two, three, small, small_recv, d_own, d_away, pair_own, pair_away = fence(
        (one, two, three, small, small_recv, d_own, d_away, pair_own, pair_away)
    )

    for stage in rest:
        three = tc.halve(three, stage)
    one = tc.total(one, cross)
    small = small + small_recv
    both_sums = ordered(seq_at, small[None, seg_at:row_end], small[None, row_end:])
    small = small[:vectors]
    small_recv = tc.swap(small, links.near)
    one, two, three, small, small_recv, both_sums = fence((one, two, three, small, small_recv, both_sums))

    one = tc.double(one, cross, pair)
    three = tc.halve(three, pair)
    two = tc.halve(two, cross)
    for stage in links.plain_far:
        small = small + small_recv
        small_recv = tc.swap(small, stage)
    one, two, three, small, small_recv, both_sums, pair_away = fence(
        (one, two, three, small, small_recv, both_sums, pair_away)
    )

    pair_away = tc.swap(pair_away, pair)
    one = tc.double(one, pair, backward[0])
    two = tc.total(two, cross)
    three = tc.halve(three, cross)
    small = small + small_recv
    pooled = matryoshka(both_sums[:, :NSEG] / both_sums[:, 8 : 8 + NSEG])
    vector_sums = [small[i] for i in range(UP_B)] + [small[UP_B : UP_B + chunks].reshape(-1)]
    vector_sums += [small[UP_B + chunks], small[UP_B + chunks + 1]]
    layer_output = ordered(seq_at, out_own[None], out_back[None])
    one, two, three, pooled, vector_sums, layer_output, pair_away = fence(
        (one, two, three, pooled, vector_sums, layer_output, pair_away)
    )

    for stage, following in zip(backward[:-2], backward[1:-1]):
        one = tc.double(one, stage, following)
    one = tc.last(one, backward[-2], first)
    two = tc.double(two, cross, pair)
    three = tc.total(three, cross)
    one, two, three = fence((one, two, three))

    one = tc.finish(one)
    two = tc.double(two, pair, backward[0])
    three = tc.double(three, cross, pair)
    one, two, three, d_away, pair_away = fence((one, two, three, d_away, pair_away))

    three = tc.double(three, pair, backward[0])
    for stage, following in zip(backward[:-2], backward[1:-1]):
        two = tc.double(two, stage, following)
    two = tc.last(two, backward[-2], first)
    d_back = tc.swap((d_away + pair_away.astype(f32)).astype(bf16), cross)
    ffn_sums = tc.run(emit, bits, one, (False, True), ffn_shape, 0)
    two, three, ffn_sums, d_back, pair_own = fence((two, three, ffn_sums, d_back, pair_own))

    for stage, following in zip(backward[:-2], backward[1:-1]):
        three = tc.double(three, stage, following)
    three = tc.last(three, backward[-2], first)
    pair_own = tc.swap(pair_own, pair)
    two = tc.finish(two)
    down_sum, up_sum = tc.run(emit, bits, two, (False, True), ffn_shape, 1, ffn_sums)
    attn_sums = tc.run(emit, bits, (three[0], three[2]), (False,), attn_shape)
    three, pair_own, down_sum, up_sum, attn_sums, d_back = fence((three, pair_own, down_sum, up_sum, attn_sums, d_back))

    three = tc.finish(three)
    d_own = d_own + pair_own.astype(f32)
    grad_tokens = ordered(seq_at, d_own.astype(bf16)[None], d_back[None])
    query_sum, key_sum, value_sum, out_sum = tc.run(emit, bits, three[2:], (True,), attn_shape, None, attn_sums)
    return (
        layer_output,
        pooled,
        grad_tokens,
        query_sum,
        vector_sums[7],
        key_sum,
        value_sum,
        vector_sums[8],
        out_sum,
        vector_sums[OUT_B],
        vector_sums[G1],
        vector_sums[B1],
        up_sum,
        vector_sums[UP_B],
        down_sum,
        vector_sums[DOWN_B],
        vector_sums[G2],
        vector_sums[B2],
    )


def solution(mesh):
    row_split = P("rows", "blk", None)
    return jax.shard_map(
        partial(local, mesh.shape["rows"], mesh.shape["blk"]),
        mesh=mesh,
        in_specs=(row_split, P("rows", "blk")) + (P(),) * 15 + (row_split,),
        out_specs=(row_split, P("rows", None, None), row_split) + (P(),) * 15,
        check_vma=False,
    )
```

```python
from functools import partial

import jax
import jax.numpy as jnp
from jax import lax
from jax.experimental import pallas as pl
from jax.experimental.pallas import tpu as pltpu
from jax.sharding import PartitionSpec as P

f32=jnp.float32; bf16=jnp.bfloat16
norm_eps=1e-12
NSEG=6
HD=64
def dot(a,b): return jnp.dot(a,b,preferred_element_type=f32)
def dot_nt(a,b): return lax.dot_general(a,b,(((1,),(1,)),((),())),preferred_element_type=f32)
def dot_tn(a,b): return lax.dot_general(a,b,(((0,),(0,)),((),())),preferred_element_type=f32)

def gelu_pair(x):
    t = 1.0 / (1.0 + (0.3275911 * 0.7071067811865476) * jnp.abs(x))
    e = jnp.exp(-0.5 * x * x)
    half = (0.5*0.254829592) + t*((0.5*-0.284496736) + t*((0.5*1.421413741) + t*((0.5*-1.453152027) + t*(0.5*1.061405429))))
    tail = half * t * e
    cdf = jnp.where(x > 0, 1.0 - tail, tail)
    return x * cdf, cdf + x * e * 0.3989422804014327

def in_hbm(*arrays):
    return tuple(pltpu.with_memory_space_constraint(a, pltpu.HBM) for a in arrays)

def wide(rows):
    return jnp.concatenate([rows[i:i+1,:] for i in range(rows.shape[0])], axis=1)

VM = pl.BlockSpec(memory_space=pltpu.VMEM)
SM = pl.BlockSpec(memory_space=pltpu.SMEM)
ANY = pl.BlockSpec(memory_space=pl.ANY)
FAR = pl.BlockSpec(memory_space=pltpu.HBM)
MIB = 1024 * 1024


def call(kernel, deps, args, in_specs, out_specs, out_shape, scratch=(), aliases=None, vmem=16, grid=(), name=None):
    n, m = len(deps), len(args)

    def body(*refs):
        kernel(*refs[n : n + m], *refs[n + m + 1 :])

    token, *outs = pl.pallas_call(
        body,
        grid=grid,
        in_specs=[ANY] * n + list(in_specs),
        out_specs=[FAR] + list(out_specs),
        out_shape=[pltpu.HBM((8, 128), f32)] + list(out_shape),
        scratch_shapes=list(scratch),
        input_output_aliases={n + k: 1 + v for k, v in (aliases or {}).items()},
        compiler_params=pltpu.CompilerParams(vmem_limit_bytes=int(vmem * MIB)),
        name=name,
    )(*deps, *args)
    return in_hbm(token)[0], outs


def same_segment(left, right):
    lab = lax.broadcasted_iota(jnp.int32, (8, 1), 0).astype(f32)
    hot = lambda s: (lab == s).astype(f32).astype(bf16)
    return (dot_tn(hot(left), hot(right)) - 1.0) * 1e30

OUT_B, G1, B1, DOWN_B, G2, B2, UP_B = range(7)
RB = 128

def rows_norm(r):
    m = jnp.mean(r, axis=-1, keepdims=True)
    c = r - m
    inv = lax.rsqrt(jnp.mean(c*c, axis=-1, keepdims=True) + norm_eps)
    return c * inv, inv

def norm_back(g, xh, inv):
    return inv * (g - jnp.mean(g, axis=-1, keepdims=True) - xh * jnp.mean(g*xh, axis=-1, keepdims=True))

def col_sum(v): return jnp.sum(v, axis=0, keepdims=True)

def mid_kernel(order_ref, att_ref, xa_ref, xb_ref, xc_ref, cota_hbm, cotb_hbm, itot_hbm, seg_ref, ob_ref, g1_ref, b1_ref, db_ref, g2_ref, b2_ref, ub_ref, wo_hbm, wu_hbm, wd_hbm,
               segsum_ref, small_ref, dres_ref, dn_ref, dt_ref, outo_hbm, outx_hbm, gout_hbm, send_one, send_two, keep_one, keep_two,
               wo, wu, wd, hid, hl, xh1, rs1, act, gp, feed, dfl, dhid, stage, cota_ref, cotb_ref, itot_ref, out_ref, gout_ref,
               wsem, gsem, csem):
    R, W = att_ref.shape
    nc = wu.shape[0]
    def rows_of(refs, i):
        for ref in refs:
            h = ref.shape[0] // RB
            if i < h:
                return ref[pl.ds(i*RB,RB),:]
            i -= h
    def copies(k):
        c = order_ref[k]
        return (pltpu.make_async_copy(wu_hbm.at[:, pl.ds(c*W, W)], wu.at[k], wsem.at[1+k]),
                pltpu.make_async_copy(wd_hbm.at[pl.ds(c*W, W), :], wd.at[k], wsem.at[1+nc+k]))
    cwo = pltpu.make_async_copy(wo_hbm, wo, wsem.at[0]); cwo.start()
    for k in range(nc):
        for cp in copies(k): cp.start()
    late = [pltpu.make_async_copy(src, dst, csem.at[i]) for i, (src, dst) in enumerate(
        ((cota_hbm, cota_ref), (cotb_hbm, cotb_ref), (itot_hbm, itot_ref), (out_ref.at[pl.ds(0, R//2), :], outo_hbm), (gout_ref, gout_hbm),
         (out_ref.at[pl.ds(R//2, R//2), :], outx_hbm)))]
    for c in late[:3]: c.start()
    NB = R // RB
    vecs = (ob_ref, g1_ref, b1_ref, db_ref, g2_ref, b2_ref)
    row = lambda i: wide(vecs[i][...])
    lanes = W // 128
    cwo.wait()
    feed[...] = dot(att_ref[...].astype(bf16), wo[...])
    for i in range(NB):
        s = pl.ds(i*RB, RB)
        r = rows_of((xa_ref, xb_ref, xc_ref), i).astype(f32) + feed[s, :] + row(OUT_B)
        xh, inv = rows_norm(r)
        xh1[s,:] = xh
        rs1[s,:] = inv
        h = xh * row(G1) + row(B1)
        hid[s,:] = h
        hl[s,:] = h.astype(bf16)
    for k in range(nc):
        for cp in copies(k): cp.wait()
        ub = wide(ub_ref[pl.ds(order_ref[k]*lanes, lanes), :])
        for j in range(W//256):
            cs = slice(j*256, (j+1)*256)
            pre = dot(hl[...], wu[k, :, cs]) + ub[:, cs]
            a_, g_ = gelu_pair(pre)
            act[k, :, cs] = a_.astype(bf16)
            gp[k, :, cs] = g_.astype(gp.dtype)
        part = dot(act[k], wd[k])
        if k == 0: feed[...] = part
        else: feed[...] += part
    late[0].wait()
    late[1].wait()
    lab = (lax.broadcasted_iota(jnp.int32, (8, 1), 0) + 1).astype(f32)
    count = jnp.zeros((8, 1), f32)
    zero = jnp.zeros((1,W),f32)
    segsum = jnp.zeros((8, W), f32)
    sg = ss = sdb = zero
    for i in range(NB):
        s = pl.ds(i*RB, RB)
        xh, inv = rows_norm(hid[s,:] + feed[s,:] + row(DOWN_B))
        o = xh * row(G2) + row(B2)
        oh = o.astype(bf16)
        out_ref[s,:] = oh
        ol = (o - oh.astype(f32)).astype(bf16)
        hot = (lab == seg_ref[0:1, i*RB:(i+1)*RB]).astype(f32)
        count = count + jnp.sum(hot, axis=1, keepdims=True)
        hot = hot.astype(bf16)
        segsum = segsum + dot(hot, oh) + dot(hot, ol)
        u = rows_of((cota_ref, cotb_ref), i).astype(f32)
        sg = sg + col_sum(u*xh)
        ss = ss + col_sum(u)
        d = norm_back(u * row(G2), xh, inv)
        dhid[s,:] = d
        dl = d.astype(bf16)
        dfl[s,:] = dl
        sdb = sdb + col_sum(dl.astype(f32))
    late[3].start()
    late[5].start()
    segsum_ref[0:8, :] = segsum
    segsum_ref[8:16, :] = jnp.broadcast_to(count, (8, W))
    small_ref[pl.ds(DOWN_B,1), :] = sdb
    small_ref[pl.ds(G2,1), :] = sg
    small_ref[pl.ds(B2,1), :] = ss
    def push(slot, k, kind):
        dst = (send_one, send_two, keep_one, keep_two)[k]
        return pltpu.make_async_copy(stage.at[slot], dst.at[pl.ds(kind*W, W), :], gsem.at[slot])
    for k in range(nc):
        stage[k] = dot_tn(act[k], dfl[...]).astype(bf16)
        push(k, k, 0).start()
        da = dot_nt(dfl[...], wd[k])
        dp = (da * gp[k].astype(f32)).astype(bf16)
        act[k] = dp
        small_ref[pl.ds(UP_B + order_ref[k],1), :] = col_sum(dp.astype(f32))
        stage[nc+k] = dot_tn(hl[...], dp).astype(bf16)
        push(nc+k, k, 1).start()
        dhid[...] += dot_nt(dp, wu[k])
    sg = ss = sdb = zero
    for i in range(NB):
        s = pl.ds(i*RB, RB)
        dh = dhid[s,:]
        xh = xh1[s,:]
        sg = sg + col_sum(dh*xh)
        ss = ss + col_sum(dh)
        d = norm_back(dh * row(G1), xh, rs1[s,:])
        dres_ref[s,:] = d
        dl = d.astype(bf16)
        dfl[s,:] = dl
        sdb = sdb + col_sum(dl.astype(f32))
    small_ref[pl.ds(OUT_B,1), :] = sdb
    small_ref[pl.ds(G1,1), :] = sg
    small_ref[pl.ds(B1,1), :] = ss
    gout_ref[...] = dot_tn(att_ref[...].astype(bf16), dfl[...]).astype(bf16)
    late[4].start()
    late[2].wait()
    l0 = lax.broadcasted_iota(jnp.int32, (128,128), 0) // HD
    l1 = lax.broadcasted_iota(jnp.int32, (128,128), 1) // HD
    same = (l0 == l1).astype(f32).astype(bf16)
    feed[...] = dot_nt(dfl[...], wo[...])
    for i in range(NB):
        s = pl.ds(i*RB, RB)
        da = feed[s,:]
        it = itot_ref[s,:]
        dn_ref[s,:] = (da * it).astype(bf16)
        p = da * att_ref[s,:]
        ph = p.astype(bf16)
        plow = (p - ph.astype(f32)).astype(bf16)
        for j in range(W//128):
            cs = slice(j*128,(j+1)*128)
            dt_ref[s, cs] = -(dot(ph[:,cs], same) + dot(plow[:,cs], same)) * it[:,cs]
    for c in late[3:]: c.wait()
    for k in range(nc):
        push(k, k, 0).wait()
        push(nc+k, k, 1).wait()

def mid(order, att, x, cot, itot, seg_row, vecs, wo, wu, wd):
    R, W = att.shape
    nc = wu.shape[1] // W
    any_ = pl.BlockSpec(memory_space=pltpu.HBM)
    vm = pl.BlockSpec(memory_space=pltpu.VMEM)
    sm = pl.BlockSpec(memory_space=pltpu.SMEM)
    sd = pltpu.HBM
    return pl.pallas_call(
        mid_kernel,
        in_specs=[sm]+[vm]*4+[any_]*3+[vm]*8+[any_]*3,
        out_specs=[vm]*5+[any_]*7,
        out_shape=[sd((16,W),f32), sd((UP_B+nc+6,W),f32), sd((R,W),f32), sd((R,W),bf16), sd((R,W),f32), sd((R//2,W),bf16), sd((R//2,W),bf16),
                   sd((W,W),bf16)]+[sd((2*W,W),bf16)]*4,
        scratch_shapes=[pltpu.VMEM((W,W),bf16), pltpu.VMEM((nc,W,W),bf16), pltpu.VMEM((nc,W,W),bf16),
                        pltpu.VMEM((R,W),f32), pltpu.VMEM((R,W),bf16), pltpu.VMEM((R,W),f32), pltpu.VMEM((R,1),f32),
                        pltpu.VMEM((nc,R,W),bf16), pltpu.VMEM((nc,R,W),f32), pltpu.VMEM((R,W),f32), pltpu.VMEM((R,W),bf16), pltpu.VMEM((R,W),f32),
                        pltpu.VMEM((2*nc,W,W),bf16), pltpu.VMEM((R//2,W),bf16), pltpu.VMEM((R//2,W),bf16), pltpu.VMEM((R,W),f32),
                        pltpu.VMEM((R,W),bf16), pltpu.VMEM((W,W),bf16),
                        pltpu.SemaphoreType.DMA((1+2*nc,)), pltpu.SemaphoreType.DMA((2*nc,)), pltpu.SemaphoreType.DMA((6,))],
        compiler_params=pltpu.CompilerParams(vmem_limit_bytes=60*1024*1024),
        name="mid",
    )(order, *in_hbm(att, *x, *cot, itot, seg_row, *vecs, wo, wu, wd))

GW = 256
ID_ROWS = 16
def head_pair_lanes():
    return lax.broadcasted_iota(jnp.int32, (1,128), 1) < HD

def gather_rows(refs, dst, sem):
    at, copies = 0, []
    for i, ref in enumerate(refs):
        n = ref.shape[0] // 128 * 128
        copies.append(pltpu.make_async_copy(ref.at[pl.ds(0, n), :], dst.at[pl.ds(at, n), :], sem.at[i]))
        at += n
    return copies

def gather_ids(refs, dst, sem):
    tails = [ref for ref in refs if ref.shape[0] % 128]
    return [
        pltpu.make_async_copy(ref.at[pl.ds(ref.shape[0] - ID_ROWS, ID_ROWS), :], dst.at[i], sem.at[i])
        for i, ref in enumerate(tails)
    ]

def ids_of(ids, width):
    return jnp.concatenate([ids[i, 0:1, 0:width].astype(f32) for i in range(ids.shape[0])], axis=1)

def attend(q, k, v, bias, first):
    nums, tots = [], []
    for p in range(q.shape[1]//128):
        cs = slice(p*128,(p+1)*128)
        qp, kp, vp = q[:,cs], k[:,cs], v[:,cs]
        one = jnp.ones_like(vp); zero=jnp.zeros_like(qp)
        res = []
        for h in range(2):
            mine = first if h==0 else jnp.logical_not(first)
            s = dot_nt(jnp.where(mine, qp, zero), kp)
            e = jnp.exp(s + bias[...]).astype(bf16)
            res.append(dot(e, jnp.where(mine, vp, one)))
        nums.append(jnp.where(first, res[0], res[1]))
        tots.append(jnp.where(first, res[1], res[0]))
    return nums, tots

def attn_some_kernel(n_parts, *refs):
    parts = refs[:n_parts]
    (wq_ref, wk_ref, wv_ref, qb_ref, vb_ref,
     q_ref, k_ref, v_ref, num_ref, tot_ref, bias, x_ref, ids, sem, isem) = refs[n_parts:]
    R, N = q_ref.shape[0], k_ref.shape[0]
    @pl.when(pl.program_id(0) == 0)
    def _():
        marks = gather_ids(parts, ids, isem)
        copies = gather_rows(parts, x_ref, sem)
        for c in marks + copies: c.start()
        for c in marks: c.wait()
        row = ids_of(ids, N // ids.shape[0])
        bias[...] = same_segment(row[:, 0:R], row)
        for c in copies: c.wait()
    lanes = GW // 128
    at = pl.ds(pl.program_id(0)*lanes, lanes)
    qb, vb = wide(qb_ref[at, :]), wide(vb_ref[at, :])
    q = (0.125*(dot(x_ref[0:R,:], wq_ref[...]) + qb)).astype(bf16)
    k = dot(x_ref[...], wk_ref[...]).astype(bf16)
    v = (dot(x_ref[...], wv_ref[...]) + vb).astype(bf16)
    q_ref[...] = q; k_ref[...] = k; v_ref[...] = v
    nums, tots = attend(q, k, v, bias, head_pair_lanes())
    for p in range(lanes):
        num_ref[:, p*128:(p+1)*128] = nums[p]
        tot_ref[:, p*128:(p+1)*128] = tots[p]

def attn_some(parts, wq, wk, wv, qb, vb, R):
    W = wq.shape[0]
    N = sum(p.shape[0] // 128 * 128 for p in parts)
    n_ids = sum(1 for p in parts if p.shape[0] % 128)
    whole = N // n_ids * (n_ids + 1)
    sd = pltpu.HBM
    full = lambda a: pl.BlockSpec(a.shape, lambda j: (0,0))
    col = lambda r: pl.BlockSpec((r,GW), lambda j: (0,j))
    return pl.pallas_call(
        partial(attn_some_kernel, len(parts)), grid=(W//GW,),
        in_specs=[pl.BlockSpec(memory_space=pltpu.HBM)]*len(parts)+[col(W), col(W), col(W), full(qb), full(vb)],
        out_specs=[col(R), col(N), col(N), col(R), col(R)],
        out_shape=[sd((R,W),bf16), sd((whole,W),bf16), sd((whole,W),bf16), sd((R,W),f32), sd((R,W),f32)],
        scratch_shapes=[pltpu.VMEM((R,N),f32), pltpu.VMEM((N,W),bf16), pltpu.VMEM((n_ids,ID_ROWS,W),bf16),
                        pltpu.SemaphoreType.DMA((len(parts),)), pltpu.SemaphoreType.DMA((n_ids,))],
        compiler_params=pltpu.CompilerParams(vmem_limit_bytes=24*1024*1024, dimension_semantics=("arbitrary",)),
        name="attn_some",
    )(*in_hbm(*parts, wq, wk, wv, qb, vb))

def attn_last_kernel(n_parts, n_all, *refs):
    parts = refs[n_all-n_parts:n_all]
    (q_ref, wk_ref, wv_ref, vb_ref, num_ref, tot_ref, _, _,
     k_ref, v_ref, att_ref, itot_ref, sk_ref, bias, x_ref, ids, sem, isem) = refs[n_all:]
    R, N = q_ref.shape[0], k_ref.shape[0]
    whole = sk_ref.shape[1]
    @pl.when(pl.program_id(0) == 0)
    def _():
        marks = gather_ids(refs[:n_all], ids, isem)
        copies = gather_rows(parts, x_ref, sem)
        for c in marks + copies: c.start()
        for c in marks: c.wait()
        row = ids_of(ids, N)
        sk_ref[...] = jnp.broadcast_to(row, sk_ref.shape)
        bias[...] = same_segment(row[:, 0:R], row[:, whole-N:whole])
        for c in copies: c.wait()
    lanes = GW // 128
    vb = wide(vb_ref[pl.ds(pl.program_id(0)*lanes, lanes), :])
    k = dot(x_ref[...], wk_ref[...]).astype(bf16)
    v = (dot(x_ref[...], wv_ref[...]) + vb).astype(bf16)
    k_ref[...] = k; v_ref[...] = v
    nums, tots = attend(q_ref[...], k, v, bias, head_pair_lanes())
    for p in range(lanes):
        cs = slice(p*128, (p+1)*128)
        it = 1.0 / pltpu.roll(tots[p] + tot_ref[:, cs], HD, 1)
        att_ref[:,cs] = (nums[p] + num_ref[:, cs]) * it
        itot_ref[:,cs] = it

def attn_last(here, parts, q, wk, wv, vb, num, tot, k, v):
    R, W = q.shape
    N = sum(p.shape[0] // 128 * 128 for p in parts)
    whole = k.shape[0]
    sd = pltpu.HBM
    every = [*here, *parts]
    n = len(every)
    n_ids = sum(1 for p in every if p.shape[0] % 128)
    any_ = pl.BlockSpec(memory_space=pltpu.HBM)
    full = lambda a: pl.BlockSpec(a.shape, lambda j: (0,0))
    col = lambda r: pl.BlockSpec((r,GW), lambda j: (0,j))
    tail = pl.BlockSpec((N,GW), lambda j: (whole//N-1,j))
    return pl.pallas_call(
        partial(attn_last_kernel, len(parts), n), grid=(W//GW,),
        in_specs=[any_]*n+[col(R), col(W), col(W), full(vb), col(R), col(R), any_, any_],
        out_specs=[tail, tail, col(R), col(R), pl.BlockSpec((8,whole), lambda j: (0,0))],
        out_shape=[sd((whole,W),bf16), sd((whole,W),bf16), sd((R,W),f32), sd((R,W),f32), sd((8,whole),f32)],
        input_output_aliases={n+6: 0, n+7: 1},
        scratch_shapes=[pltpu.VMEM((R,N),f32), pltpu.VMEM((N,W),bf16), pltpu.VMEM((n_ids,ID_ROWS,W),bf16),
                        pltpu.SemaphoreType.DMA((n,)), pltpu.SemaphoreType.DMA((n_ids,))],
        compiler_params=pltpu.CompilerParams(vmem_limit_bytes=20*1024*1024, dimension_semantics=("arbitrary",)),
        name="attn_last",
    )(*in_hbm(*every, q, wk, wv, vb, num, tot), k, v)

def attn_bwd_kernel(q_ref, k_ref, v_ref, dn_ref, dt_ref, sk_ref, dq_ref, dk_ref, dv_ref, bias):
    @pl.when(pl.program_id(0) == 0)
    def _():
        row = sk_ref[0:1, :]
        bias[...] = same_segment(row, row[:, 0:q_ref.shape[0]])
    first = head_pair_lanes()
    lane = lax.broadcasted_iota(jnp.int32, (1,128), 1)
    for p in range(q_ref.shape[1]//128):
        cs = slice(p*128,(p+1)*128)
        qp, kp, vp, dnp = q_ref[:,cs], k_ref[:,cs], v_ref[:,cs], dn_ref[:,cs]
        dtr = pltpu.roll(dt_ref[:,cs], HD, 1)
        hi = dtr.astype(bf16)
        rest = dtr - hi.astype(f32)
        mid_ = rest.astype(bf16)
        low = (rest - mid_.astype(f32)).astype(bf16)
        res=[]
        for h in range(2):
            mine = first if h==0 else jnp.logical_not(first)
            o = HD if h==0 else 0
            ex = jnp.where(lane==o, hi, jnp.where(lane==o+1, mid_, jnp.where(lane==o+2, low, jnp.zeros_like(hi))))
            dne = jnp.where(mine, dnp, ex)
            ve = jnp.where(mine, vp, jnp.where((lane>=o)&(lane<o+3), jnp.ones_like(vp), jnp.zeros_like(vp)))
            s = dot_nt(jnp.where(mine, kp, jnp.zeros_like(kp)), qp)
            e = jnp.exp(s + bias[...])
            pr = dot_nt(ve, dne)
            ds = (e * pr).astype(bf16)
            dv = dot(e.astype(bf16), dnp)
            dk = dot(ds, qp)
            dq = dot_tn(kp, ds)
            res.append((dq,dk,dv))
        dq = jnp.concatenate([res[0][0][0:HD, :], res[1][0][HD:, :]], axis=0)
        dq_ref[:,cs] = (jnp.transpose(dq).astype(bf16).astype(f32)*0.125).astype(bf16)
        dk_ref[:,cs] = jnp.where(first, res[0][1], res[1][1]).astype(bf16)
        dv_ref[:,cs] = jnp.where(first, res[0][2], res[1][2]).astype(bf16)

def attn_bwd(deps,q,k,v,dn,dt,sk,start,count):
    R,W=q.shape; N=k.shape[0]
    sd = pltpu.HBM
    GB=128
    col = lambda r: pl.BlockSpec((r,GB), lambda j: (0,j+start))
    out = lambda r: pl.BlockSpec((r,GB), lambda j: (0,j))
    return call(
        attn_bwd_kernel, deps, in_hbm(q,k,v,dn,dt,sk),
        [col(R), col(N), col(N), col(R), col(R), pl.BlockSpec(sk.shape, lambda j: (0,0))],
        [out(R), out(N), out(N)],
        [sd((R,GB*count),bf16), sd((N,GB*count),bf16), sd((N,GB*count),bf16)],
        [pltpu.VMEM((N,R),f32)], grid=(count,), vmem=16, name="attn_bwd",
    )

def spans(refs):
    at, out = 0, []
    for r in refs:
        out.append(slice(at, at + r.shape[1]))
        at += r.shape[1]
    return out

def token_grad_kernel(n_grads, *refs):
    grads, (wq_ref, wk_ref, wv_ref, dres_ref, own_ref, away_ref, pa_ref, pb_ref) = refs[:n_grads], refs[n_grads:]
    dq, dk, dv = grads[0::3], grads[1::3], grads[2::3]
    R = dq[0].shape[0]
    parts = spans(dq)
    def back(refs, w_ref, rows):
        total = dot_nt(refs[0][rows,:], w_ref[:,parts[0]])
        for r, cs in zip(refs[1:], parts[1:]): total = total + dot_nt(r[rows,:], w_ref[:,cs])
        return total
    top, rest = slice(0,R), slice(R,2*R)
    pair = (back(dk, wk_ref, rest) + back(dv, wv_ref, rest)).astype(bf16)
    pa_ref[...] = pair[:R//2]
    pb_ref[...] = pair[R//2:]
    mine = (dres_ref[...] + back(dq, wq_ref, top) + back(dk, wk_ref, top)
            + back(dv, wv_ref, top))
    own_ref[...] = mine[:R//2]
    away_ref[...] = mine[R//2:]

def token_grad(deps, grads, wq, wk, wv, dres):
    R, W = dres.shape
    sd = pltpu.HBM
    return call(
        partial(token_grad_kernel, len(grads)), deps, in_hbm(*grads, wq, wk, wv, dres),
        [VM]*(len(grads)+4), [VM]*4, [sd((R//2,W),f32)]*2+[sd((R//2,W),bf16)]*2, vmem=24, name="token_grad",
    )

def weight_grad_kernel(n_parts, n_grads, *refs):
    tokens, grads = refs[:n_parts], refs[n_parts:n_parts+n_grads]
    dq, dk, dv = grads[0::3], grads[1::3], grads[2::3]
    (bit_ref, gout_ref, bsum_ref, gsend_hbm, gkeep_hbm, stage, x_ref, sem, xsem) = refs[n_parts+n_grads:]
    copies = gather_rows(tokens, x_ref, xsem)
    for c in copies: c.start()
    W = x_ref.shape[1]
    bit = bit_ref[0]
    parts = spans(dq)
    def push(i, start):
        src = gout_ref if i == 3 else stage.at[i]
        def go(dst):
            cp = pltpu.make_async_copy(src, dst.at[pl.ds((i%2)*W, W), :], sem.at[i])
            cp.start() if start else cp.wait()
        @pl.when(bit == i//2)
        def _(): go(gkeep_hbm)
        @pl.when(bit != i//2)
        def _(): go(gsend_hbm)
    push(3, True)
    for c in copies: c.wait()
    for i, refs in ((2,dv), (1,dk), (0,dq)):
        for ref, cs in zip(refs, parts):
            n = ref.shape[0]
            stage[i, :, cs] = dot_tn(x_ref[0:n,:], ref[...]).astype(bf16)
        push(i, True)
    for ref, cs in zip(dq, parts): bsum_ref[0:1,cs] = col_sum(ref[...].astype(f32))
    for ref, cs in zip(dv, parts): bsum_ref[1:2,cs] = col_sum(ref[...].astype(f32))
    for i in range(4): push(i, False)

def weight_grad(deps, bits, grads, tokens, gout):
    R = grads[0].shape[0]
    W = gout.shape[0]
    sd = pltpu.HBM
    return call(
        partial(weight_grad_kernel, len(tokens), len(grads)), deps, (*in_hbm(*tokens, *grads), bits, *in_hbm(gout)),
        [FAR]*len(tokens)+[VM]*len(grads)+[SM, VM], [VM,FAR,FAR],
        [sd((2,W),f32), sd((2*W,W),bf16), sd((2*W,W),bf16)],
        [pltpu.VMEM((3,W,W),bf16), pltpu.VMEM((2*R,W),bf16), pltpu.SemaphoreType.DMA((4,)), pltpu.SemaphoreType.DMA((len(tokens),))],
        vmem=22, name="weight_grad",
    )

def emit_kernel(up_from, n_prev, second, bits_ref, *refs):
    n_in = len(second) * 2
    pieces_in, outs, (stage, sem) = refs[:n_in], refs[n_in+n_prev:-2], refs[-2:]
    n, W = pieces_in[0].shape
    bit, mine, theirs = bits_ref[0], bits_ref[1], bits_ref[2]
    pieces = []
    for i, s in enumerate(second):
        pieces.append((bit, 1 - mine if s else mine, pieces_in[2*i]))
        pieces.append((1 - bit, 1 - theirs if s else theirs, pieces_in[2*i+1]))
    def send(i, start):
        half, block, ref = pieces[i]
        for b in range(2):
            for h in range(2):
                if up_from is None: dst = outs[2*h + b]
                elif b == 0: dst = outs[0].at[pl.ds((2*h + up_from)*W, W), :]
                else: dst = outs[1].at[:, pl.ds((2*h + up_from)*W, W)]
                @pl.when((half == h) & (block == b))
                def _():
                    cp = pltpu.make_async_copy(stage.at[i], dst, sem.at[i])
                    cp.start() if start else cp.wait()
    for i, (half, block, ref) in enumerate(pieces):
        stage[i] = ref[...].astype(f32)
        send(i, True)
    for i in range(len(pieces)): send(i, False)

def emit(deps, bits, pieces, second, out_shape, up_from=None, prev=()):
    n, W = pieces[0].shape
    m = len(pieces)
    return call(
        partial(emit_kernel, up_from, len(prev), second), deps, (bits, *pieces, *prev),
        [SM]+[VM]*m+[FAR]*len(prev), [FAR]*len(out_shape), [pltpu.HBM(s, f32) for s in out_shape],
        [pltpu.VMEM((m,n,W),f32), pltpu.SemaphoreType.DMA((m,))],
        {1+m+i: i for i in range(len(prev))}, vmem=18, name="emit",
    )

def split_kernel(index, bits_ref, keep_hbm, recv_hbm, *refs):
    outs, (a, b, o, sem) = refs[:2], refs[2:]
    n = outs[0].shape[0]
    bit = bits_ref[index]
    steps = o.shape[0] // 2
    rows = n // steps
    def load(i):
        src = pl.ds((bit if i // steps else 1 - bit)*n + i % steps*rows, rows)
        return (pltpu.make_async_copy(keep_hbm.at[src, :], a.at[i], sem.at[0, i]),
                pltpu.make_async_copy(recv_hbm.at[src, :], b.at[i], sem.at[1, i]))
    def store(i):
        return pltpu.make_async_copy(o.at[i], outs[i // steps].at[pl.ds(i % steps*rows, rows), :], sem.at[2, i])
    for i in range(2*steps):
        for c in load(i): c.start()
    for i in range(2*steps):
        for c in load(i): c.wait()
        o[i] = (a[i].astype(f32) + b[i].astype(f32)).astype(bf16)
        store(i).start()
    for i in range(2*steps): store(i).wait()

def split_add(deps, bits, index, keep, recv):
    n, W = keep.shape[0] // 2, keep.shape[1]
    if n % 16:
        keep, recv, deps = lax.optimization_barrier((keep, recv, tuple(deps)))
        bit = bits[index]
        halves = [[lax.dynamic_slice_in_dim(a, b * n, n, 0).astype(f32) for a in (keep, recv)] for b in (1 - bit, bit)]
        return deps[0], [(a + b).astype(bf16) for a, b in halves]
    steps = n // 192 if n % 192 == 0 else 1
    return call(
        partial(split_kernel, index), deps, (bits, *in_hbm(keep), recv), [SM, FAR, ANY], [FAR]*2,
        [pltpu.HBM((n,W),bf16)]*2,
        [pltpu.VMEM((2*steps,n//steps,W),bf16)]*3+[pltpu.SemaphoreType.DMA((3,2*steps))],
        vmem=14*n*W/MIB+1, name="split_add",
    )

def join_kernel(index, bits_ref, mine_hbm, recv_hbm, out_hbm, both, sem):
    n = mine_hbm.shape[0]
    bit = bits_ref[index]
    loads = [pltpu.make_async_copy(src, both.at[pl.ds(at*n, n), :], sem.at[i])
             for i, (src, at) in enumerate(((mine_hbm, bit), (recv_hbm, 1 - bit)))]
    for c in loads: c.start()
    for c in loads: c.wait()
    out = pltpu.make_async_copy(both, out_hbm, sem.at[2])
    out.start()
    out.wait()

def join(deps, bits, index, mine, recv):
    n, W = mine.shape
    if n % 16:
        mine, recv, deps = lax.optimization_barrier((mine, recv, tuple(deps)))
        return deps[0], [jnp.where(bits[index] == 0, jnp.concatenate([mine, recv], 0), jnp.concatenate([recv, mine], 0))]
    return call(
        partial(join_kernel, index), deps, (bits, mine, recv), [SM, ANY, ANY], [ANY],
        [jax.ShapeDtypeStruct((2*n,W),bf16)], [pltpu.VMEM((2*n,W),bf16), pltpu.SemaphoreType.DMA((3,))],
        vmem=8*n*W/MIB+1, name="join",
    )

def add_kernel(a_ref, b_ref, o_ref):
    o_ref[...] = (a_ref[...].astype(f32) + b_ref[...].astype(f32)).astype(o_ref.dtype)

def add_to(deps, a, b, dtype):
    return call(add_kernel, deps, (a, b), [VM, VM], [VM], [jax.ShapeDtypeStruct(a.shape, dtype)], vmem=8, name="add")

def stack_kernel(*refs):
    out, at = refs[-1], 0
    for r in refs[:-1]:
        out[at:at+r.shape[0], :] = r[...]
        at += r.shape[0]

def stack_rows(deps, arrays):
    rows = sum(a.shape[0] for a in arrays)
    return call(stack_kernel, deps, arrays, [VM]*len(arrays), [VM],
                [jax.ShapeDtypeStruct((rows, arrays[0].shape[1]), f32)], vmem=4, name="stack_rows")

D = 768
pool_eps = 1e-06


def matryoshka(averages):
    pieces = []
    for prefix in (D, D * 2 // 3, D // 3, D // 6, D // 12):
        leading = averages[..., :prefix]
        centred = leading - jnp.mean(leading, axis=-1, keepdims=True)
        pieces.append(
            centred * lax.rsqrt(jnp.mean(centred * centred, axis=-1, keepdims=True) + pool_eps)
        )
    return jnp.concatenate(pieces, axis=-1)


def part_of(value, index, count):
    rows = value.shape[0] // count
    return lax.dynamic_slice_in_dim(value, index * rows, rows, 0)


def ordered(bit, mine, theirs):
    first = lax.broadcasted_iota(jnp.int32, (2,) + (1,) * mine.ndim, 0) == bit
    return jnp.where(first, mine[None], theirs[None]).reshape((-1,) + mine.shape[1:])


def sum_of(arrays):
    total = arrays[0].astype(f32)
    for array in arrays[1:]:
        total = total + array.astype(f32)
    return total.astype(bf16)


fence = lax.optimization_barrier


class Links:
    def __init__(self, n_rows, n_blk):
        self.size = {"rows": n_rows, "blk": n_blk}
        self.at = {"rows": lax.axis_index("rows"), "blk": lax.axis_index("blk")}
        self.near = ("rows", 0, 0)
        self.near_bit = self.at["rows"] % 2
        far = list(range(1, n_rows.bit_length() - 1))
        self.far = [("rows", a, b) for a, b in zip(far, far[::-1])]
        self.plain_far = [("rows", a, a) for a in far]
        self.blk_bits = [("blk", k, k) for k in range(n_blk.bit_length() - 1)]

    def bit(self, stage, flip=False):
        axis, even, odd = stage
        at = self.at[axis]
        if even == odd:
            return (at >> even) % 2
        near = 1 - self.near_bit if flip else self.near_bit
        return jnp.where(near == 0, (at >> even) % 2, (at >> odd) % 2)

    def swap(self, value, stage):
        axis, even, odd = stage
        pairs = [(i, i ^ (1 << (odd if i % 2 and even != odd else even))) for i in range(self.size[axis])]
        return lax.ppermute(value, axis, pairs)


class Steps:
    def __init__(self, links):
        self.links = links
        self.stages = links.far + links.blk_bits
        first = links.far[0]
        bits = [links.near_bit, links.bit(first), links.bit(first, True)]
        self.base = len(bits)
        bits += [links.bit(stage) for stage in self.stages]
        self.bits = jnp.stack(bits).astype(jnp.int32)
        self.swap = links.swap

    def run(self, function, *args):
        return function((), *args)[1]

    def cut(self, addends, stage):
        return self.run(split_add, self.bits, self.base + self.stages.index(stage), *addends)

    def halve(self, addends, stage):
        bit = self.links.bit(stage)
        send = sum_of([part_of(a, 1 - bit, 2) for a in addends])
        keep = sum_of([part_of(a, bit, 2) for a in addends])
        return keep, self.swap(send, stage)

    def total(self, addends, stage):
        value = sum_of(addends)
        return value, self.swap(value, stage)

    def double(self, pieces, stage, following):
        value = ordered(self.links.bit(stage), *pieces)
        return value, self.swap(value, following)

    def last(self, pieces, stage, final):
        value = ordered(self.links.bit(stage), *pieces)
        return value, self.swap(value, final), self.swap(value, self.links.near)

    def finish(self, group):
        return group[0], group[2], group[1], self.swap(group[1], self.links.near)


def local(
    n_rows,
    n_blk,
    tokens,
    segments,
    query_weight,
    query_bias,
    key_weight,
    value_weight,
    value_bias,
    out_weight,
    out_bias,
    first_gain,
    first_shift,
    up_weight,
    up_bias,
    down_weight,
    down_bias,
    second_gain,
    second_shift,
    cotangent,
):
    links = Links(n_rows, n_blk)
    pair, cross = links.blk_bits
    seq_at = links.at["blk"] // 2
    near_bit = links.near_bit
    num_seq, tok_rows, width = tokens.shape
    ff = up_weight.shape[1]
    chunks = ff // width
    total_rows = 2 * tok_rows

    piece = tok_rows // 2
    pick = lambda a, s: lax.dynamic_index_in_dim(a, s, 0, keepdims=False)
    other = pick(tokens, 1 - seq_at)
    id_rows = jnp.pad(segments.astype(bf16)[:, None, :], ((0, 0), (0, ID_ROWS - 1), (0, width - tok_rows)))
    own = jnp.concatenate([pick(tokens, seq_at), pick(id_rows, seq_at)], 0)
    other_b = jnp.concatenate([other[piece:], pick(id_rows, 1 - seq_at)], 0)
    far_a = links.swap(other[:piece], cross)
    far_b = links.swap(other_b, cross)
    near_block = links.swap(own, pair)
    last_a = links.swap(far_a, pair)
    last_b = links.swap(far_b, pair)
    cot_other = pick(cotangent, 1 - seq_at)
    cot_other, far_b, far_a = fence((cot_other, far_b, far_a))
    cot_far = links.swap(cot_other, cross)
    here, late = [own, far_a, far_b, near_block], [last_a, last_b]
    value_wide = value_bias.reshape(-1, 128)
    queries, keys, values, numer, totals = attn_some(
        here, query_weight, key_weight, value_weight, query_bias.reshape(-1, 128), value_wide, total_rows
    )
    cot_own = pick(cotangent, seq_at)
    cot_own, late, queries, keys, values, numer, totals = fence(
        (cot_own, late, queries, keys, values, numer, totals)
    )
    blocks = [*here, *late]
    keys, values, attended, inv_totals, seg_row = attn_last(
        here, late, queries, key_weight, value_weight, value_wide, numer, totals, keys, values
    )
    vectors = [
        v.reshape(-1, 128)
        for v in (out_bias, first_gain, first_shift, down_bias, second_gain, second_shift, up_bias)
    ]
    half = chunks // 2
    order = jnp.concatenate(
        [(1 - near_bit) * half + jnp.arange(half), near_bit * half + jnp.arange(half)]
    ).astype(jnp.int32)
    (
        seg_sums, small, d_resid, d_numer, d_total, out_own, out_away, grad_out,
        send_one, send_two, keep_one, keep_two,
    ) = mid(
        order, attended, (own, far_a, far_b), (cot_own, cot_far), inv_totals, seg_row,
        vectors, out_weight, up_weight, down_weight,
    )
    back_in = (queries, keys, values, d_numer, d_total)
    tc = Steps(links)
    bits = tc.bits
    first, *rest = links.far
    backward = rest[::-1] + [first]
    ffn_shape, attn_shape = ((ff, width), (width, ff)), ((width, width),) * 4
    vectors = UP_B + chunks + 2
    seg_at, row_end = vectors, vectors + 16
    pairs = width // 128

    near_end = pairs // 3
    recv_one = tc.swap(send_one, links.near)
    recv_two = tc.swap(send_two, links.near)
    grads_a = tc.run(attn_bwd, *back_in, seg_row, 0, near_end)
    recv_one, recv_two, grads_a, back_in, out_away = fence((recv_one, recv_two, grads_a, back_in, out_away))

    send_one, one = tc.cut((keep_one, recv_one), first)
    send_one, recv_two, back_in, out_away = fence((send_one, recv_two, back_in, out_away))
    one = one, tc.swap(send_one, first)
    send_two, two = tc.cut((keep_two, recv_two), first)
    send_two, back_in, out_away = fence((send_two, back_in, out_away))
    two = two, tc.swap(send_two, first)
    out_back = tc.swap(out_away, cross)
    grads_b = tc.run(attn_bwd, *back_in, seg_row, near_end, pairs - near_end)
    send_one, one = tc.cut(one, rest[0])
    send_one, grads_a, grads_b, out_back = fence((send_one, grads_a, grads_b, out_back))
    one = one, tc.swap(send_one, rest[0])
    grads = (*grads_a, *grads_b)
    bias_sums, attn_send, attn_keep = tc.run(weight_grad, bits, grads, blocks, grad_out)
    one, two, grads, bias_sums, attn_send = fence((one, two, grads, bias_sums, attn_send))

    for stage in rest:
        two = tc.halve(two, stage)
    for stage in [*rest[1:], pair]:
        one = tc.halve(one, stage)
    attn_recv = tc.swap(attn_send, links.near)
    send_three, three = tc.cut((attn_keep, attn_recv), first)
    small = jnp.concatenate([small[: UP_B + chunks], bias_sums, seg_sums], 0)
    small_recv = tc.swap(small, cross)
    one, two, three, send_three, small, small_recv = fence((one, two, three, send_three, small, small_recv))

    three = three, tc.swap(send_three, first)
    one = tc.halve(one, cross)
    two = tc.halve(two, pair)
    small = jnp.concatenate([small[:vectors] + small_recv[:vectors], small[vectors:], small_recv[vectors:]], 0)
    small_recv = tc.swap(small, pair)
    d_own, d_away, pair_own, pair_away = tc.run(token_grad, grads, query_weight, key_weight, value_weight, d_resid)
    one, two, three, small, small_recv, d_own, d_away, pair_own, pair_away = fence(
        (one, two, three, small, small_recv, d_own, d_away, pair_own, pair_away)
    )

    for stage in rest:
        three = tc.halve(three, stage)
    one = tc.total(one, cross)
    small = small + small_recv
    both_sums = ordered(seq_at, small[None, seg_at:row_end], small[None, row_end:])
    small = small[:vectors]
    small_recv = tc.swap(small, links.near)
    one, two, three, small, small_recv, both_sums = fence((one, two, three, small, small_recv, both_sums))

    one = tc.double(one, cross, pair)
    three = tc.halve(three, pair)
    two = tc.halve(two, cross)
    for stage in links.plain_far:
        small = small + small_recv
        small_recv = tc.swap(small, stage)
    one, two, three, small, small_recv, both_sums, pair_away = fence(
        (one, two, three, small, small_recv, both_sums, pair_away)
    )

    pair_away = tc.swap(pair_away, pair)
    one = tc.double(one, pair, backward[0])
    two = tc.total(two, cross)
    three = tc.halve(three, cross)
    small = small + small_recv
    pooled = matryoshka(both_sums[:, :NSEG] / both_sums[:, 8 : 8 + NSEG])
    vector_sums = [small[i] for i in range(UP_B)] + [small[UP_B : UP_B + chunks].reshape(-1)]
    vector_sums += [small[UP_B + chunks], small[UP_B + chunks + 1]]
    layer_output = ordered(seq_at, out_own[None], out_back[None])
    one, two, three, pooled, vector_sums, layer_output, pair_away = fence(
        (one, two, three, pooled, vector_sums, layer_output, pair_away)
    )

    for stage, following in zip(backward[:-2], backward[1:-1]):
        one = tc.double(one, stage, following)
    one = tc.last(one, backward[-2], first)
    two = tc.double(two, cross, pair)
    three = tc.total(three, cross)
    d_away = (d_away + pair_away.astype(f32)).astype(bf16)
    one, two, three, d_away = fence((one, two, three, d_away))

    one = tc.finish(one)
    two = tc.double(two, pair, backward[0])
    three = tc.double(three, cross, pair)
    one, two, three, d_away = fence((one, two, three, d_away))

    three = tc.double(three, pair, backward[0])
    for stage, following in zip(backward[:-2], backward[1:-1]):
        two = tc.double(two, stage, following)
    two = tc.last(two, backward[-2], first)
    d_back = tc.swap(d_away, cross)
    ffn_sums = tc.run(emit, bits, one, (False, True), ffn_shape, 0)
    two, three, ffn_sums, d_back, pair_own = fence((two, three, ffn_sums, d_back, pair_own))

    for stage, following in zip(backward[:-2], backward[1:-1]):
        three = tc.double(three, stage, following)
    three = tc.last(three, backward[-2], first)
    pair_own = tc.swap(pair_own, pair)
    two = tc.finish(two)
    down_sum, up_sum = tc.run(emit, bits, two, (False, True), ffn_shape, 1, ffn_sums)
    attn_sums = tc.run(emit, bits, (three[0], three[2]), (False,), attn_shape)
    three, pair_own, down_sum, up_sum, attn_sums, d_back = fence((three, pair_own, down_sum, up_sum, attn_sums, d_back))

    three = tc.finish(three)
    d_own = d_own + pair_own.astype(f32)
    grad_tokens = ordered(seq_at, d_own.astype(bf16)[None], d_back[None])
    query_sum, key_sum, value_sum, out_sum = tc.run(emit, bits, three[2:], (True,), attn_shape, None, attn_sums)
    return (
        layer_output,
        pooled,
        grad_tokens,
        query_sum,
        vector_sums[7],
        key_sum,
        value_sum,
        vector_sums[8],
        out_sum,
        vector_sums[OUT_B],
        vector_sums[G1],
        vector_sums[B1],
        up_sum,
        vector_sums[UP_B],
        down_sum,
        vector_sums[DOWN_B],
        vector_sums[G2],
        vector_sums[B2],
    )


def solution(mesh):
    row_split = P("rows", "blk", None)
    return jax.shard_map(
        partial(local, mesh.shape["rows"], mesh.shape["blk"]),
        mesh=mesh,
        in_specs=(row_split, P("rows", "blk")) + (P(),) * 15 + (row_split,),
        out_specs=(row_split, P("rows", None, None), row_split) + (P(),) * 15,
        check_vma=False,
    )
```
